32 devices in a mesh: dp: 8 (over z, y), ctx: 4 (over x, core).
Axes of the slice: x: 2, y: 2, z: 4, core: 2. Of those that a mesh axis runs over, the one named last changes fastest.
Arguments:
- hidden_in: bfloat16 [8, 4096, 512], P('dp', 'ctx'), may hold values from -6 to 6
- seq_lengths: int32 [8], P('dp'), may hold values from 1024 to 4096, as said below
- out_cotangent: bfloat16 [8, 4096, 512], P('dp', 'ctx'), may hold values from -6 to 6
- norm1_gain: bfloat16 [512], P('dp'), may hold values from 0.5 to 1.5
- norm1_shift: bfloat16 [512], P('dp'), may hold values from -2 to 2
- qkv_weight: bfloat16 [512, 1536], P('dp'), may hold values from -0.375 to 0.375
- qv_bias: bfloat16 [2, 512], P(None, 'dp'), may hold values from -2 to 2
- out_weight: bfloat16 [512, 512], P('dp'), may hold values from -1 to 1
- out_bias: bfloat16 [512], P('dp'), may hold values from -2 to 2
- norm2_gain: bfloat16 [512], P('dp'), may hold values from 0.5 to 1.5
- norm2_shift: bfloat16 [512], P('dp'), may hold values from -2 to 2
- up_weight: bfloat16 [512, 2048], P('dp'), may hold values from -0.25 to 0.25
- up_bias: bfloat16 [2048], P('dp'), may hold values from -2 to 2
- down_weight: bfloat16 [2048, 512], P('dp'), may hold values from -0.1875 to 0.1875
- down_bias: bfloat16 [512], P('dp'), may hold values from -2 to 2
Outputs:
- hidden_out: bfloat16 [8, 4096, 512], P('dp', 'ctx')
- grad_hidden: bfloat16 [8, 4096, 512], P('dp', 'ctx')
- grad_norm1_gain: float32 [512], P('dp')
- grad_norm1_shift: float32 [512], P('dp')
- grad_qkv_weight: float32 [512, 1536], P('dp')
- grad_qv_bias: float32 [2, 512], P(None, 'dp')
- grad_out_weight: float32 [512, 512], P('dp')
- grad_out_bias: float32 [512], P('dp')
- grad_norm2_gain: float32 [512], P('dp')
- grad_norm2_shift: float32 [512], P('dp')
- grad_up_weight: float32 [512, 2048], P('dp')
- grad_up_bias: float32 [2048], P('dp')
- grad_down_weight: float32 [2048, 512], P('dp')
- grad_down_bias: float32 [512], P('dp')
The draws below stay inside these ranges and needn't reach their ends.
Inputs may be any that keep to these rules, and one draw needn't show every extreme that they name: `seq_lengths`: some slot has exactly 4096 valid positions and another exactly 1024.
All inputs are finite; a program needn't handle non-finite values.
Results may differ from the reference program's by a relative error of at most 0.02.
Values may be sent and summed in bfloat16 or wider, within the bound.
No kernel may reach another device: no remote copies, remote signals or barrier semaphores. Data moves between devices by JAX's collectives and lax.ppermute only.
A program may use at most 192 MiB of HBM per device.

```python
import jax
import jax.numpy as jnp
from jax import lax

D = 512
HEADS = 8
HEAD_DIM = 64
FF = 2048
SLOT_LEN = 4096
MIN_LEN = 1024
SLOTS = 8


def draw_seq_lengths(key, part):
    key_one, key_two, key_three = jax.random.split(key, 3)
    lengths = jax.random.randint(key_one, (SLOTS,), MIN_LEN, SLOT_LEN + 1)
    longest = jax.random.randint(key_two, (), 0, SLOTS)
    shortest = (longest + 1 + jax.random.randint(key_three, (), 0, SLOTS - 1)) % SLOTS
    lengths = lengths.at[longest].set(SLOT_LEN)
    lengths = lengths.at[shortest].set(MIN_LEN)
    return lengths.astype(jnp.int32)


def levels(key, extent, shards, smallest, high):
    def one(axis_at, blocks):
        draws = jax.random.uniform(jax.random.fold_in(jax.random.fold_in(key, 6), axis_at), (blocks,), jnp.float32, smallest / len(shards), high / len(shards))
        return jnp.repeat(jnp.exp(draws), extent[axis_at] // blocks).reshape((-1,) + (1,) * (len(extent) - axis_at - 1))

    loudness = one(*shards[0])
    for cut in shards[1:]:
        loudness = loudness * one(*cut)
    return loudness


def noise(stream_key, dims, deviation, bound, cuts=(), held_as=jnp.bfloat16):
    level = levels(stream_key, dims, cuts, -0.22, 0.18) if cuts else 1.0
    result = jax.random.normal(stream_key, dims, jnp.float32) * deviation * level
    return jnp.minimum(jnp.maximum(result, -bound), bound).astype(held_as)


def setup_inputs(seed: int = 0) -> dict:
    seeds = jax.random.split(jax.random.key(seed), 16)
    hidden_in = noise(seeds[0], (SLOTS, SLOT_LEN, D), 1.0, 6.0, ((0, 8), (1, 4)))
    seq_lengths = draw_seq_lengths(jax.random.fold_in(seeds[15], 71), 0)
    out_cotangent = noise(seeds[2], (SLOTS, SLOT_LEN, D), 1.0, 6.0, ((0, 8), (1, 4)))
    norm1_gain = jnp.clip(1.0 + 0.1 * jax.random.normal(seeds[3], (D,), jnp.float32), 0.5, 1.5).astype(jnp.bfloat16)
    norm1_shift = noise(seeds[4], (D,), 0.3, 2.0, ((0, 8),))
    qkv_weight = noise(seeds[5], (D, 3 * D), (D // 2) ** -0.5, 0.375, ((0, 8),))
    qv_bias = noise(seeds[6], (2, D), 0.3, 2.0, ((1, 8),))
    out_weight = noise(seeds[7], (D, D), (D // 16) ** -0.5, 1.0, ((0, 8),))
    out_bias = noise(seeds[8], (D,), 0.3, 2.0, ((0, 8),))
    norm2_gain = jnp.clip(1.0 + 0.1 * jax.random.normal(seeds[9], (D,), jnp.float32), 0.5, 1.5).astype(jnp.bfloat16)
    norm2_shift = noise(seeds[10], (D,), 0.3, 2.0, ((0, 8),))
    up_weight = noise(seeds[11], (D, FF), D ** -0.5, 0.25, ((0, 8),))
    up_bias = noise(seeds[12], (FF,), 0.3, 2.0, ((0, 8),))
    down_weight = noise(seeds[13], (FF, D), (FF // 2) ** -0.5, 0.1875, ((0, 8),))
    down_bias = noise(seeds[14], (D,), 0.3, 2.0, ((0, 8),))
    return {"hidden_in": hidden_in, "seq_lengths": seq_lengths, "out_cotangent": out_cotangent, "norm1_gain": norm1_gain, "norm1_shift": norm1_shift, "qkv_weight": qkv_weight, "qv_bias": qv_bias, "out_weight": out_weight, "out_bias": out_bias, "norm2_gain": norm2_gain, "norm2_shift": norm2_shift, "up_weight": up_weight, "up_bias": up_bias, "down_weight": down_weight, "down_bias": down_bias}


@jax.custom_vjp
def low(v):
    return lax.optimization_barrier(v.astype(jnp.bfloat16)).astype(jnp.float32)

@jax.custom_vjp
def low_back(v):
    return v

def low_keep(v):
    return (low(v), None)

def low_pass(kept, grad):
    return (grad,)

def back_keep(v):
    return (v, None)

def back_low(kept, grad):
    return (low(grad),)
low.defvjp(low_keep, low_pass)
low_back.defvjp(back_keep, back_low)
epsilon = 1e-05

def exact_dot(left, right):
    return jnp.dot(left, right, precision=lax.Precision.HIGHEST, preferred_element_type=jnp.float32)

def layer_norm(inputs, norm_gain, norm_shift):
    center = inputs - lax.optimization_barrier(jnp.mean(inputs, axis=-1, keepdims=True))
    spread = lax.optimization_barrier(jnp.mean(center * center, axis=-1, keepdims=True))
    return center * lax.rsqrt(spread + epsilon) * norm_gain + norm_shift

def attend_block(query_block, key_rows, value_rows, key_valid):
    scores = jnp.einsum('qhd,khd->hqk', query_block, key_rows, precision=lax.Precision.HIGHEST) * HEAD_DIM ** (-0.5)
    scores = low_back(scores)
    scores = jnp.where(key_valid[None, None, :], scores, -1e+30)
    weights = low(jax.nn.softmax(scores, axis=-1))
    return jnp.einsum('hqk,khd->qhd', weights, value_rows, precision=lax.Precision.HIGHEST)

def slot_forward(slot_in, slot_len, params):
    gain_one, shift_one, w_qkv, bias_qv, w_out, bias_out, gain_two, shift_two, w_up, bias_up, w_down, bias_down = params
    normed_one = low(layer_norm(slot_in, gain_one, shift_one))
    bias_full = jnp.concatenate([bias_qv[0], jnp.zeros_like(bias_qv[0]), bias_qv[1]])
    projected = exact_dot(normed_one, w_qkv) + bias_full
    queries = low(low_back(projected[:, :D])).reshape(SLOT_LEN, HEADS, HEAD_DIM)
    key_rows = low(low_back(projected[:, D:2 * D])).reshape(SLOT_LEN, HEADS, HEAD_DIM)
    value_rows = low(low_back(projected[:, 2 * D:])).reshape(SLOT_LEN, HEADS, HEAD_DIM)
    key_valid = jnp.arange(SLOT_LEN) < slot_len
    blk_size = min(512, SLOT_LEN)
    query_blocks = queries.reshape(SLOT_LEN // blk_size, blk_size, HEADS, HEAD_DIM)

    def block_attention(query_block):
        return attend_block(query_block, key_rows, value_rows, key_valid)
    attended = lax.map(jax.checkpoint(block_attention), query_blocks).reshape(SLOT_LEN, D)
    attended = low(low_back(attended))
    middle = slot_in + low_back(exact_dot(attended, w_out) + bias_out)
    normed_two = low(layer_norm(middle, gain_two, shift_two))
    pre_act = low_back(exact_dot(normed_two, w_up) + bias_up)
    activated = low(jax.nn.gelu(pre_act, approximate=True))
    return middle + low_back(exact_dot(activated, w_down) + bias_down)

def reference(hidden_in, seq_lengths, out_cotangent, norm1_gain, norm1_shift, qkv_weight, qv_bias, out_weight, out_bias, norm2_gain, norm2_shift, up_weight, up_bias, down_weight, down_bias):
    params = (norm1_gain.astype(jnp.float32), norm1_shift.astype(jnp.float32), qkv_weight.astype(jnp.float32), qv_bias.astype(jnp.float32), out_weight.astype(jnp.float32), out_bias.astype(jnp.float32), norm2_gain.astype(jnp.float32), norm2_shift.astype(jnp.float32), up_weight.astype(jnp.float32), up_bias.astype(jnp.float32), down_weight.astype(jnp.float32), down_bias.astype(jnp.float32))
    positions = jnp.arange(SLOT_LEN)

    def per_slot(totals, inputs):
        slot_in, slot_len, slot_cot = inputs

        def forward(values_in, param_set):
            return slot_forward(values_in, slot_len, param_set)
        output, pullback = jax.vjp(forward, slot_in.astype(jnp.float32), params)
        rowmask = (positions < slot_len).astype(jnp.float32)[:, None]
        grad_in, grad_params = pullback(slot_cot.astype(jnp.float32) * rowmask)
        totals = jax.tree.map(lambda tensor_a, tensor_b: tensor_a + tensor_b, totals, grad_params)
        return (totals, (output.astype(jnp.bfloat16), grad_in.astype(jnp.bfloat16)))
    zero_grads = jax.tree.map(jnp.zeros_like, params)
    totals, (outputs, grad_inputs) = lax.scan(per_slot, zero_grads, (hidden_in, seq_lengths, out_cotangent))
    return (outputs, grad_inputs, totals[0], totals[1], totals[2], totals[3], totals[4], totals[5], totals[6], totals[7], totals[8], totals[9], totals[10], totals[11])
```

```python
import functools

import jax
import jax.numpy as jnp
from jax import lax
from jax.experimental import pallas as pl
from jax.experimental.pallas import tpu as pltpu
from jax.sharding import PartitionSpec as P

HEADS = 8
HEAD_DIM = 64
EPS = 1e-05
LOG2E = 1.4426950408889634
LN2 = 0.6931471805599453
LOW = -1e30
TOP = 1e30
f32 = jnp.float32
bf16 = jnp.bfloat16


def dot(left, right, left_dim, right_dim):
    return lax.dot_general(left, right, (((left_dim,), (right_dim,)), ((), ())), preferred_element_type=f32)


def split_three(values):
    one = values.astype(bf16)
    rest = values - one.astype(f32)
    two = rest.astype(bf16)
    return one, two, (rest - two.astype(f32)).astype(bf16)


def forward_kernel(count_ref, qa_ref, qb_ref, ka_ref, kb_ref, va_ref, vb_ref, o_ref, stat_ref, p_ref, keys, values, *, blk):
    chunk = pl.program_id(1)
    rows = qa_ref.shape[1]
    span = keys.shape[0]
    alive = count_ref[0] + count_ref[1] > 0

    @pl.when(jnp.logical_and(alive, chunk == 0))
    def _():
        pos = lax.broadcasted_iota(jnp.int32, (HEAD_DIM, rows), 1)
        row = lax.broadcasted_iota(jnp.int32, (HEAD_DIM, rows), 0)
        low_row = lax.broadcasted_iota(jnp.int32, (16, rows), 0)
        for part, (k_ref, v_ref) in enumerate(((ka_ref, va_ref), (kb_ref, vb_ref))):
            mask = jnp.where(pos < count_ref[part], 0.0, LOW)
            extra = jnp.where(row < 3, 1.0, jnp.where(row == 3, mask, 0.0)).astype(bf16)
            keys[pl.ds(part * rows, rows), :] = jnp.concatenate([k_ref[...], extra], 0).T
            values[0:HEAD_DIM, pl.ds(part * rows, rows)] = v_ref[...]
            values[HEAD_DIM : HEAD_DIM + 16, pl.ds(part * rows, rows)] = jnp.where(low_row == 0, 1.0, 0.0).astype(bf16)

    @pl.when(jnp.logical_not(alive))
    def _():
        o_ref[...] = jnp.zeros_like(o_ref)
        stat_row = lax.broadcasted_iota(jnp.int32, (8, rows), 0)
        stat_ref[0] = jnp.where(stat_row == 1, LOW, 0.0)

    @pl.when(alive)
    def _():
        query = jnp.where(chunk == 0, qa_ref[...], qb_ref[...])
        row = lax.broadcasted_iota(jnp.int32, (HEAD_DIM, rows), 0)
        head_blk = min(256, rows)

        def extend(top):
            one, two, three = [jnp.broadcast_to(-x.astype(f32), (HEAD_DIM, rows)) for x in split_three(top)]
            extra = jnp.where(row == 0, one, jnp.where(row == 1, two, jnp.where(row == 2, three, jnp.where(row == 3, 1.0, 0.0))))
            return jnp.concatenate([query, extra.astype(bf16)], 0)

        plain = extend(jnp.zeros((1, rows), f32))
        start = pl.multiple_of(count_ref[2], head_blk)
        guess = jnp.max(dot(keys[pl.ds(start, head_blk), :], plain, 1, 0), axis=0, keepdims=True)

        def run(top, unroll):
            query_ext = extend(top)

            def body(step, total):
                off = step * blk if isinstance(step, int) else pl.multiple_of(step * blk, blk)
                probs = jnp.exp2(dot(keys[pl.ds(off, blk), :], query_ext, 1, 0)).astype(bf16)
                p_ref[0, 0, pl.ds(off, blk), :] = probs
                return total + dot(values[:, pl.ds(off, blk)], probs, 1, 0)

            total = jnp.zeros((HEAD_DIM + 16, rows), f32)
            if unroll:
                for step in range(span // blk):
                    total = body(step, total)
            else:
                total = lax.fori_loop(0, span // blk, body, total)
            sums = total[HEAD_DIM : HEAD_DIM + 1]
            stat_ref[0] = jnp.concatenate([sums, top, jnp.zeros((6, rows), f32)], 0)
            o_ref[...] = total[0:HEAD_DIM]
            return jnp.max(sums)

        largest = run(guess, True)

        @pl.when(jnp.logical_not(largest < TOP))
        def _():
            def wider(step, top):
                off = pl.multiple_of(step * head_blk, head_blk)
                return jnp.maximum(top, jnp.max(dot(keys[pl.ds(off, head_blk), :], plain, 1, 0), axis=0, keepdims=True))

            run(lax.fori_loop(0, span // head_blk, wider, jnp.full((1, rows), LOW, f32)), False)


def attend(counts, query_a, query_b, key_a, key_b, heads):
    rows = query_a.shape[1]
    span = 2 * rows
    blk = min(512, rows)
    spec = lambda base: pl.BlockSpec((HEAD_DIM, rows), lambda h, i, n: (base + h, 0))
    return pl.pallas_call(
        functools.partial(forward_kernel, blk=blk),
        grid_spec=pltpu.PrefetchScalarGridSpec(
            num_scalar_prefetch=1,
            grid=(heads, 2),
            in_specs=[spec(0), spec(0), spec(heads), spec(heads), spec(2 * heads), spec(2 * heads)],
            out_specs=[
                pl.BlockSpec((HEAD_DIM, rows), lambda h, i, n: (h, i)),
                pl.BlockSpec((1, 8, rows), lambda h, i, n: (h, 0, i)),
                pl.BlockSpec((1, 1, span, rows), lambda h, i, n: (h, i, 0, 0)),
            ],
            scratch_shapes=[pltpu.VMEM((span, 2 * HEAD_DIM), bf16), pltpu.VMEM((HEAD_DIM + 16, span), bf16)],
        ),
        out_shape=[
            jax.ShapeDtypeStruct((heads * HEAD_DIM, span), f32),
            jax.ShapeDtypeStruct((heads, 8, span), f32),
            jax.ShapeDtypeStruct((heads, 2, span, rows), bf16),
        ],
        cost_estimate=pl.CostEstimate(
            flops=16 * heads * span * span * HEAD_DIM, bytes_accessed=2 * heads * span * span, transcendentals=heads * span * span
        ),
        name="attend",
    )(counts, query_a, query_b, key_a, key_b, key_a, key_b)


def backward_kernel(
    count_ref, qa_ref, qb_ref, ka_ref, kb_ref, va_ref, vb_ref, ga_ref, gb_ref, o_ref, f_ref, p_ref,
    dq_ref, dk_ref, dv_ref, values, dk_sum, dv_sum, *, blk,
):
    chunk = pl.program_id(1)
    rows = qa_ref.shape[1]
    span = values.shape[0]
    alive = count_ref[0] + count_ref[1] > 0
    row = lax.broadcasted_iota(jnp.int32, (HEAD_DIM, rows), 0)

    @pl.when(chunk == 0)
    def _():
        extra = jnp.where(row < 3, 1.0, 0.0).astype(bf16)
        for part, v_ref in enumerate((va_ref, vb_ref)):
            values[pl.ds(part * rows, rows), :] = jnp.concatenate([v_ref[...], extra], 0).T
        dk_sum[...] = jnp.zeros_like(dk_sum)
        dv_sum[...] = jnp.zeros_like(dv_sum)

    @pl.when(jnp.logical_not(alive))
    def _():
        dq_ref[...] = jnp.zeros_like(dq_ref)

    @pl.when(alive)
    def _():
        query = jnp.where(chunk == 0, qa_ref[...], qb_ref[...])
        grad = jnp.where(chunk == 0, ga_ref[...], gb_ref[...])
        grad = (grad.astype(f32) * f_ref[0, 0:1]).astype(bf16)
        delta = jnp.sum(grad.astype(f32) * o_ref[...], axis=0, keepdims=True)
        one, two, three = [jnp.broadcast_to(-x.astype(f32), (HEAD_DIM, rows)) for x in split_three(delta)]
        extra = jnp.where(row == 0, one, jnp.where(row == 1, two, jnp.where(row == 2, three, 0.0))).astype(bf16)
        grad_ext = jnp.concatenate([grad, extra], 0)
        dq = jnp.zeros((HEAD_DIM, rows), f32)
        for step in range(span // blk):
            off = step * blk
            probs = p_ref[0, 0, pl.ds(off, blk), :]
            grad_scores = (probs.astype(f32) * dot(values[pl.ds(off, blk), :], grad_ext, 1, 0)).astype(bf16)
            k_ref = (ka_ref, kb_ref)[off // rows]
            dq = dq + dot(k_ref[:, pl.ds(off % rows, blk)], grad_scores, 1, 0)
            dv_sum[:, pl.ds(off, blk)] += dot(grad, probs, 1, 1)
            dk_sum[:, pl.ds(off, blk)] += dot(query, grad_scores, 1, 1)
        dq_ref[...] = dq

    @pl.when(chunk == pl.num_programs(1) - 1)
    def _():
        dk_ref[...] = (dk_sum[...] * LN2).astype(dk_ref.dtype)
        dv_ref[...] = dv_sum[...].astype(dv_ref.dtype)


def attend_back(counts, query_a, query_b, key_a, key_b, grad_a, grad_b, out_t, factor, probs, heads, sum_type):
    rows = query_a.shape[1]
    span = 2 * rows
    blk = min(512, rows)
    spec = lambda base: pl.BlockSpec((HEAD_DIM, rows), lambda h, i, n: (base + h, 0))
    whole = pl.BlockSpec((HEAD_DIM, span), lambda h, i, n: (h, 0))
    part = pl.BlockSpec((HEAD_DIM, rows), lambda h, i, n: (h, i))
    return pl.pallas_call(
        functools.partial(backward_kernel, blk=blk),
        grid_spec=pltpu.PrefetchScalarGridSpec(
            num_scalar_prefetch=1,
            grid=(heads, 2),
            in_specs=[
                spec(0), spec(0), spec(heads), spec(heads), spec(2 * heads), spec(2 * heads), spec(0), spec(0),
                part,
                pl.BlockSpec((1, 8, rows), lambda h, i, n: (h, 0, i)),
                pl.BlockSpec((1, 1, span, rows), lambda h, i, n: (h, i, 0, 0)),
            ],
            out_specs=[part, whole, whole],
            scratch_shapes=[
                pltpu.VMEM((span, 2 * HEAD_DIM), bf16),
                pltpu.VMEM((HEAD_DIM, span), f32),
                pltpu.VMEM((HEAD_DIM, span), f32),
            ],
        ),
        out_shape=[
            jax.ShapeDtypeStruct((heads * HEAD_DIM, span), f32),
            jax.ShapeDtypeStruct((heads * HEAD_DIM, span), sum_type),
            jax.ShapeDtypeStruct((heads * HEAD_DIM, span), sum_type),
        ],
        cost_estimate=pl.CostEstimate(
            flops=32 * heads * span * span * HEAD_DIM, bytes_accessed=2 * heads * span * span, transcendentals=0
        ),
        name="attend_back",
    )(counts, query_a, query_b, key_a, key_b, key_a, key_b, grad_a, grad_b, out_t, factor, probs)


def swap(values, axis, flip):
    size = lax.axis_size(axis)
    return lax.ppermute(values, axis, [(i, i ^ flip) for i in range(size)])


def place(pieces, index, count):
    shape = pieces[0].shape
    stacked = jnp.zeros((count,) + shape, pieces[0].dtype)
    for k, piece in enumerate(pieces):
        stacked = lax.dynamic_update_slice_in_dim(stacked, piece[None], index ^ k, 0)
    return stacked


def gather_bits(values, axis, shift, count):
    index = (lax.axis_index(axis) >> shift) & (count - 1)
    pieces = [values] + [swap(values, axis, k << shift) for k in range(1, count)]
    return place(pieces, index, count)


def scatter_bits(values, axis, shift, count):
    index = (lax.axis_index(axis) >> shift) & (count - 1)
    pick = lambda k: lax.dynamic_index_in_dim(values, index ^ k, 0, keepdims=False)
    total = pick(0).astype(f32)
    for k in range(1, count):
        total = total + swap(pick(k).astype(bf16), axis, k << shift).astype(f32)
    return total


def gelu_and_slope(u):
    a = 0.7978845608028654
    inner = a * (u + 0.044715 * u * u * u)
    t = jnp.tanh(inner)
    slope = 0.5 * (1 + t) + 0.5 * u * (1 - t * t) * a * (1 + 3 * 0.044715 * u * u)
    return 0.5 * u * (1 + t), slope


def norm_parts(inputs):
    center = inputs - jnp.mean(inputs, axis=-1, keepdims=True)
    scale = lax.rsqrt(jnp.mean(center * center, axis=-1, keepdims=True) + EPS)
    return center * scale, scale


def norm_back(grad, hat, scale, gain):
    e = grad * gain
    return scale * (e - jnp.mean(e, axis=-1, keepdims=True) - hat * jnp.mean(e * hat, axis=-1, keepdims=True))


def on_device(
    hidden_in, seq_lengths, out_cotangent, norm1_gain, norm1_shift, qkv_weight, qv_bias, out_weight, out_bias,
    norm2_gain, norm2_shift, up_weight, up_bias, down_weight, down_bias,
):
    rows, width = hidden_in.shape[1:]
    hidden_in, out_cotangent = hidden_in[0], out_cotangent[0]
    ff = up_weight.shape[1]
    dp, ctx = lax.axis_size("dp"), lax.axis_size("ctx")
    dp_low = 2 if dp == 8 else 4
    ring = ctx // 2
    me = lax.axis_index("ctx")
    core = me % 2
    half_heads = HEADS // 2
    half = half_heads * HEAD_DIM
    shard = width // dp
    length = seq_lengths[0]

    def by_core(cols):
        return cols.reshape(cols.shape[:-1] + (3, 2, half)).swapaxes(-3, -2).reshape(cols.shape)

    def from_core(cols):
        return cols.reshape(cols.shape[:-1] + (2, 3, half)).swapaxes(-3, -2).reshape(cols.shape)

    small = jnp.concatenate([norm1_gain, norm1_shift, out_bias, norm2_gain, norm2_shift, down_bias, qv_bias[0], qv_bias[1], up_bias])[None]
    small = gather_bits(gather_bits(small, "dp", dp_low.bit_length() - 1, dp // dp_low), "dp", 0, dp_low)
    small = small.swapaxes(0, 1).reshape(dp, -1)
    vector = lambda at: small[:, at * shard : (at + 1) * shard].reshape(width).astype(f32)
    gain_one, shift_one, bias_out, gain_two, shift_two, bias_down, bias_q, bias_v = [vector(at) for at in range(8)]
    bias_up = small[:, 8 * shard :].reshape(ff).astype(f32)

    piece = lax.dynamic_slice_in_dim(qkv_weight, me * (shard // ctx), shard // ctx, 0)
    piece = by_core(piece)
    piece = gather_bits(piece, "dp", dp_low.bit_length() - 1, dp // dp_low)
    piece = gather_bits(piece, "dp", 0, dp_low)
    piece = gather_bits(piece, "ctx", 1, ring)
    piece = gather_bits(piece, "ctx", 0, 2)
    w_qkv = piece.transpose(3, 2, 1, 0, 4, 5).reshape(width, 3 * width)

    rest = jnp.concatenate([out_weight, down_weight] + [up_weight[:, j * width : (j + 1) * width] for j in range(ff // width)], 0)
    rest, w_qkv = lax.optimization_barrier((rest, w_qkv))
    rest = lax.all_gather(rest, "dp", axis=0, tiled=False)
    w_out = rest[:, :shard].reshape(width, width)
    w_down = rest[:, shard : shard + ff // dp].reshape(ff, width)
    w_up = rest[:, shard + ff // dp :].reshape(dp, ff // width, shard, width).swapaxes(1, 2).reshape(width, ff)

    residual = hidden_in.astype(f32)
    hat_one, scale_one = norm_parts(residual)
    normed_one = (hat_one * gain_one + shift_one).astype(bf16)
    bias_full = by_core(jnp.concatenate([bias_q, jnp.zeros_like(bias_q), bias_v]))
    factors = by_core(jnp.concatenate([jnp.full((width,), LOG2E * HEAD_DIM**-0.5, f32), jnp.ones((2 * width,), f32)]))
    projected = ((dot(w_qkv, normed_one, 0, 1) + bias_full[:, None]) * factors[:, None]).astype(bf16)
    projected = projected.reshape(2, 3 * half, rows)
    mine = lax.dynamic_index_in_dim(projected, core, 0, keepdims=False)
    theirs = swap(lax.dynamic_index_in_dim(projected, 1 - core, 0, keepdims=False), "ctx", 1)

    def counts_of(source):
        first = jnp.clip(length - source * rows, 0, rows)
        second = jnp.clip(length - (source ^ 1) * rows, 0, rows)
        return jnp.stack([first, second, (source % 2) * rows]).astype(jnp.int32)

    sources = [(mine, theirs)] + [(swap(mine, "ctx", 2 * k), swap(theirs, "ctx", 2 * k)) for k in range(1, ring)]
    counts = [counts_of(me ^ (2 * k)) for k in range(ring)]
    parts = [attend(counts[k], mine, theirs, *sources[k], half_heads) for k in range(ring)]
    tops = [stat[:, 1:2] for _, stat, _ in parts]
    top = functools.reduce(jnp.maximum, tops)
    shares = [jnp.exp2(t - top) for t in tops]
    total = sum(share * stat[:, 0:1] for share, (_, stat, _) in zip(shares, parts))
    factor = [jnp.broadcast_to(share / total, (half_heads, 8, 2 * rows)) for share in shares]
    attended = sum(o.reshape(half_heads, HEAD_DIM, 2 * rows) * fac[:, 0:1] for fac, (o, _, _) in zip(factor, parts)).reshape(half, 2 * rows)
    attended_low = attended.astype(bf16)
    from_mine, from_theirs = attended_low[:, :rows], swap(attended_low[:, rows:], "ctx", 1)
    order = lambda a, b: jnp.concatenate([jnp.where(core == 0, a, b), jnp.where(core == 0, b, a)], 0)
    attended_t = order(from_mine, from_theirs)

    middle = residual + dot(attended_t, w_out, 0, 0) + bias_out
    hat_two, scale_two = norm_parts(middle)
    normed_two = (hat_two * gain_two + shift_two).astype(bf16)
    activated, slope = gelu_and_slope(dot(normed_two, w_up, 1, 0) + bias_up)
    activated = activated.astype(bf16)
    hidden_out = (middle + dot(activated, w_down, 1, 0) + bias_down).astype(bf16)
    row_valid = (me * rows + lax.iota(jnp.int32, rows) < length)[:, None]
    grad_z = jnp.where(row_valid, out_cotangent, jnp.zeros_like(out_cotangent))
    grad_out = grad_z.astype(f32)
    grad_w_down = dot(activated, grad_z, 0, 0)
    grad_pre = (dot(grad_z, w_down, 1, 1) * slope).astype(bf16)
    grad_w_up = dot(normed_two, grad_pre, 0, 0)
    grad_norm_two = dot(grad_pre, w_up, 1, 1)
    grad_mid = grad_out + norm_back(grad_norm_two, hat_two, scale_two, gain_two)
    grad_branch = grad_mid.astype(bf16)
    grad_w_out = dot(attended_t, grad_branch, 1, 0)
    grad_att = dot(w_out, grad_branch, 1, 1).astype(bf16).reshape(2, half, rows)
    grad_mine = lax.dynamic_index_in_dim(grad_att, core, 0, keepdims=False)
    grad_theirs = swap(lax.dynamic_index_in_dim(grad_att, 1 - core, 0, keepdims=False), "ctx", 1)

    up_rows = grad_w_up.astype(bf16).reshape(dp, shard, ff // width, width).swapaxes(1, 2).reshape(dp, -1, width)
    packed = jnp.concatenate([grad_w_out.astype(bf16).reshape(dp, shard, width), grad_w_down.astype(bf16).reshape(dp, -1, width), up_rows], 1)
    packed = lax.psum_scatter(packed, "dp", scatter_dimension=0, tiled=False)

    backs = [None] * ring
    for k in range(ring - 1, -1, -1):
        backs[k] = attend_back(
            counts[k], mine, theirs, *sources[k], grad_mine, grad_theirs, attended, factor[k], parts[k][2], half_heads, f32 if k == 0 else bf16
        )
    grad_q = sum(b[0] for b in backs) * HEAD_DIM**-0.5
    grad_k, grad_v = backs[0][1], backs[0][2]
    for k in range(1, ring):
        grad_k = grad_k + swap(backs[k][1], "ctx", 2 * k).astype(f32)
        grad_v = grad_v + swap(backs[k][2], "ctx", 2 * k).astype(f32)
    grad_p = jnp.concatenate([grad_q, grad_k, grad_v], 0).astype(bf16)
    grad_p = order(grad_p[:, :rows], swap(grad_p[:, rows:], "ctx", 1))

    grad_w_qkv = dot(normed_one, grad_p, 0, 1)
    grad_norm_one = dot(grad_p, w_qkv, 0, 1)
    grad_hidden = (grad_mid + norm_back(grad_norm_one, hat_one, scale_one, gain_one)).astype(bf16)

    full = lambda x: jnp.sum(x.astype(f32), axis=0).reshape(dp, -1)
    bias_sums = from_core(jnp.sum(grad_p.astype(f32), axis=1))
    smalls = jnp.concatenate(
        [
            full(grad_norm_one * hat_one),
            full(grad_norm_one),
            full(grad_branch),
            full(grad_norm_two * hat_two),
            full(grad_norm_two),
            full(grad_z),
            bias_sums[:width].reshape(dp, -1),
            bias_sums[2 * width :].reshape(dp, -1),
            full(grad_pre),
        ],
        1,
    )
    for flip in [1 << b for b in range(ctx.bit_length() - 1)]:
        smalls = smalls + swap(smalls, "ctx", flip)
    smalls = smalls.reshape(dp // dp_low, dp_low, 1, -1)
    smalls = scatter_bits(smalls.swapaxes(0, 1), "dp", 0, dp_low)
    smalls = scatter_bits(smalls, "dp", dp_low.bit_length() - 1, dp // dp_low)[0]

    pieces = grad_w_qkv.astype(bf16).reshape(dp // dp_low, dp_low, ring, 2, shard // ctx, 3 * width).transpose(3, 2, 1, 0, 4, 5)
    pieces = scatter_bits(pieces, "ctx", 0, 2)
    pieces = scatter_bits(pieces, "ctx", 1, ring)
    pieces = scatter_bits(pieces, "dp", 0, dp_low)
    pieces = scatter_bits(pieces, "dp", dp_low.bit_length() - 1, dp // dp_low)
    pieces = gather_bits(gather_bits(pieces.astype(bf16), "ctx", 1, ring), "ctx", 0, 2)
    grad_qkv = from_core(pieces.swapaxes(0, 1).reshape(shard, 3 * width)).astype(f32)

    packed = packed.astype(f32)
    for flip in [1 << b for b in range(ctx.bit_length() - 1)]:
        packed = packed + swap(packed.astype(bf16), "ctx", flip).astype(f32)
    grad_down = packed[shard : shard + ff // dp]
    grad_up = packed[shard + ff // dp :].reshape(ff // width, shard, width).swapaxes(0, 1).reshape(shard, ff)
    small_out = lambda at: smalls[at * shard : (at + 1) * shard]
    return (
        hidden_out[None],
        grad_hidden[None],
        small_out(0),
        small_out(1),
        grad_qkv,
        jnp.stack([small_out(6), small_out(7)]),
        packed[:shard],
        small_out(2),
        small_out(3),
        small_out(4),
        grad_up,
        smalls[8 * shard :],
        grad_down,
        small_out(5),
    )


def solution(mesh):
    return jax.shard_map(
        on_device,
        mesh=mesh,
        in_specs=(
            P("dp", "ctx", None), P("dp"), P("dp", "ctx", None), P("dp"), P("dp"), P("dp", None), P(None, "dp"),
            P("dp", None), P("dp"), P("dp"), P("dp"), P("dp", None), P("dp"), P("dp", None), P("dp"),
        ),
        out_specs=(
            P("dp", "ctx", None), P("dp", "ctx", None), P("dp"), P("dp"), P("dp", None), P(None, "dp"), P("dp", None),
            P("dp"), P("dp"), P("dp"), P("dp", None), P("dp"), P("dp", None), P("dp"),
        ),
        check_vma=False,
    )
```

```python
import functools

import jax
import jax.numpy as jnp
from jax import lax
from jax.experimental import pallas as pl
from jax.experimental.pallas import tpu as pltpu
from jax.sharding import PartitionSpec as P

HEADS = 8
HEAD_DIM = 64
EPS = 1e-05
LOG2E = 1.4426950408889634
LN2 = 0.6931471805599453
LOW = -1e30
TOP = 1e30
f32 = jnp.float32
bf16 = jnp.bfloat16


def dot(left, right, left_dim, right_dim):
    return lax.dot_general(left, right, (((left_dim,), (right_dim,)), ((), ())), preferred_element_type=f32)


def split_three(values):
    one = values.astype(bf16)
    rest = values - one.astype(f32)
    two = rest.astype(bf16)
    return one, two, (rest - two.astype(f32)).astype(bf16)


def forward_kernel(count_ref, qa_ref, qb_ref, ka_ref, kb_ref, va_ref, vb_ref, *rest, blk, first, last, aliases):
    prev, rest = ((None, None), rest) if first else (rest[:2], rest[2:])
    rest = rest[aliases:]
    low_ref, rest = (rest[0], rest[1:]) if last else (None, rest)
    o_ref, stat_ref, own_ref, p_ref, keys, values = rest
    chunk = pl.program_id(1)
    rows = qa_ref.shape[1]
    span = keys.shape[0]
    alive = count_ref[0] + count_ref[1] > 0

    def finish(out, sums, top):
        own_ref[0] = jnp.broadcast_to(top, (8, rows))
        if not first:
            old_sums, old_top = prev[1][0, 0:1], prev[1][0, 1:2]
            new_top = jnp.maximum(top, old_top)
            scale, old_scale = jnp.exp2(top - new_top), jnp.exp2(old_top - new_top)
            out = out * scale + prev[0][...] * old_scale
            sums = sums * scale + old_sums * old_scale
            top = new_top
        stat_ref[0] = jnp.concatenate([sums, top, jnp.zeros((6, rows), f32)], 0)
        if last:
            out = out / sums
            low_ref[...] = out.astype(bf16)
        o_ref[...] = out

    @pl.when(jnp.logical_and(alive, chunk == 0))
    def _():
        pos = lax.broadcasted_iota(jnp.int32, (HEAD_DIM, rows), 1)
        row = lax.broadcasted_iota(jnp.int32, (HEAD_DIM, rows), 0)
        for part, (k_ref, v_ref) in enumerate(((ka_ref, va_ref), (kb_ref, vb_ref))):
            mask = jnp.where(pos < count_ref[part], 0.0, LOW)
            extra = jnp.where(row < 3, 1.0, jnp.where(row == 3, mask, 0.0)).astype(bf16)
            keys[pl.ds(part * rows, rows), :] = jnp.concatenate([k_ref[...], extra], 0).T
            values[:, pl.ds(part * rows, rows)] = v_ref[...]

    @pl.when(jnp.logical_not(alive))
    def _():
        finish(jnp.zeros((HEAD_DIM, rows), f32), jnp.zeros((1, rows), f32), jnp.full((1, rows), LOW, f32))

    @pl.when(alive)
    def _():
        query = jnp.where(chunk == 0, qa_ref[...], qb_ref[...])
        row = lax.broadcasted_iota(jnp.int32, (HEAD_DIM, rows), 0)
        head_blk = 64

        def extend(top):
            one, two, three = [jnp.broadcast_to(-x.astype(f32), (HEAD_DIM, rows)) for x in split_three(top)]
            extra = jnp.where(row == 0, one, jnp.where(row == 1, two, jnp.where(row == 2, three, jnp.where(row == 3, 1.0, 0.0))))
            return jnp.concatenate([query, extra.astype(bf16)], 0)

        plain = extend(jnp.zeros((1, rows), f32))
        start = pl.multiple_of(count_ref[2], head_blk)
        guess = jnp.max(dot(keys[pl.ds(start, head_blk), :], plain, 1, 0), axis=0, keepdims=True)

        def run(top, unroll):
            query_ext = extend(top)

            def body(step, carry):
                total, sums = carry
                off = step * blk if isinstance(step, int) else pl.multiple_of(step * blk, blk)
                wide = jnp.exp2(dot(keys[pl.ds(off, blk), :], query_ext, 1, 0))
                probs = wide.astype(bf16)
                p_ref[0, 0, pl.ds(off, blk), :] = probs
                sums = sums + jnp.sum(wide.reshape(blk // 8, 8, rows), axis=0)
                return total + dot(values[:, pl.ds(off, blk)], probs, 1, 0), sums

            carry = jnp.zeros((HEAD_DIM, rows), f32), jnp.zeros((8, rows), f32)
            if unroll:
                for step in range(span // blk):
                    carry = body(step, carry)
            else:
                carry = lax.fori_loop(0, span // blk, body, carry)
            sums = jnp.sum(carry[1], axis=0, keepdims=True)
            finish(carry[0], sums, top)
            return jnp.max(sums)

        largest = run(guess, True)

        @pl.when(jnp.logical_not(largest < TOP))
        def _():
            def wider(step, top):
                off = pl.multiple_of(step * head_blk, head_blk)
                return jnp.maximum(top, jnp.max(dot(keys[pl.ds(off, head_blk), :], plain, 1, 0), axis=0, keepdims=True))

            run(lax.fori_loop(0, span // head_blk, wider, jnp.full((1, rows), LOW, f32)), False)


def head_rows(base, step, rows):
    return pl.BlockSpec((HEAD_DIM, rows), lambda h, i, n: (base + step * h, 0))


def attend(counts, query_a, query_b, key_a, key_b, kv_base, first_head, heads, prev, low, last):
    rows = query_a.shape[1]
    span = 2 * rows
    blk = min(512, rows)
    keys, vals, ask = head_rows(kv_base, 2, rows), head_rows(kv_base + 1, 2, rows), head_rows(first_head, 1, rows)
    out_spec = pl.BlockSpec((HEAD_DIM, rows), lambda h, i, n: (first_head + h, i))
    stat_spec = pl.BlockSpec((1, 8, rows), lambda h, i, n: (first_head + h, 0, i))
    all_heads = HEADS // 2
    extra_in = [out_spec, stat_spec] if prev else []
    extra_args = list(prev) if prev else []
    if low is not None:
        extra_in, extra_args = extra_in + [pl.BlockSpec(memory_space=pl.ANY)], extra_args + [low]
    out_specs = [out_spec, stat_spec, pl.BlockSpec((1, 8, rows), lambda h, i, n: (h, 0, i)), pl.BlockSpec((1, 1, span, rows), lambda h, i, n: (h, i, 0, 0))]
    out_shape = [
        jax.ShapeDtypeStruct((all_heads * HEAD_DIM, span), f32),
        jax.ShapeDtypeStruct((all_heads, 8, span), f32),
        jax.ShapeDtypeStruct((heads, 8, span), f32),
        jax.ShapeDtypeStruct((heads, 2, span, rows), bf16),
    ]
    shift = 1 if last else 0
    if last:
        out_specs, out_shape = [out_spec] + out_specs, [jax.ShapeDtypeStruct((all_heads * HEAD_DIM, span), bf16)] + out_shape
    alias = {7: shift, 8: shift + 1} if prev else {}
    if low is not None:
        alias = {**alias, 9: 0}
    return pl.pallas_call(
        functools.partial(forward_kernel, blk=blk, first=not prev, last=last, aliases=0 if low is None else 1),
        grid_spec=pltpu.PrefetchScalarGridSpec(
            num_scalar_prefetch=1,
            grid=(heads, 2),
            in_specs=[ask, ask, keys, keys, vals, vals] + extra_in,
            out_specs=out_specs,
            scratch_shapes=[pltpu.VMEM((span, 2 * HEAD_DIM), bf16), pltpu.VMEM((HEAD_DIM, span), bf16)],
        ),
        out_shape=out_shape,
        input_output_aliases=alias,
        cost_estimate=pl.CostEstimate(
            flops=16 * heads * span * span * HEAD_DIM, bytes_accessed=2 * heads * span * span, transcendentals=heads * span * span
        ),
        name="attend",
    )(counts, query_a, query_b, key_a, key_b, key_a, key_b, *extra_args)


def backward_kernel(
    count_ref, qa_ref, qb_ref, ka_ref, kb_ref, va_ref, vb_ref, ga_ref, gb_ref, o_ref, stat_ref, own_ref, p_ref,
    *rest, blk, adds, aliases, last,
):
    before_ref, rest = (rest[0], rest[1:]) if adds else (None, rest)
    dq_ref, dkv_ref, values, dk_sum, dv_sum = rest[aliases:]
    chunk = pl.program_id(1)
    rows = qa_ref.shape[1]
    span = values.shape[0]
    alive = count_ref[0] + count_ref[1] > 0
    row = lax.broadcasted_iota(jnp.int32, (HEAD_DIM, rows), 0)

    def finish(dq):
        if adds:
            dq = dq + before_ref[...]
        if last:
            dq = dq * HEAD_DIM**-0.5
        dq_ref[...] = dq.astype(dq_ref.dtype)

    @pl.when(chunk == 0)
    def _():
        extra = jnp.where(row < 3, 1.0, 0.0).astype(bf16)
        for part, v_ref in enumerate((va_ref, vb_ref)):
            values[pl.ds(part * rows, rows), :] = jnp.concatenate([v_ref[...], extra], 0).T
        dk_sum[...] = jnp.zeros_like(dk_sum)
        dv_sum[...] = jnp.zeros_like(dv_sum)

    @pl.when(jnp.logical_not(alive))
    def _():
        finish(jnp.zeros((HEAD_DIM, rows), f32))

    @pl.when(alive)
    def _():
        query = jnp.where(chunk == 0, qa_ref[...], qb_ref[...])
        grad = jnp.where(chunk == 0, ga_ref[...], gb_ref[...])
        factor = jnp.exp2(own_ref[0, 0:1] - stat_ref[0, 1:2]) / stat_ref[0, 0:1]
        grad = (grad.astype(f32) * factor).astype(bf16)
        delta = jnp.sum(grad.astype(f32) * o_ref[...], axis=0, keepdims=True)
        one, two, three = [jnp.broadcast_to(-x.astype(f32), (HEAD_DIM, rows)) for x in split_three(delta)]
        extra = jnp.where(row == 0, one, jnp.where(row == 1, two, jnp.where(row == 2, three, 0.0))).astype(bf16)
        grad_ext = jnp.concatenate([grad, extra], 0)
        dq = jnp.zeros((HEAD_DIM, rows), f32)
        for step in range(span // blk):
            off = step * blk
            probs = p_ref[0, 0, pl.ds(off, blk), :]
            grad_scores = (probs.astype(f32) * dot(values[pl.ds(off, blk), :], grad_ext, 1, 0)).astype(bf16)
            k_ref = (ka_ref, kb_ref)[off // rows]
            dq = dq + dot(k_ref[:, pl.ds(off % rows, blk)], grad_scores, 1, 0)
            dv_sum[:, pl.ds(off, blk)] += dot(grad, probs, 1, 1)
            dk_sum[:, pl.ds(off, blk)] += dot(query, grad_scores, 1, 1)
        finish(dq)

    @pl.when(chunk == pl.num_programs(1) - 1)
    def _():
        dkv_ref[0, 0] = (dk_sum[...] * LN2).astype(dkv_ref.dtype)
        dkv_ref[0, 1] = dv_sum[...].astype(dkv_ref.dtype)


def attend_back(counts, query_a, query_b, key_a, key_b, kv_base, first_head, heads, grad_a, grad_b, attended, stat, own, probs, before, last):
    rows = query_a.shape[1]
    span = 2 * rows
    blk = min(512, rows)
    keys, vals, ask = head_rows(kv_base, 2, rows), head_rows(kv_base + 1, 2, rows), head_rows(first_head, 1, rows)
    part = pl.BlockSpec((HEAD_DIM, rows), lambda h, i, n: (first_head + h, i))
    buffer, adds = before
    alias, extra_in, extra_args = {}, [], []
    if adds:
        extra_in, extra_args = [part], [buffer]
        alias = {} if last else {13: 0}
    elif buffer is not None:
        extra_in, extra_args, alias = [pl.BlockSpec(memory_space=pl.ANY)], [buffer], {13: 0}
    return pl.pallas_call(
        functools.partial(backward_kernel, blk=blk, adds=adds, aliases=len(extra_in) - int(adds), last=last),
        grid_spec=pltpu.PrefetchScalarGridSpec(
            num_scalar_prefetch=1,
            grid=(heads, 2),
            in_specs=[
                ask, ask, keys, keys, vals, vals, ask, ask,
                part,
                pl.BlockSpec((1, 8, rows), lambda h, i, n: (first_head + h, 0, i)),
                pl.BlockSpec((1, 8, rows), lambda h, i, n: (h, 0, i)),
                pl.BlockSpec((1, 1, span, rows), lambda h, i, n: (h, i, 0, 0)),
            ] + extra_in,
            out_specs=[part, pl.BlockSpec((1, 2, HEAD_DIM, span), lambda h, i, n: (h, 0, 0, 0))],
            scratch_shapes=[
                pltpu.VMEM((span, 2 * HEAD_DIM), bf16),
                pltpu.VMEM((HEAD_DIM, span), f32),
                pltpu.VMEM((HEAD_DIM, span), f32),
            ],
        ),
        out_shape=[
            jax.ShapeDtypeStruct((HEADS // 2 * HEAD_DIM, span), bf16 if last else f32),
            jax.ShapeDtypeStruct((heads, 2, HEAD_DIM, span), f32 if last else bf16),
        ],
        input_output_aliases=alias,
        cost_estimate=pl.CostEstimate(
            flops=32 * heads * span * span * HEAD_DIM, bytes_accessed=2 * heads * span * span, transcendentals=0
        ),
        name="attend_back",
    )(counts, query_a, query_b, key_a, key_b, key_a, key_b, grad_a, grad_b, attended, stat, own, probs, *extra_args)


def middle_kernel(
    info_ref, mine_ref, theirs_ref, hidden_ref, cot_ref, w_ref, vec_ref,
    out_ref, grad_mid_ref, grad_mine_ref, grad_theirs_ref, packed_ref, sums_ref,
    total, act_s, slope_s, *, ff,
):
    step = pl.program_id(0)
    rows, width = hidden_ref.shape
    dp = w_ref.shape[0]
    shard = width // dp
    down_at, up_at = shard, shard + ff // dp
    own, other = info_ref[0], 1 - info_ref[0]
    halves = lambda which: (pl.ds(which * (dp // 2), dp // 2), pl.ds(0, shard), slice(None))
    down_rows = lambda j: (pl.ds(j * dp * width // ff, dp * width // ff), pl.ds(down_at, ff // dp), slice(None))
    up_rows = lambda j: (slice(None), pl.ds(up_at + j * shard, shard), slice(None))
    half = mine_ref.shape[0]
    blocks = ff // width

    @pl.when(step == 0)
    def _():
        total[...] = jnp.zeros_like(total)
        sums_ref[...] = jnp.zeros_like(sums_ref)

    w_mine = w_ref[halves(own)].reshape(half, width)
    w_theirs = w_ref[halves(other)].reshape(half, width)
    middle = hidden_ref[...].astype(f32) + dot(mine_ref[...], w_mine, 0, 0) + dot(theirs_ref[...], w_theirs, 0, 0) + vec_ref[0:1, 0:width]
    gain, shift, bias_down = [vec_ref[0:1, k * width : (k + 1) * width] for k in (1, 2, 3)]
    hat, scale = norm_parts(middle)
    normed = (hat * gain + shift).astype(bf16)
    out = middle + bias_down
    for j in range(blocks):
        cols = slice(j * width, (j + 1) * width)
        activated, slope = gelu_and_slope(dot(normed, w_ref[up_rows(j)].reshape(width, width), 1, 0) + vec_ref[1:2, cols])
        activated = activated.astype(bf16)
        act_s[:, cols] = activated
        slope_s[:, cols] = slope
        out = out + dot(activated, w_ref[down_rows(j)].reshape(width, width), 1, 0)
    out_ref[...] = out.astype(bf16)

    pos = step * rows + lax.broadcasted_iota(jnp.int32, (rows, width), 0)
    grad_z = jnp.where(pos < info_ref[1], cot_ref[...], jnp.zeros_like(cot_ref))
    grad_norm = jnp.zeros((rows, width), f32)
    for j in range(blocks):
        cols = slice(j * width, (j + 1) * width)
        grad_act = dot(grad_z, w_ref[down_rows(j)].reshape(width, width), 1, 1) * slope_s[:, cols]
        sums_ref[0:1, cols] += jnp.sum(grad_act, axis=0, keepdims=True)
        grad_pre = grad_act.astype(bf16)
        total[down_rows(j)] += dot(act_s[:, cols], grad_z, 0, 0).reshape(dp * width // ff, ff // dp, width)
        total[up_rows(j)] += dot(normed, grad_pre, 0, 0).reshape(dp, shard, width)
        grad_norm = grad_norm + dot(grad_pre, w_ref[up_rows(j)].reshape(width, width), 1, 1)
    grad_out = grad_z.astype(f32)
    grad_mid = grad_out + norm_back(grad_norm, hat, scale, gain)
    grad_mid_ref[...] = grad_mid
    branch = grad_mid.astype(bf16)
    for k, value in enumerate((branch.astype(f32), grad_norm * hat, grad_norm, grad_out)):
        sums_ref[1:2, k * width : (k + 1) * width] += jnp.sum(value, axis=0, keepdims=True)
    grad_mine_ref[...] = dot(w_mine, branch, 1, 1).astype(bf16)
    grad_theirs_ref[...] = dot(w_theirs, branch, 1, 1).astype(bf16)
    total[halves(own)] += dot(mine_ref[...], branch, 1, 0).reshape(dp // 2, shard, width)
    total[halves(other)] += dot(theirs_ref[...], branch, 1, 0).reshape(dp // 2, shard, width)

    @pl.when(step == pl.num_programs(0) - 1)
    def _():
        packed_ref[...] = total[...].astype(bf16)


def middle_part(info, mine, theirs, hidden, cot, weights, vectors, ff):
    half = mine.shape[0]
    rows, width = hidden.shape
    blk = min(512, rows)
    packed = weights.shape
    tall = pl.BlockSpec((blk, width), lambda i, n: (i, 0))
    wide = pl.BlockSpec((half, blk), lambda i, n: (0, i))
    fixed = lambda shape: pl.BlockSpec(shape, lambda i, n: (0,) * len(shape))
    return pl.pallas_call(
        functools.partial(middle_kernel, ff=ff),
        grid_spec=pltpu.PrefetchScalarGridSpec(
            num_scalar_prefetch=1,
            grid=(rows // blk,),
            in_specs=[wide, wide, tall, tall, fixed(packed), fixed(vectors.shape)],
            out_specs=[tall, tall, wide, wide, fixed(packed), fixed((8, ff))],
            scratch_shapes=[pltpu.VMEM(packed, f32), pltpu.VMEM((blk, ff), bf16), pltpu.VMEM((blk, ff), f32)],
        ),
        out_shape=[
            jax.ShapeDtypeStruct((rows, width), bf16),
            jax.ShapeDtypeStruct((rows, width), f32),
            jax.ShapeDtypeStruct((half, rows), bf16),
            jax.ShapeDtypeStruct((half, rows), bf16),
            jax.ShapeDtypeStruct(packed, bf16),
            jax.ShapeDtypeStruct((8, ff), f32),
        ],
        cost_estimate=pl.CostEstimate(flops=12 * rows * width * (2 * ff + width) // 2, bytes_accessed=16 << 20, transcendentals=rows * ff),
        name="middle",
    )(info, mine, theirs, hidden, cot, weights, vectors)


def tail_kernel(info_ref, mine_ref, theirs_ref, hidden_ref, mid_ref, w_ref, vec_ref, out_ref, dw_ref, sums_ref, total):
    step = pl.program_id(0)
    rows, width = hidden_ref.shape
    own, other = info_ref[0], 1 - info_ref[0]
    cols = mine_ref.shape[0]

    @pl.when(step == 0)
    def _():
        total[...] = jnp.zeros_like(total)
        sums_ref[...] = jnp.zeros_like(sums_ref)

    gain, shift = vec_ref[0:1, 0:width], vec_ref[0:1, width : 2 * width]
    hat, scale = norm_parts(hidden_ref[...].astype(f32))
    normed = (hat * gain + shift).astype(bf16)
    ones = jnp.where(lax.broadcasted_iota(jnp.int32, (16, rows), 0) == 0, 1.0, 0.0).astype(bf16)
    normed_t = jnp.concatenate([normed.T, ones], 0)
    total[pl.ds(own, 1)] += dot(normed_t, mine_ref[...], 1, 1)[None]
    total[pl.ds(other, 1)] += dot(normed_t, theirs_ref[...], 1, 1)[None]
    grad_norm = dot(w_ref[pl.ds(own, 1)].reshape(width, cols), mine_ref[...], 1, 0)
    grad_norm = (grad_norm + dot(w_ref[pl.ds(other, 1)].reshape(width, cols), theirs_ref[...], 1, 0)).T
    sums_ref[0:1, 0:width] += jnp.sum(grad_norm * hat, axis=0, keepdims=True)
    sums_ref[0:1, width : 2 * width] += jnp.sum(grad_norm, axis=0, keepdims=True)
    out_ref[...] = (mid_ref[...] + norm_back(grad_norm, hat, scale, gain)).astype(bf16)

    @pl.when(step == pl.num_programs(0) - 1)
    def _():
        dw_ref[...] = total[:, 0:width, :].astype(bf16)
        for which in range(2):
            sums_ref[1 + which : 2 + which, 0:cols] = total[which, width : width + 1, :]


def tail_part(info, mine, theirs, hidden, grad_mid, weights, vectors):
    cols = mine.shape[0]
    rows, width = hidden.shape
    blk = min(512, rows)
    tall = pl.BlockSpec((blk, width), lambda i, n: (i, 0))
    wide = pl.BlockSpec((cols, blk), lambda i, n: (0, i))
    fixed = lambda shape: pl.BlockSpec(shape, lambda i, n: (0,) * len(shape))
    return pl.pallas_call(
        tail_kernel,
        grid_spec=pltpu.PrefetchScalarGridSpec(
            num_scalar_prefetch=1,
            grid=(rows // blk,),
            in_specs=[wide, wide, tall, tall, fixed(weights.shape), fixed(vectors.shape)],
            out_specs=[tall, fixed(weights.shape), fixed((8, 2 * width))],
            scratch_shapes=[pltpu.VMEM((2, width + 16, cols), f32)],
        ),
        out_shape=[
            jax.ShapeDtypeStruct((rows, width), bf16),
            jax.ShapeDtypeStruct(weights.shape, bf16),
            jax.ShapeDtypeStruct((8, 2 * width), f32),
        ],
        cost_estimate=pl.CostEstimate(flops=8 * rows * width * cols, bytes_accessed=16 << 20, transcendentals=rows),
        name="tail",
    )(info, mine, theirs, hidden, grad_mid, weights, vectors)


def swap(values, axis, flip):
    size = lax.axis_size(axis)
    return lax.ppermute(values, axis, [(i, i ^ flip) for i in range(size)])


def place(pieces, index, count):
    shape = pieces[0].shape
    stacked = jnp.zeros((count,) + shape, pieces[0].dtype)
    for k, piece in enumerate(pieces):
        stacked = lax.dynamic_update_slice_in_dim(stacked, piece[None], index ^ k, 0)
    return stacked


def gather_bits(values, axis, shift, count):
    index = (lax.axis_index(axis) >> shift) & (count - 1)
    pieces = [values] + [swap(values, axis, k << shift) for k in range(1, count)]
    return place(pieces, index, count)


def scatter_bits(values, axis, shift, count):
    index = (lax.axis_index(axis) >> shift) & (count - 1)
    pick = lambda k: lax.dynamic_index_in_dim(values, index ^ k, 0, keepdims=False)
    total = pick(0).astype(f32)
    for k in range(1, count):
        total = total + swap(pick(k).astype(bf16), axis, k << shift).astype(f32)
    return total


def gelu_and_slope(u):
    a = 0.7978845608028654
    inner = a * (u + 0.044715 * u * u * u)
    t = jnp.tanh(inner)
    slope = 0.5 * (1 + t) + 0.5 * u * (1 - t * t) * a * (1 + 3 * 0.044715 * u * u)
    return 0.5 * u * (1 + t), slope


def norm_parts(inputs):
    center = inputs - jnp.mean(inputs, axis=-1, keepdims=True)
    scale = lax.rsqrt(jnp.mean(center * center, axis=-1, keepdims=True) + EPS)
    return center * scale, scale


def norm_back(grad, hat, scale, gain):
    e = grad * gain
    return scale * (e - jnp.mean(e, axis=-1, keepdims=True) - hat * jnp.mean(e * hat, axis=-1, keepdims=True))


def on_device(
    hidden_in, seq_lengths, out_cotangent, norm1_gain, norm1_shift, qkv_weight, qv_bias, out_weight, out_bias,
    norm2_gain, norm2_shift, up_weight, up_bias, down_weight, down_bias,
):
    rows, width = hidden_in.shape[1:]
    hidden_in, out_cotangent = hidden_in[0], out_cotangent[0]
    ff = up_weight.shape[1]
    dp, ctx = lax.axis_size("dp"), lax.axis_size("ctx")
    dp_low = 2 if dp == 8 else 4
    dp_high, high_at = dp // dp_low, dp_low.bit_length() - 1
    ring = ctx // 2
    me = lax.axis_index("ctx")
    core = me % 2
    heads = HEADS // 2
    half = heads * HEAD_DIM
    shard = width // dp
    length = seq_lengths[0]

    def by_core(cols):
        lead = cols.shape[:-1]
        cols = cols.reshape(lead + (3, 2, heads, HEAD_DIM))
        asks = cols[..., 0, :, :, :].reshape(lead + (2, half))
        pairs = jnp.moveaxis(cols[..., 1:, :, :, :], -4, -2).reshape(lead + (2, 2 * half))
        return jnp.concatenate([asks, pairs], -1)

    def from_core(cols):
        lead = cols.shape[:-2]
        asks = cols[..., :half].reshape(lead + (1, 2, heads, HEAD_DIM))
        pairs = jnp.moveaxis(cols[..., half:].reshape(lead + (2, heads, 2, HEAD_DIM)), -2, -4)
        return jnp.concatenate([asks, pairs], -4).reshape(lead + (6 * half,))

    small = jnp.concatenate([norm1_gain, norm1_shift, out_bias, norm2_gain, norm2_shift, down_bias, qv_bias[0], qv_bias[1], up_bias])[None]
    small = gather_bits(gather_bits(small, "dp", high_at, dp_high), "dp", 0, dp_low)
    small = small.swapaxes(0, 1).reshape(dp, -1).astype(f32)
    vector = lambda at: small[:, at * shard : (at + 1) * shard].reshape(width)
    gain_one, shift_one, bias_out, gain_two, shift_two, bias_down, bias_q, bias_v = [vector(at) for at in range(8)]
    bias_up = small[:, 8 * shard :].reshape(ff)
    first_rows = jnp.pad(jnp.stack([jnp.concatenate([gain_one, shift_one])]), ((0, 7), (0, 0)))
    second_rows = jnp.pad(jnp.stack([jnp.concatenate([bias_out, gain_two, shift_two, bias_down]), bias_up]), ((0, 6), (0, 0)))

    piece = lax.dynamic_slice_in_dim(qkv_weight, me * (shard // ctx), shard // ctx, 0)
    piece = by_core(piece).swapaxes(0, 1)
    piece = gather_bits(piece, "dp", high_at, dp_high)
    piece = gather_bits(piece, "dp", 0, dp_low)

    others = jnp.concatenate([out_weight, down_weight] + [up_weight[:, j * width : (j + 1) * width] for j in range(ff // width)], 0)
    others, piece = lax.optimization_barrier((others, piece))
    others = lax.all_gather(others, "dp", axis=0, tiled=False)

    piece = gather_bits(piece, "ctx", 1, ring)
    piece = gather_bits(piece, "ctx", 0, 2)
    w_qkv = piece.transpose(4, 3, 2, 1, 0, 5, 6).reshape(2, width, 3 * half)

    hat_one, _ = norm_parts(hidden_in.astype(f32))
    normed_one = (hat_one * gain_one + shift_one).astype(bf16)
    bias_full = by_core(jnp.concatenate([bias_q, jnp.zeros_like(bias_q), bias_v]))
    factors = jnp.where(jnp.arange(3 * half) < half, LOG2E * HEAD_DIM**-0.5, 1.0)

    def projected(which):
        pick = lambda x: lax.dynamic_index_in_dim(x, which, 0, keepdims=False)
        return ((dot(pick(w_qkv), normed_one, 0, 1) + pick(bias_full)[:, None]) * factors[:, None]).astype(bf16)

    theirs = swap(projected(1 - core), "ctx", 1)
    mine = projected(core)

    def counts_of(source):
        first = jnp.clip(length - source * rows, 0, rows)
        second = jnp.clip(length - (source ^ 1) * rows, 0, rows)
        return jnp.stack([first, second, (source % 2) * rows]).astype(jnp.int32)

    groups = [(0, 2), (2, 1), (3, 1)] if ring == 2 else [(0, heads)]
    far = []
    for k in range(1, ring):
        for at, many in groups:
            cut = slice(half + at * 2 * HEAD_DIM, half + (at + many) * 2 * HEAD_DIM)
            far.append((k, at, many, swap(mine[cut], "ctx", 2 * k), swap(theirs[cut], "ctx", 2 * k)))
    *sums, own, probs = attend(counts_of(me), mine, theirs, mine, theirs, heads, 0, heads, None, None, ring == 1)
    near = (own, probs)
    saved, low = [], None
    for k, at, many, key_a, key_b in far:
        last = k == ring - 1
        out = attend(counts_of(me ^ (2 * k)), mine, theirs, key_a, key_b, 0, at, many, sums, low if last else None, last)
        if last:
            low, out = out[0], out[1:]
        sums, own, probs = out[:2], out[2], out[3]
        saved.append((own, probs))
    attended, stat = sums
    low_mine, low_theirs = low[:, :rows], swap(low[:, rows:], "ctx", 1)

    info = jnp.stack([core, jnp.clip(length - me * rows, 0, rows)]).astype(jnp.int32)
    hidden_out, grad_mid, grad_mine, grad_theirs, packed, sums_two = middle_part(
        info, low_mine, low_theirs, hidden_in, out_cotangent, others, second_rows, ff
    )
    grad_theirs = swap(grad_theirs, "ctx", 1)

    packed = lax.psum_scatter(packed, "dp", scatter_dimension=0, tiled=False)

    buffer, returned = None, []
    for (k, at, many, key_a, key_b), (own, probs) in zip(far[::-1], saved[::-1]):
        buffer, dkv = attend_back(
            counts_of(me ^ (2 * k)), mine, theirs, key_a, key_b, 0, at, many, grad_mine, grad_theirs, attended, stat, own, probs,
            (buffer, k < ring - 1), False,
        )
        returned.append((at, k, swap(dkv, "ctx", 2 * k)))
    dq, dkv = attend_back(
        counts_of(me), mine, theirs, mine, theirs, heads, 0, heads, grad_mine, grad_theirs, attended, stat, *near, (buffer, True), True
    )
    for k in range(1, ring):
        dkv = dkv + jnp.concatenate([x for at, which, x in sorted(returned, key=lambda r: r[0]) if which == k], 0).astype(f32)
    grad_p = jnp.concatenate([dq, dkv.astype(bf16).reshape(2 * half, 2 * rows)], 0)
    p_theirs = swap(grad_p[:, rows:], "ctx", 1)

    packed = packed.astype(f32)
    packed = scatter_bits(packed.reshape((2, -1) + packed.shape[1:]), "ctx", 0, 2)
    for flip in [2 << b for b in range(ring.bit_length() - 1)]:
        packed = packed + swap(packed.astype(bf16), "ctx", flip).astype(f32)
    packed = gather_bits(packed.astype(bf16), "ctx", 0, 2).reshape(-1, width).astype(f32)

    grad_hidden, grad_w_qkv, sums_one = tail_part(info, grad_p[:, :rows], p_theirs, hidden_in, grad_mid, w_qkv, first_rows)

    bias_sums = from_core(sums_one[1:3, : 3 * half])
    spread = lambda x: x.reshape(-1, dp, x.shape[-1] // dp).swapaxes(0, 1).reshape(dp, -1)
    smalls = jnp.concatenate(
        [
            spread(sums_one[0].reshape(2, width)),
            spread(sums_two[1].reshape(4, width)),
            spread(bias_sums.reshape(3, width)),
            spread(sums_two[0].reshape(1, ff)),
        ],
        1,
    )
    for flip in [1 << b for b in range(ctx.bit_length() - 1)]:
        smalls = smalls + swap(smalls, "ctx", flip)
    smalls = smalls.reshape(dp_high, dp_low, 1, -1)
    smalls = scatter_bits(smalls.swapaxes(0, 1), "dp", 0, dp_low)
    smalls = scatter_bits(smalls, "dp", high_at, dp_high)[0]

    pieces = grad_w_qkv.reshape(2, dp_high, dp_low, ring, 2, shard // ctx, 3 * half).transpose(4, 3, 2, 1, 0, 5, 6)
    pieces = scatter_bits(pieces, "ctx", 0, 2)
    pieces = scatter_bits(pieces, "ctx", 1, ring)
    pieces = scatter_bits(pieces, "dp", 0, dp_low)
    pieces = scatter_bits(pieces, "dp", high_at, dp_high)
    pieces = gather_bits(gather_bits(pieces.astype(bf16), "ctx", 1, ring), "ctx", 0, 2)
    grad_qkv = from_core(pieces.transpose(1, 0, 3, 2, 4).reshape(shard, 2, 3 * half)).astype(f32)

    grad_down = packed[shard : shard + ff // dp]
    grad_up = packed[shard + ff // dp :].reshape(ff // width, shard, width).swapaxes(0, 1).reshape(shard, ff)
    small_out = lambda at: smalls[at * shard : (at + 1) * shard]
    return (
        hidden_out[None],
        grad_hidden[None],
        small_out(0),
        small_out(1),
        grad_qkv,
        jnp.stack([small_out(6), small_out(8)]),
        packed[:shard],
        small_out(2),
        small_out(3),
        small_out(4),
        grad_up,
        smalls[9 * shard :],
        grad_down,
        small_out(5),
    )


def solution(mesh):
    return jax.shard_map(
        on_device,
        mesh=mesh,
        in_specs=(
            P("dp", "ctx", None), P("dp"), P("dp", "ctx", None), P("dp"), P("dp"), P("dp", None), P(None, "dp"),
            P("dp", None), P("dp"), P("dp"), P("dp"), P("dp", None), P("dp"), P("dp", None), P("dp"),
        ),
        out_specs=(
            P("dp", "ctx", None), P("dp", "ctx", None), P("dp"), P("dp"), P("dp", None), P(None, "dp"), P("dp", None),
            P("dp"), P("dp"), P("dp"), P("dp", None), P("dp"), P("dp", None), P("dp"),
        ),
        check_vma=False,
    )
```

```python
import functools

import jax
import jax.numpy as jnp
from jax import lax
from jax.experimental import pallas as pl
from jax.experimental.pallas import tpu as pltpu
from jax.sharding import PartitionSpec as P

HEADS = 8
HEAD_DIM = 64
EPS = 1e-05
LOG2E = 1.4426950408889634
LN2 = 0.6931471805599453
LOW = -1e30
TOP = 1e30
f32 = jnp.float32
bf16 = jnp.bfloat16


def dot(left, right, left_dim, right_dim):
    return lax.dot_general(left, right, (((left_dim,), (right_dim,)), ((), ())), preferred_element_type=f32)


def split_three(values):
    one = values.astype(bf16)
    rest = values - one.astype(f32)
    two = rest.astype(bf16)
    return one, two, (rest - two.astype(f32)).astype(bf16)


def counts_of(info_ref, hop, rows):
    length, source = info_ref[2], info_ref[3] ^ (2 * hop)
    return jnp.clip(length - source * rows, 0, rows), jnp.clip(length - (source ^ 1) * rows, 0, rows), info_ref[0] * rows


def forward_kernel(info_ref, qa_ref, qb_ref, ka_ref, kb_ref, va_ref, vb_ref, *rest, blk, hop, first, last, aliases):
    prev, rest = ((None, None), rest) if first else (rest[:2], rest[2:])
    rest = rest[aliases:]
    low_refs, rest = (rest[:2], rest[2:]) if last else (None, rest)
    o_ref, stat_ref, own_ref, p_ref, keys, values = rest
    chunk = pl.program_id(1)
    rows = qa_ref.shape[1]
    span = keys.shape[0]
    *valid, start = counts_of(info_ref, hop, rows)
    alive = valid[0] + valid[1] > 0

    def finish(out, sums, top):
        own_ref[0] = jnp.broadcast_to(top, (8, rows))
        if not first:
            old_sums, old_top = prev[1][0, 0:1], prev[1][0, 1:2]
            new_top = jnp.maximum(top, old_top)
            scale, old_scale = jnp.exp2(top - new_top), jnp.exp2(old_top - new_top)
            out = out * scale + prev[0][...] * old_scale
            sums = sums * scale + old_sums * old_scale
            top = new_top
        stat_ref[0] = jnp.concatenate([sums, top, jnp.zeros((6, rows), f32)], 0)
        if last:
            out = out / sums
            for which, low_ref in enumerate(low_refs):

                @pl.when(chunk == which)
                def _():
                    low_ref[...] = out.astype(bf16)

        o_ref[...] = out

    @pl.when(jnp.logical_and(alive, chunk == 0))
    def _():
        pos = lax.broadcasted_iota(jnp.int32, (HEAD_DIM, rows), 1)
        row = lax.broadcasted_iota(jnp.int32, (HEAD_DIM, rows), 0)
        for part, (k_ref, v_ref) in enumerate(((ka_ref, va_ref), (kb_ref, vb_ref))):
            mask = jnp.where(pos < valid[part], 0.0, LOW)
            extra = jnp.where(row < 3, 1.0, jnp.where(row == 3, mask, 0.0)).astype(bf16)
            keys[pl.ds(part * rows, rows), :] = jnp.concatenate([k_ref[...], extra], 0).T
            values[:, pl.ds(part * rows, rows)] = v_ref[...]

    @pl.when(jnp.logical_not(alive))
    def _():
        finish(jnp.zeros((HEAD_DIM, rows), f32), jnp.zeros((1, rows), f32), jnp.full((1, rows), LOW, f32))

    @pl.when(alive)
    def _():
        query = jnp.where(chunk == 0, qa_ref[...], qb_ref[...])
        row = lax.broadcasted_iota(jnp.int32, (HEAD_DIM, rows), 0)
        head_blk = 64

        def extend(top):
            one, two, three = [jnp.broadcast_to(-x.astype(f32), (HEAD_DIM, rows)) for x in split_three(top)]
            extra = jnp.where(row == 0, one, jnp.where(row == 1, two, jnp.where(row == 2, three, jnp.where(row == 3, 1.0, 0.0))))
            return jnp.concatenate([query, extra.astype(bf16)], 0)

        plain = extend(jnp.zeros((1, rows), f32))
        guess = jnp.max(dot(keys[pl.ds(pl.multiple_of(start, head_blk), head_blk), :], plain, 1, 0), axis=0, keepdims=True)

        def run(top, unroll):
            query_ext = extend(top)

            def body(step, carry):
                total, sums = carry
                off = step * blk if isinstance(step, int) else pl.multiple_of(step * blk, blk)
                wide = jnp.exp2(dot(keys[pl.ds(off, blk), :], query_ext, 1, 0))
                probs = wide.astype(bf16)
                p_ref[0, 0, pl.ds(off, blk), :] = probs
                sums = sums + jnp.sum(wide.reshape(blk // 8, 8, rows), axis=0)
                return total + dot(values[:, pl.ds(off, blk)], probs, 1, 0), sums

            carry = jnp.zeros((HEAD_DIM, rows), f32), jnp.zeros((8, rows), f32)
            if unroll:
                for step in range(span // blk):
                    carry = body(step, carry)
            else:
                carry = lax.fori_loop(0, span // blk, body, carry)
            sums = jnp.sum(carry[1], axis=0, keepdims=True)
            finish(carry[0], sums, top)
            return jnp.max(sums)

        largest = run(guess, True)

        @pl.when(jnp.logical_not(largest < TOP))
        def _():
            def wider(step, top):
                off = pl.multiple_of(step * head_blk, head_blk)
                return jnp.maximum(top, jnp.max(dot(keys[pl.ds(off, head_blk), :], plain, 1, 0), axis=0, keepdims=True))

            run(lax.fori_loop(0, span // head_blk, wider, jnp.full((1, rows), LOW, f32)), False)


def head_rows(base, step, rows):
    return pl.BlockSpec((HEAD_DIM, rows), lambda h, i, n: (base + step * h, 0))


def attend(info, hop, query_a, query_b, key_a, key_b, kv_base, first_head, heads, prev, low, last):
    rows = query_a.shape[1]
    span = 2 * rows
    blk = min(512, rows)
    keys, vals, ask = head_rows(kv_base, 2, rows), head_rows(kv_base + 1, 2, rows), head_rows(first_head, 1, rows)
    out_spec = pl.BlockSpec((HEAD_DIM, rows), lambda h, i, n: (first_head + h, i))
    stat_spec = pl.BlockSpec((1, 8, rows), lambda h, i, n: (first_head + h, 0, i))
    all_heads = HEADS // 2
    extra_in = [out_spec, stat_spec] if prev else []
    extra_args = list(prev) if prev else []
    if low is not None:
        extra_in, extra_args = extra_in + [pl.BlockSpec(memory_space=pl.ANY)] * 2, extra_args + list(low)
    out_specs = [out_spec, stat_spec, pl.BlockSpec((1, 8, rows), lambda h, i, n: (h, 0, i)), pl.BlockSpec((1, 1, span, rows), lambda h, i, n: (h, i, 0, 0))]
    out_shape = [
        jax.ShapeDtypeStruct((all_heads * HEAD_DIM, span), f32),
        jax.ShapeDtypeStruct((all_heads, 8, span), f32),
        jax.ShapeDtypeStruct((heads, 8, span), f32),
        jax.ShapeDtypeStruct((heads, 2, span, rows), bf16),
    ]
    shift = 2 if last else 0
    if last:
        out_specs = [head_rows(first_head, 1, rows)] * 2 + out_specs
        out_shape = [jax.ShapeDtypeStruct((all_heads * HEAD_DIM, rows), bf16)] * 2 + out_shape
    alias = {7: shift, 8: shift + 1} if prev else {}
    if low is not None:
        alias = {**alias, 9: 0, 10: 1}
    return pl.pallas_call(
        functools.partial(forward_kernel, blk=blk, hop=hop, first=not prev, last=last, aliases=0 if low is None else 2),
        grid_spec=pltpu.PrefetchScalarGridSpec(
            num_scalar_prefetch=1,
            grid=(heads, 2),
            in_specs=[ask, ask, keys, keys, vals, vals] + extra_in,
            out_specs=out_specs,
            scratch_shapes=[pltpu.VMEM((span, 2 * HEAD_DIM), bf16), pltpu.VMEM((HEAD_DIM, span), bf16)],
        ),
        out_shape=out_shape,
        input_output_aliases=alias,
        cost_estimate=pl.CostEstimate(
            flops=16 * heads * span * span * HEAD_DIM, bytes_accessed=2 * heads * span * span, transcendentals=heads * span * span
        ),
        name="attend",
    )(info, query_a, query_b, key_a, key_b, key_a, key_b, *extra_args)


def backward_kernel(
    info_ref, qa_ref, qb_ref, ka_ref, kb_ref, va_ref, vb_ref, ga_ref, gb_ref, o_ref, stat_ref, own_ref, p_ref,
    *rest, blk, hop, adds, aliases, last,
):
    before_ref, rest = (rest[0], rest[1:]) if adds else (None, rest)
    rest = rest[aliases:]
    dq_refs, (*dkv_refs, values, dk_sum, dv_sum) = (rest[:2], rest[2:]) if last else (rest[:1], rest[1:])
    chunk = pl.program_id(1)
    rows = qa_ref.shape[1]
    span = values.shape[0]
    valid_a, valid_b, _ = counts_of(info_ref, hop, rows)
    alive = valid_a + valid_b > 0
    row = lax.broadcasted_iota(jnp.int32, (HEAD_DIM, rows), 0)

    def finish(dq):
        if adds:
            dq = dq + before_ref[...]
        if not last:
            dq_refs[0][...] = dq
            return
        for which, dq_ref in enumerate(dq_refs):

            @pl.when(chunk == which)
            def _():
                dq_ref[...] = (dq * HEAD_DIM**-0.5).astype(bf16)

    @pl.when(chunk == 0)
    def _():
        extra = jnp.where(row < 3, 1.0, 0.0).astype(bf16)
        for part, v_ref in enumerate((va_ref, vb_ref)):
            values[pl.ds(part * rows, rows), :] = jnp.concatenate([v_ref[...], extra], 0).T
        dk_sum[...] = jnp.zeros_like(dk_sum)
        dv_sum[...] = jnp.zeros_like(dv_sum)

    @pl.when(jnp.logical_not(alive))
    def _():
        finish(jnp.zeros((HEAD_DIM, rows), f32))

    @pl.when(alive)
    def _():
        query = jnp.where(chunk == 0, qa_ref[...], qb_ref[...])
        grad = jnp.where(chunk == 0, ga_ref[...], gb_ref[...])
        factor = jnp.exp2(own_ref[0, 0:1] - stat_ref[0, 1:2]) / stat_ref[0, 0:1]
        grad = (grad.astype(f32) * factor).astype(bf16)
        delta = jnp.sum(grad.astype(f32) * o_ref[...], axis=0, keepdims=True)
        one, two, three = [jnp.broadcast_to(-x.astype(f32), (HEAD_DIM, rows)) for x in split_three(delta)]
        extra = jnp.where(row == 0, one, jnp.where(row == 1, two, jnp.where(row == 2, three, 0.0))).astype(bf16)
        grad_ext = jnp.concatenate([grad, extra], 0)
        dq = jnp.zeros((HEAD_DIM, rows), f32)
        for step in range(span // blk):
            off = step * blk
            probs = p_ref[0, 0, pl.ds(off, blk), :]
            grad_scores = (probs.astype(f32) * dot(values[pl.ds(off, blk), :], grad_ext, 1, 0)).astype(bf16)
            k_ref = (ka_ref, kb_ref)[off // rows]
            dq = dq + dot(k_ref[:, pl.ds(off % rows, blk)], grad_scores, 1, 0)
            dv_sum[:, pl.ds(off, blk)] += dot(grad, probs, 1, 1)
            dk_sum[:, pl.ds(off, blk)] += dot(query, grad_scores, 1, 1)
        finish(dq)

    @pl.when(chunk == pl.num_programs(1) - 1)
    def _():
        for which, dkv_ref in enumerate(dkv_refs):
            dkv_ref[0:HEAD_DIM] = (dk_sum[:, which * rows : (which + 1) * rows] * LN2).astype(bf16)
            dkv_ref[HEAD_DIM:] = dv_sum[:, which * rows : (which + 1) * rows].astype(bf16)


def attend_back(info, hop, query_a, query_b, key_a, key_b, kv_base, first_head, heads, grad_a, grad_b, attended, stat, own, probs, before, last):
    rows = query_a.shape[1]
    span = 2 * rows
    blk = min(512, rows)
    keys, vals, ask = head_rows(kv_base, 2, rows), head_rows(kv_base + 1, 2, rows), head_rows(first_head, 1, rows)
    part = pl.BlockSpec((HEAD_DIM, rows), lambda h, i, n: (first_head + h, i))
    buffer, adds = before
    alias, extra_in, extra_args = {}, [], []
    if adds:
        extra_in, extra_args = [part], [buffer]
        alias = {} if last else {13: 0}
    elif buffer is not None:
        extra_in, extra_args, alias = [pl.BlockSpec(memory_space=pl.ANY)], [buffer], {13: 0}
    return pl.pallas_call(
        functools.partial(backward_kernel, blk=blk, adds=adds, hop=hop, aliases=len(extra_in) - int(adds), last=last),
        grid_spec=pltpu.PrefetchScalarGridSpec(
            num_scalar_prefetch=1,
            grid=(heads, 2),
            in_specs=[
                ask, ask, keys, keys, vals, vals, ask, ask,
                part,
                pl.BlockSpec((1, 8, rows), lambda h, i, n: (first_head + h, 0, i)),
                pl.BlockSpec((1, 8, rows), lambda h, i, n: (h, 0, i)),
                pl.BlockSpec((1, 1, span, rows), lambda h, i, n: (h, i, 0, 0)),
            ] + extra_in,
            out_specs=([head_rows(first_head, 1, rows)] * 2 if last else [part]) + [pl.BlockSpec((2 * HEAD_DIM, rows), lambda h, i, n: (h, 0))] * 2,
            scratch_shapes=[
                pltpu.VMEM((span, 2 * HEAD_DIM), bf16),
                pltpu.VMEM((HEAD_DIM, span), f32),
                pltpu.VMEM((HEAD_DIM, span), f32),
            ],
        ),
        out_shape=[
            *([jax.ShapeDtypeStruct((HEADS // 2 * HEAD_DIM, rows), bf16)] * 2 if last else [jax.ShapeDtypeStruct((HEADS // 2 * HEAD_DIM, span), f32)]),
            *[jax.ShapeDtypeStruct((heads * 2 * HEAD_DIM, rows), bf16)] * 2,
        ],
        input_output_aliases=alias,
        cost_estimate=pl.CostEstimate(
            flops=32 * heads * span * span * HEAD_DIM, bytes_accessed=2 * heads * span * span, transcendentals=0
        ),
        name="attend_back",
    )(info, query_a, query_b, key_a, key_b, key_a, key_b, grad_a, grad_b, attended, stat, own, probs, *extra_args)


def middle_kernel(
    info_ref, mine_ref, theirs_ref, hidden_ref, cot_ref, w_ref, vec_ref,
    out_ref, grad_mid_ref, grad_mine_ref, grad_theirs_ref, packed_ref, sums_ref,
    total, act_s, slope_s, *, ff,
):
    step = pl.program_id(0)
    rows, width = hidden_ref.shape
    dp = w_ref.shape[0]
    shard = width // dp
    down_at, up_at = shard, shard + ff // dp
    own, other = info_ref[0], 1 - info_ref[0]
    halves = lambda which: (pl.ds(which * (dp // 2), dp // 2), pl.ds(0, shard), slice(None))
    down_rows = lambda j: (pl.ds(j * dp * width // ff, dp * width // ff), pl.ds(down_at, ff // dp), slice(None))
    up_rows = lambda j: (slice(None), pl.ds(up_at + j * shard, shard), slice(None))
    half = mine_ref.shape[0]
    blocks = ff // width

    @pl.when(step == 0)
    def _():
        total[...] = jnp.zeros_like(total)
        sums_ref[...] = jnp.zeros_like(sums_ref)

    w_mine = w_ref[halves(own)].reshape(half, width)
    w_theirs = w_ref[halves(other)].reshape(half, width)
    middle = hidden_ref[...].astype(f32) + dot(mine_ref[...], w_mine, 0, 0) + dot(theirs_ref[...], w_theirs, 0, 0) + vec_ref[0:1, 0:width]
    gain, shift, bias_down = [vec_ref[0:1, k * width : (k + 1) * width] for k in (1, 2, 3)]
    hat, scale = norm_parts(middle)
    normed = (hat * gain + shift).astype(bf16)
    out = middle + bias_down
    for j in range(blocks):
        cols = slice(j * width, (j + 1) * width)
        activated, slope = gelu_and_slope(dot(normed, w_ref[up_rows(j)].reshape(width, width), 1, 0) + vec_ref[1:2, cols])
        activated = activated.astype(bf16)
        act_s[:, cols] = activated
        slope_s[:, cols] = slope
        out = out + dot(activated, w_ref[down_rows(j)].reshape(width, width), 1, 0)
    out_ref[...] = out.astype(bf16)

    pos = step * rows + lax.broadcasted_iota(jnp.int32, (rows, width), 0)
    grad_z = jnp.where(pos < info_ref[1], cot_ref[...], jnp.zeros_like(cot_ref))
    grad_norm = jnp.zeros((rows, width), f32)
    for j in range(blocks):
        cols = slice(j * width, (j + 1) * width)
        grad_act = dot(grad_z, w_ref[down_rows(j)].reshape(width, width), 1, 1) * slope_s[:, cols]
        sums_ref[0:1, cols] += jnp.sum(grad_act, axis=0, keepdims=True)
        grad_pre = grad_act.astype(bf16)
        total[down_rows(j)] += dot(act_s[:, cols], grad_z, 0, 0).reshape(dp * width // ff, ff // dp, width)
        total[up_rows(j)] += dot(normed, grad_pre, 0, 0).reshape(dp, shard, width)
        grad_norm = grad_norm + dot(grad_pre, w_ref[up_rows(j)].reshape(width, width), 1, 1)
    grad_out = grad_z.astype(f32)
    grad_mid = grad_out + norm_back(grad_norm, hat, scale, gain)
    grad_mid_ref[...] = grad_mid
    branch = grad_mid.astype(bf16)
    for k, value in enumerate((branch.astype(f32), grad_norm * hat, grad_norm, grad_out)):
        sums_ref[1:2, k * width : (k + 1) * width] += jnp.sum(value, axis=0, keepdims=True)
    grad_mine_ref[...] = dot(w_mine, branch, 1, 1).astype(bf16)
    grad_theirs_ref[...] = dot(w_theirs, branch, 1, 1).astype(bf16)
    total[halves(own)] += dot(mine_ref[...], branch, 1, 0).reshape(dp // 2, shard, width)
    total[halves(other)] += dot(theirs_ref[...], branch, 1, 0).reshape(dp // 2, shard, width)

    @pl.when(step == pl.num_programs(0) - 1)
    def _():
        packed_ref[:, 0 : total.shape[1]] = total[...].astype(bf16)


def middle_part(info, mine, theirs, hidden, cot, weights, vectors, ff):
    half = mine.shape[0]
    rows, width = hidden.shape
    blk = min(512, rows)
    packed = weights.shape
    tall = pl.BlockSpec((blk, width), lambda i, n: (i, 0))
    wide = pl.BlockSpec((half, blk), lambda i, n: (0, i))
    fixed = lambda shape: pl.BlockSpec(shape, lambda i, n: (0,) * len(shape))
    return pl.pallas_call(
        functools.partial(middle_kernel, ff=ff),
        grid_spec=pltpu.PrefetchScalarGridSpec(
            num_scalar_prefetch=1,
            grid=(rows // blk,),
            in_specs=[wide, wide, tall, tall, fixed(packed), fixed(vectors.shape)],
            out_specs=[tall, tall, wide, wide, fixed(packed), fixed((8, ff))],
            scratch_shapes=[pltpu.VMEM((packed[0], packed[1] - 16, width), f32), pltpu.VMEM((blk, ff), bf16), pltpu.VMEM((blk, ff), f32)],
        ),
        out_shape=[
            jax.ShapeDtypeStruct((rows, width), bf16),
            jax.ShapeDtypeStruct((rows, width), f32),
            jax.ShapeDtypeStruct((half, rows), bf16),
            jax.ShapeDtypeStruct((half, rows), bf16),
            jax.ShapeDtypeStruct(packed, bf16),
            jax.ShapeDtypeStruct((8, ff), f32),
        ],
        cost_estimate=pl.CostEstimate(flops=12 * rows * width * (2 * ff + width) // 2, bytes_accessed=16 << 20, transcendentals=rows * ff),
        name="middle",
    )(info, mine, theirs, hidden, cot, weights, vectors)


def pack_kernel(out_ref, down_ref, up_ref, row_ref, packed_ref):
    shard, width = out_ref.shape
    at = shard + down_ref.shape[0]
    packed_ref[0:shard] = out_ref[...]
    packed_ref[shard:at] = down_ref[...]
    for j in range(up_ref.shape[1] // width):
        packed_ref[at + j * shard : at + (j + 1) * shard] = up_ref[:, j * width : (j + 1) * width]
    end = at + up_ref.shape[1] // width * shard
    packed_ref[end:] = jnp.broadcast_to(row_ref[...], (packed_ref.shape[0] - end, width))


def pack_part(out_weight, down_weight, up_weight, row):
    shard, width = out_weight.shape
    total = shard + down_weight.shape[0] + up_weight.shape[1] // width * shard + 16
    return pl.pallas_call(pack_kernel, out_shape=jax.ShapeDtypeStruct((total, width), bf16), name="pack")(out_weight, down_weight, up_weight, row)


def place_kernel(info_ref, mine_ref, theirs_ref, out_ref):
    for k in range(mine_ref.shape[0]):
        at = info_ref[4] ^ k
        out_ref[:, pl.ds(at, 1), pl.ds(info_ref[0], 1)] = mine_ref[k][:, None, None]
        out_ref[:, pl.ds(at, 1), pl.ds(1 - info_ref[0], 1)] = theirs_ref[k][:, None, None]


def place_part(info, mine, theirs):
    count, _, rows, cols = mine.shape
    full = pl.BlockSpec(memory_space=pltpu.VMEM)
    return pl.pallas_call(
        place_kernel,
        in_specs=[pl.BlockSpec(memory_space=pltpu.SMEM), full, full],
        out_specs=full,
        out_shape=jax.ShapeDtypeStruct((2, count, 2, rows, cols), bf16),
        name="place",
    )(info, mine, theirs)


def project_grad_kernel(*refs, groups, transposed):
    left_ref, dq_ref, dkv_ref = refs[:3]
    far, (dw_ref, sum_ref, grads_ref, *left_out, total) = refs[3 : 3 + len(groups)], refs[3 + len(groups) :]
    step = pl.program_id(0)
    width = dw_ref.shape[0]
    half = dq_ref.shape[0]

    @pl.when(step == 0)
    def _():
        total[...] = jnp.zeros_like(total)

    if transposed:
        left = left_ref[...]
    else:
        rows = left_ref.shape[0]
        ones = jnp.where(lax.broadcasted_iota(jnp.int32, (16, rows), 0) == 0, 1.0, 0.0).astype(bf16)
        left = jnp.concatenate([left_ref[...].T, ones], 0)
        left_out[0][...] = left
    grads_ref[0:half] = dq_ref[...]
    for (at, many), far_ref in zip(groups, far):
        cut = slice(at * 2 * HEAD_DIM, (at + many) * 2 * HEAD_DIM)
        where = slice(half + cut.start, half + cut.stop)
        grads_ref[where] = (dkv_ref[cut].astype(f32) + far_ref[...].astype(f32)).astype(bf16)
    total[...] += dot(left, grads_ref[...], 1, 1)

    @pl.when(step == pl.num_programs(0) - 1)
    def _():
        dw_ref[...] = total[0:width].astype(bf16)
        sum_ref[...] = jnp.broadcast_to(total[width : width + 1], sum_ref.shape)


def project_grad(left, dq, dkv, groups, far, transposed):
    half, rows = dq.shape
    cols = 3 * half
    width = 2 * half
    blk = min(512, rows)
    wide = lambda n: pl.BlockSpec((n, blk), lambda i: (0, i))
    fixed = lambda shape: pl.BlockSpec(shape, lambda i: (0,) * len(shape))
    tall = pl.BlockSpec((blk, width), lambda i: (i, 0))
    out_specs = [fixed((width, cols)), fixed((8, cols)), wide(cols)]
    out_shape = [
        jax.ShapeDtypeStruct((width, cols), bf16),
        jax.ShapeDtypeStruct((8, cols), f32),
        jax.ShapeDtypeStruct((cols, rows), bf16),
    ]
    if not transposed:
        out_specs, out_shape = out_specs + [wide(width + 16)], out_shape + [jax.ShapeDtypeStruct((width + 16, rows), bf16)]
    return pl.pallas_call(
        functools.partial(project_grad_kernel, groups=groups, transposed=transposed),
        grid=(rows // blk,),
        in_specs=[wide(width + 16) if transposed else tall, wide(half), wide(2 * half)] + [wide(many * 2 * HEAD_DIM) for _, many in groups],
        out_specs=out_specs,
        out_shape=out_shape,
        scratch_shapes=[pltpu.VMEM((width + 16, cols), f32)],
        cost_estimate=pl.CostEstimate(flops=2 * rows * width * cols, bytes_accessed=6 << 20, transcendentals=0),
        name="project_grad",
    )(left, dq, dkv, *far)


def tail_kernel(info_ref, mine_ref, theirs_ref, hidden_ref, mid_ref, w_ref, vec_ref, out_ref, sums_ref):
    step = pl.program_id(0)
    width = hidden_ref.shape[1]
    cols = mine_ref.shape[0]

    @pl.when(step == 0)
    def _():
        sums_ref[...] = jnp.zeros_like(sums_ref)

    hat, scale = norm_parts(hidden_ref[...].astype(f32))
    grad_norm = dot(w_ref[pl.ds(info_ref[0], 1)].reshape(width, cols), mine_ref[...], 1, 0)
    grad_norm = (grad_norm + dot(w_ref[pl.ds(1 - info_ref[0], 1)].reshape(width, cols), theirs_ref[...], 1, 0)).T
    sums_ref[0:1] += jnp.sum(grad_norm * hat, axis=0, keepdims=True)
    sums_ref[1:2] += jnp.sum(grad_norm, axis=0, keepdims=True)
    out_ref[...] = (mid_ref[...] + norm_back(grad_norm, hat, scale, vec_ref[0:1])).astype(bf16)


def tail_part(info, mine, theirs, hidden, grad_mid, weights, vectors):
    cols = mine.shape[0]
    rows, width = hidden.shape
    blk = min(512, rows)
    tall = pl.BlockSpec((blk, width), lambda i, n: (i, 0))
    wide = pl.BlockSpec((cols, blk), lambda i, n: (0, i))
    fixed = lambda shape: pl.BlockSpec(shape, lambda i, n: (0,) * len(shape))
    return pl.pallas_call(
        tail_kernel,
        grid_spec=pltpu.PrefetchScalarGridSpec(
            num_scalar_prefetch=1,
            grid=(rows // blk,),
            in_specs=[wide, wide, tall, tall, fixed(weights.shape), fixed(vectors.shape)],
            out_specs=[tall, fixed((8, width))],
        ),
        out_shape=[jax.ShapeDtypeStruct((rows, width), bf16), jax.ShapeDtypeStruct((8, width), f32)],
        cost_estimate=pl.CostEstimate(flops=4 * rows * width * cols, bytes_accessed=8 << 20, transcendentals=rows),
        name="tail",
    )(info, mine, theirs, hidden, grad_mid, weights, vectors)


def swap(values, axis, flip):
    size = lax.axis_size(axis)
    return lax.ppermute(values, axis, [(i, i ^ flip) for i in range(size)])


def place(pieces, index, count):
    shape = pieces[0].shape
    stacked = jnp.zeros((count,) + shape, pieces[0].dtype)
    for k, piece in enumerate(pieces):
        stacked = lax.dynamic_update_slice_in_dim(stacked, piece[None], index ^ k, 0)
    return stacked


def gather_bits(values, axis, shift, count):
    index = (lax.axis_index(axis) >> shift) & (count - 1)
    pieces = [values] + [swap(values, axis, k << shift) for k in range(1, count)]
    return place(pieces, index, count)


def scatter_bits(values, axis, shift, count):
    index = (lax.axis_index(axis) >> shift) & (count - 1)
    pick = lambda k: lax.dynamic_index_in_dim(values, index ^ k, 0, keepdims=False)
    total = pick(0).astype(f32)
    for k in range(1, count):
        total = total + swap(pick(k).astype(bf16), axis, k << shift).astype(f32)
    return total


def gelu_and_slope(u):
    a = 0.7978845608028654
    inner = a * (u + 0.044715 * u * u * u)
    t = jnp.tanh(inner)
    slope = 0.5 * (1 + t) + 0.5 * u * (1 - t * t) * a * (1 + 3 * 0.044715 * u * u)
    return 0.5 * u * (1 + t), slope


def norm_parts(inputs):
    center = inputs - jnp.mean(inputs, axis=-1, keepdims=True)
    scale = lax.rsqrt(jnp.mean(center * center, axis=-1, keepdims=True) + EPS)
    return center * scale, scale


def norm_back(grad, hat, scale, gain):
    e = grad * gain
    return scale * (e - jnp.mean(e, axis=-1, keepdims=True) - hat * jnp.mean(e * hat, axis=-1, keepdims=True))


def tie(*values):
    return lax.optimization_barrier(values)


def on_device(
    hidden_in, seq_lengths, out_cotangent, norm1_gain, norm1_shift, qkv_weight, qv_bias, out_weight, out_bias,
    norm2_gain, norm2_shift, up_weight, up_bias, down_weight, down_bias,
):
    rows, width = hidden_in.shape[1:]
    hidden_in, out_cotangent = hidden_in[0], out_cotangent[0]
    ff = up_weight.shape[1]
    dp, ctx = lax.axis_size("dp"), lax.axis_size("ctx")
    dp_low = 2 if dp == 8 else 4
    dp_high, high_at = dp // dp_low, dp_low.bit_length() - 1
    ring = ctx // 2
    me = lax.axis_index("ctx")
    core = me % 2
    heads = HEADS // 2
    half = heads * HEAD_DIM
    shard = width // dp
    length = seq_lengths[0]
    info = jnp.stack([core, jnp.clip(length - me * rows, 0, rows), length, me, lax.axis_index("dp")]).astype(jnp.int32)

    def by_core(cols):
        lead = cols.shape[:-1]
        cols = cols.reshape(lead + (3, 2, heads, HEAD_DIM))
        asks = cols[..., 0, :, :, :].reshape(lead + (2, half))
        pairs = jnp.moveaxis(cols[..., 1:, :, :, :], -4, -2).reshape(lead + (2, 2 * half))
        return jnp.concatenate([asks, pairs], -1)

    def from_core(cols):
        lead = cols.shape[:-2]
        asks = cols[..., :half].reshape(lead + (1, 2, heads, HEAD_DIM))
        pairs = jnp.moveaxis(cols[..., half:].reshape(lead + (2, heads, 2, HEAD_DIM)), -2, -4)
        return jnp.concatenate([asks, pairs], -4).reshape(lead + (6 * half,))

    def gather_pieces(piece):
        highs = [piece] + [swap(piece, "dp", k << high_at) for k in range(1, dp_high)]
        lows = {(k, j): swap(highs[k], "dp", j) for k in range(dp_high) for j in range(1, dp_low)}
        return [highs[k] if j == 0 else lows[k, j] for k in range(dp_high) for j in range(dp_low)]

    piece = lax.dynamic_slice_in_dim(qkv_weight, core * (shard // 2), shard // 2, 0)
    piece = by_core(piece).swapaxes(0, 1)
    early = jnp.concatenate([norm1_gain, norm1_shift, qv_bias[0], qv_bias[1]])[None]
    pieces = jnp.stack(gather_pieces(piece))
    early = gather_bits(gather_bits(early, "dp", high_at, dp_high), "dp", 0, dp_low)
    early = early.swapaxes(0, 1).reshape(dp, 4, shard).swapaxes(0, 1).reshape(4, width).astype(f32)
    gain_one, shift_one, bias_q, bias_v = early

    late = jnp.concatenate([out_bias, norm2_gain, norm2_shift, down_bias, up_bias])
    late = jnp.pad(late, (0, width - late.shape[0]))[None]
    others = pack_part(out_weight, down_weight, up_weight, late)
    others, pieces = tie(others, pieces)
    others = lax.all_gather(others, "dp", axis=0, tiled=False)
    w_qkv = place_part(info, pieces, swap(pieces, "ctx", 1)).reshape(2, width, 3 * half)

    hat_one, _ = norm_parts(hidden_in.astype(f32))
    normed_one = (hat_one * gain_one + shift_one).astype(bf16)
    bias_full = by_core(jnp.concatenate([bias_q, jnp.zeros_like(bias_q), bias_v]))
    factors = jnp.where(jnp.arange(3 * half) < half, LOG2E * HEAD_DIM**-0.5, 1.0)

    def projected(which):
        pick = lambda x: lax.dynamic_index_in_dim(x, which, 0, keepdims=False)
        return ((dot(pick(w_qkv), normed_one, 0, 1) + pick(bias_full)[:, None]) * factors[:, None]).astype(bf16)

    foreign = projected(1 - core)
    mine = projected(core)
    theirs = swap(foreign, "ctx", 1)

    groups = [(0, 2), (2, 2)] if ring == 2 else [(0, heads)]
    far = []
    for k in range(1, ring):
        for at, many in groups:
            cut = slice(half + at * 2 * HEAD_DIM, half + (at + many) * 2 * HEAD_DIM)
            far.append((k, at, many, swap(mine[cut], "ctx", 2 * k), swap(foreign[cut], "ctx", 2 * k + 1)))
    *sums, own, probs = attend(info, 0, mine, theirs, mine, theirs, heads, 0, heads, None, None, ring == 1)
    near = (own, probs)
    saved, low = [], None
    for k, at, many, key_a, key_b in far:
        last = k == ring - 1
        out = attend(info, k, mine, theirs, key_a, key_b, 0, at, many, sums, low if last else None, last)
        if last:
            low, out = out[:2], out[2:]
        sums, own, probs = out[:2], out[2], out[3]
        saved.append((own, probs))
    attended, stat = sums
    low_theirs = swap(low[1], "ctx", 1)

    rest = others[:, -16].astype(f32)
    vector = lambda at: rest[:, at * shard : (at + 1) * shard].reshape(width)
    second_rows = jnp.pad(
        jnp.stack([jnp.concatenate([vector(0), vector(1), vector(2), vector(3)]), rest[:, 4 * shard : 4 * shard + ff // dp].reshape(ff)]), ((0, 6), (0, 0))
    )
    hidden_out, grad_mid, grad_mine, grad_theirs, packed, sums_two = middle_part(
        info, low[0], low_theirs, hidden_in, out_cotangent, others, second_rows, ff
    )
    grad_theirs = swap(grad_theirs, "ctx", 1)

    spread = lambda x: x.reshape(-1, dp, x.shape[-1] // dp).swapaxes(0, 1).reshape(dp, -1)
    late = jnp.concatenate([spread(sums_two[1].reshape(4, width)), spread(sums_two[0].reshape(1, ff))], 1)
    late = jnp.pad(late, ((0, 0), (0, width - late.shape[1])))[:, None].astype(bf16)
    packed = lax.dynamic_update_slice(packed, jnp.broadcast_to(late, (dp, 16, width)), (0, packed.shape[1] - 16, 0))
    packed = lax.psum_scatter(packed, "dp", scatter_dimension=0, tiled=False)

    buffer, back_mine, back_theirs = None, {}, {}
    for (k, at, many, key_a, key_b), (own, probs) in zip(far[::-1], saved[::-1]):
        buffer, dkv_mine, dkv_theirs = attend_back(
            info, k, mine, theirs, key_a, key_b, 0, at, many, grad_mine, grad_theirs, attended, stat, own, probs, (buffer, k < ring - 1), False
        )
        back_mine.setdefault(at, []).append(swap(dkv_mine, "ctx", 2 * k))
        back_theirs.setdefault(at, []).append(swap(dkv_theirs, "ctx", 2 * k + 1))
    dq_mine, dq_out, dkv_mine, dkv_out = attend_back(
        info, 0, mine, theirs, mine, theirs, heads, 0, heads, grad_mine, grad_theirs, attended, stat, *near, (buffer, True), True
    )
    dq_theirs, dkv_theirs = swap(dq_out, "ctx", 1), swap(dkv_out, "ctx", 1)
    sum_far = lambda parts: [functools.reduce(lambda a, b: (a.astype(f32) + b.astype(f32)).astype(bf16), parts[at]) for at, _ in groups]

    dw_out, bias_mine, grads_mine, left = project_grad(normed_one, dq_mine, dkv_mine, groups, sum_far(back_mine), False)
    dw_in = swap(dw_out, "ctx", 1)
    dw, bias_theirs, grads_theirs = project_grad(left, dq_theirs, dkv_theirs, groups, sum_far(back_theirs), True)
    gains = jnp.broadcast_to(gain_one[None], (8, width))
    grad_hidden, sums_one = tail_part(info, grads_mine, grads_theirs, hidden_in, grad_mid, w_qkv, gains)

    packed = packed.astype(f32)
    packed = packed.reshape((2, -1) + packed.shape[1:])
    packed = scatter_bits(packed, "ctx", 0, 2)

    dw = dw.astype(f32) + dw_in.astype(f32)
    dw = scatter_bits(dw.reshape(dp_high, dp_low, ring, shard // ring, 3 * half).transpose(2, 1, 0, 3, 4), "ctx", 1, ring)

    bias_one = jnp.where(core == 0, bias_mine[0], bias_theirs[0])
    bias_two = jnp.where(core == 0, bias_theirs[0], bias_mine[0])
    bias_sums = from_core(jnp.stack([bias_one, bias_two])).reshape(3, width)
    smalls = jnp.concatenate([spread(sums_one[0:2]), spread(bias_sums[0:1]), spread(bias_sums[2:3])], 1)
    smalls = smalls + swap(smalls, "ctx", 1)

    dw, packed, smalls = tie(dw, packed, smalls)
    for flip in [2 << b for b in range(ring.bit_length() - 1)]:
        smalls = smalls + swap(smalls, "ctx", flip)
        packed = packed + swap(packed.astype(bf16), "ctx", flip).astype(f32)
    dw = scatter_bits(dw, "dp", 0, dp_low)
    dw, packed, smalls = tie(dw, packed, smalls)
    packed = gather_bits(packed.astype(bf16), "ctx", 0, 2).reshape(-1, width).astype(f32)
    smalls = smalls.reshape(dp_high, dp_low, 1, -1)
    smalls = scatter_bits(smalls.swapaxes(0, 1), "dp", 0, dp_low)
    dw = scatter_bits(dw, "dp", high_at, dp_high)
    dw, smalls = tie(dw.astype(bf16), smalls)
    smalls = scatter_bits(smalls, "dp", high_at, dp_high)[0]
    dw = gather_bits(dw, "ctx", 1, ring).reshape(shard, 3 * half)
    dw_other = swap(dw, "ctx", 1)
    dw = jnp.stack([jnp.where(core == 0, dw_other, dw), jnp.where(core == 0, dw, dw_other)], 1)
    grad_qkv = from_core(dw).astype(f32)

    down_at, up_at, end = shard, shard + ff // dp, shard + 2 * (ff // dp)
    grad_up = packed[up_at:end].reshape(ff // width, shard, width).swapaxes(0, 1).reshape(shard, ff)
    small_out = lambda at: smalls[at * shard : (at + 1) * shard]
    late_out = lambda at: packed[-16, at * shard : (at + 1) * shard]
    return (
        hidden_out[None],
        grad_hidden[None],
        small_out(0),
        small_out(1),
        grad_qkv,
        jnp.stack([small_out(2), small_out(3)]),
        packed[:shard],
        late_out(0),
        late_out(1),
        late_out(2),
        grad_up,
        packed[-16, 4 * shard : 4 * shard + ff // dp],
        packed[down_at:up_at],
        late_out(3),
    )


def solution(mesh):
    return jax.shard_map(
        on_device,
        mesh=mesh,
        in_specs=(
            P("dp", "ctx", None), P("dp"), P("dp", "ctx", None), P("dp"), P("dp"), P("dp", None), P(None, "dp"),
            P("dp", None), P("dp"), P("dp"), P("dp"), P("dp", None), P("dp"), P("dp", None), P("dp"),
        ),
        out_specs=(
            P("dp", "ctx", None), P("dp", "ctx", None), P("dp"), P("dp"), P("dp", None), P(None, "dp"), P("dp", None),
            P("dp"), P("dp"), P("dp"), P("dp", None), P("dp"), P("dp", None), P("dp"),
        ),
        check_vma=False,
    )
```

```python
import functools

import jax
import jax.numpy as jnp
from jax import lax
from jax.experimental import pallas as pl
from jax.experimental.pallas import tpu as pltpu
from jax.sharding import PartitionSpec as P

HEADS = 8
HEAD_DIM = 64
EPS = 1e-05
LOG2E = 1.4426950408889634
LN2 = 0.6931471805599453
LOW = -1e30
TOP = 1e30
f32 = jnp.float32
bf16 = jnp.bfloat16


def dot(left, right, left_dim, right_dim):
    return lax.dot_general(left, right, (((left_dim,), (right_dim,)), ((), ())), preferred_element_type=f32)


def split_three(values):
    one = values.astype(bf16)
    rest = values - one.astype(f32)
    two = rest.astype(bf16)
    return one, two, (rest - two.astype(f32)).astype(bf16)


def counts_of(info_ref, hop, rows):
    length, source = info_ref[2], info_ref[3] ^ (2 * hop)
    return jnp.clip(length - source * rows, 0, rows), jnp.clip(length - (source ^ 1) * rows, 0, rows), info_ref[0] * rows


def forward_kernel(info_ref, qa_ref, qb_ref, ka_ref, kb_ref, va_ref, vb_ref, *rest, blk, hop, first, last, aliases):
    prev, rest = ((None, None), rest) if first else (rest[:2], rest[2:])
    rest = rest[aliases:]
    low_refs, rest = (rest[:2], rest[2:]) if last else (None, rest)
    o_ref, stat_ref, own_ref, p_ref, keys, values = rest
    chunk = pl.program_id(1)
    rows = qa_ref.shape[1]
    span = keys.shape[0]
    *valid, start = counts_of(info_ref, hop, rows)
    alive = valid[0] + valid[1] > 0

    def finish(out, sums, top):
        own_ref[0] = jnp.broadcast_to(top, (8, rows))
        if not first:
            old_sums, old_top = prev[1][0, 0:1], prev[1][0, 1:2]
            new_top = jnp.maximum(top, old_top)
            scale, old_scale = jnp.exp2(top - new_top), jnp.exp2(old_top - new_top)
            out = out * scale + prev[0][...] * old_scale
            sums = sums * scale + old_sums * old_scale
            top = new_top
        stat_ref[0] = jnp.concatenate([sums, top, jnp.zeros((6, rows), f32)], 0)
        if last:
            out = out / sums
            for which, low_ref in enumerate(low_refs):

                @pl.when(chunk == which)
                def _():
                    low_ref[...] = out.astype(bf16)

        o_ref[...] = out

    @pl.when(jnp.logical_and(alive, chunk == 0))
    def _():
        pos = lax.broadcasted_iota(jnp.int32, (HEAD_DIM, rows), 1)
        row = lax.broadcasted_iota(jnp.int32, (HEAD_DIM, rows), 0)
        for part, (k_ref, v_ref) in enumerate(((ka_ref, va_ref), (kb_ref, vb_ref))):
            mask = jnp.where(pos < valid[part], 0.0, LOW)
            extra = jnp.where(row < 3, 1.0, jnp.where(row == 3, mask, 0.0)).astype(bf16)
            keys[pl.ds(part * rows, rows), :] = jnp.concatenate([k_ref[...], extra], 0).T
            values[:, pl.ds(part * rows, rows)] = v_ref[...]

    @pl.when(jnp.logical_not(alive))
    def _():
        finish(jnp.zeros((HEAD_DIM, rows), f32), jnp.zeros((1, rows), f32), jnp.full((1, rows), LOW, f32))

    @pl.when(alive)
    def _():
        query = jnp.where(chunk == 0, qa_ref[...], qb_ref[...])
        row = lax.broadcasted_iota(jnp.int32, (HEAD_DIM, rows), 0)
        head_blk = 64

        def extend(top):
            one, two, three = [jnp.broadcast_to(-x.astype(f32), (HEAD_DIM, rows)) for x in split_three(top)]
            extra = jnp.where(row == 0, one, jnp.where(row == 1, two, jnp.where(row == 2, three, jnp.where(row == 3, 1.0, 0.0))))
            return jnp.concatenate([query, extra.astype(bf16)], 0)

        plain = extend(jnp.zeros((1, rows), f32))
        guess = jnp.max(dot(keys[pl.ds(pl.multiple_of(start, head_blk), head_blk), :], plain, 1, 0), axis=0, keepdims=True)

        def run(top, unroll):
            query_ext = extend(top)

            def body(step, carry):
                total, sums = carry
                off = step * blk if isinstance(step, int) else pl.multiple_of(step * blk, blk)
                wide = jnp.exp2(dot(keys[pl.ds(off, blk), :], query_ext, 1, 0))
                probs = wide.astype(bf16)
                p_ref[0, 0, pl.ds(off, blk), :] = probs
                sums = sums + jnp.sum(wide.reshape(blk // 8, 8, rows), axis=0)
                return total + dot(values[:, pl.ds(off, blk)], probs, 1, 0), sums

            carry = jnp.zeros((HEAD_DIM, rows), f32), jnp.zeros((8, rows), f32)
            if unroll:
                for step in range(span // blk):
                    carry = body(step, carry)
            else:
                carry = lax.fori_loop(0, span // blk, body, carry)
            sums = jnp.sum(carry[1], axis=0, keepdims=True)
            finish(carry[0], sums, top)
            return jnp.max(sums)

        largest = run(guess, True)

        @pl.when(jnp.logical_not(largest < TOP))
        def _():
            def wider(step, top):
                off = pl.multiple_of(step * head_blk, head_blk)
                return jnp.maximum(top, jnp.max(dot(keys[pl.ds(off, head_blk), :], plain, 1, 0), axis=0, keepdims=True))

            run(lax.fori_loop(0, span // head_blk, wider, jnp.full((1, rows), LOW, f32)), False)


def head_rows(base, step, rows):
    return pl.BlockSpec((HEAD_DIM, rows), lambda h, i, n: (base + step * h, 0))


def attend(info, hop, query_a, query_b, key_a, key_b, kv_base, first_head, heads, prev, low, last):
    rows = query_a.shape[1]
    span = 2 * rows
    blk = min(512, rows)
    keys, vals, ask = head_rows(kv_base, 2, rows), head_rows(kv_base + 1, 2, rows), head_rows(first_head, 1, rows)
    out_spec = pl.BlockSpec((HEAD_DIM, rows), lambda h, i, n: (first_head + h, i))
    stat_spec = pl.BlockSpec((1, 8, rows), lambda h, i, n: (first_head + h, 0, i))
    all_heads = HEADS // 2
    extra_in = [out_spec, stat_spec] if prev else []
    extra_args = list(prev) if prev else []
    if low is not None:
        extra_in, extra_args = extra_in + [pl.BlockSpec(memory_space=pl.ANY)] * 2, extra_args + list(low)
    out_specs = [out_spec, stat_spec, pl.BlockSpec((1, 8, rows), lambda h, i, n: (h, 0, i)), pl.BlockSpec((1, 1, span, rows), lambda h, i, n: (h, i, 0, 0))]
    out_shape = [
        jax.ShapeDtypeStruct((all_heads * HEAD_DIM, span), f32),
        jax.ShapeDtypeStruct((all_heads, 8, span), f32),
        jax.ShapeDtypeStruct((heads, 8, span), f32),
        jax.ShapeDtypeStruct((heads, 2, span, rows), bf16),
    ]
    shift = 2 if last else 0
    if last:
        out_specs = [head_rows(first_head, 1, rows)] * 2 + out_specs
        out_shape = [jax.ShapeDtypeStruct((all_heads * HEAD_DIM, rows), bf16)] * 2 + out_shape
    alias = {7: shift, 8: shift + 1} if prev else {}
    if low is not None:
        alias = {**alias, 9: 0, 10: 1}
    return pl.pallas_call(
        functools.partial(forward_kernel, blk=blk, hop=hop, first=not prev, last=last, aliases=0 if low is None else 2),
        grid_spec=pltpu.PrefetchScalarGridSpec(
            num_scalar_prefetch=1,
            grid=(heads, 2),
            in_specs=[ask, ask, keys, keys, vals, vals] + extra_in,
            out_specs=out_specs,
            scratch_shapes=[pltpu.VMEM((span, 2 * HEAD_DIM), bf16), pltpu.VMEM((HEAD_DIM, span), bf16)],
        ),
        out_shape=out_shape,
        input_output_aliases=alias,
        cost_estimate=pl.CostEstimate(
            flops=16 * heads * span * span * HEAD_DIM, bytes_accessed=2 * heads * span * span, transcendentals=heads * span * span
        ),
        name="attend",
    )(info, query_a, query_b, key_a, key_b, key_a, key_b, *extra_args)


def backward_kernel(
    info_ref, qa_ref, qb_ref, ka_ref, kb_ref, va_ref, vb_ref, ga_ref, gb_ref, o_ref, stat_ref, own_ref, p_ref,
    *rest, blk, hop, adds, aliases, last,
):
    before_ref, rest = (rest[0], rest[1:]) if adds else (None, rest)
    rest = rest[aliases:]
    dq_refs, (*dkv_refs, values, dk_sum, dv_sum) = (rest[:2], rest[2:]) if last else (rest[:1], rest[1:])
    chunk = pl.program_id(1)
    rows = qa_ref.shape[1]
    span = values.shape[0]
    valid_a, valid_b, _ = counts_of(info_ref, hop, rows)
    alive = valid_a + valid_b > 0
    row = lax.broadcasted_iota(jnp.int32, (HEAD_DIM, rows), 0)

    def finish(dq):
        if adds:
            dq = dq + before_ref[...]
        if not last:
            dq_refs[0][...] = dq
            return
        for which, dq_ref in enumerate(dq_refs):

            @pl.when(chunk == which)
            def _():
                dq_ref[...] = (dq * HEAD_DIM**-0.5).astype(bf16)

    @pl.when(chunk == 0)
    def _():
        extra = jnp.where(row < 3, 1.0, 0.0).astype(bf16)
        for part, v_ref in enumerate((va_ref, vb_ref)):
            values[pl.ds(part * rows, rows), :] = jnp.concatenate([v_ref[...], extra], 0).T
        dk_sum[...] = jnp.zeros_like(dk_sum)
        dv_sum[...] = jnp.zeros_like(dv_sum)

    @pl.when(jnp.logical_not(alive))
    def _():
        finish(jnp.zeros((HEAD_DIM, rows), f32))

    @pl.when(alive)
    def _():
        query = jnp.where(chunk == 0, qa_ref[...], qb_ref[...])
        grad = jnp.where(chunk == 0, ga_ref[...], gb_ref[...])
        factor = jnp.exp2(own_ref[0, 0:1] - stat_ref[0, 1:2]) / stat_ref[0, 0:1]
        grad = (grad.astype(f32) * factor).astype(bf16)
        delta = jnp.sum(grad.astype(f32) * o_ref[...], axis=0, keepdims=True)
        one, two, three = [jnp.broadcast_to(-x.astype(f32), (HEAD_DIM, rows)) for x in split_three(delta)]
        extra = jnp.where(row == 0, one, jnp.where(row == 1, two, jnp.where(row == 2, three, 0.0))).astype(bf16)
        grad_ext = jnp.concatenate([grad, extra], 0)
        dq = jnp.zeros((HEAD_DIM, rows), f32)
        for step in range(span // blk):
            off = step * blk
            probs = p_ref[0, 0, pl.ds(off, blk), :]
            grad_scores = (probs.astype(f32) * dot(values[pl.ds(off, blk), :], grad_ext, 1, 0)).astype(bf16)
            k_ref = (ka_ref, kb_ref)[off // rows]
            dq = dq + dot(k_ref[:, pl.ds(off % rows, blk)], grad_scores, 1, 0)
            dv_sum[:, pl.ds(off, blk)] += dot(grad, probs, 1, 1)
            dk_sum[:, pl.ds(off, blk)] += dot(query, grad_scores, 1, 1)
        finish(dq)

    @pl.when(chunk == pl.num_programs(1) - 1)
    def _():
        for which, dkv_ref in enumerate(dkv_refs):
            dkv_ref[0:HEAD_DIM] = (dk_sum[:, which * rows : (which + 1) * rows] * LN2).astype(bf16)
            dkv_ref[HEAD_DIM:] = dv_sum[:, which * rows : (which + 1) * rows].astype(bf16)


def attend_back(info, hop, query_a, query_b, key_a, key_b, kv_base, p_base, first_head, heads, grad_a, grad_b, attended, stat, own, probs, before, last):
    rows = query_a.shape[1]
    span = 2 * rows
    blk = min(512, rows)
    keys, vals, ask = head_rows(kv_base, 2, rows), head_rows(kv_base + 1, 2, rows), head_rows(first_head, 1, rows)
    part = pl.BlockSpec((HEAD_DIM, rows), lambda h, i, n: (first_head + h, i))
    buffer, adds = before
    alias, extra_in, extra_args = {}, [], []
    if adds:
        extra_in, extra_args = [part], [buffer]
        alias = {} if last else {13: 0}
    elif buffer is not None:
        extra_in, extra_args, alias = [pl.BlockSpec(memory_space=pl.ANY)], [buffer], {13: 0}
    return pl.pallas_call(
        functools.partial(backward_kernel, blk=blk, adds=adds, hop=hop, aliases=len(extra_in) - int(adds), last=last),
        grid_spec=pltpu.PrefetchScalarGridSpec(
            num_scalar_prefetch=1,
            grid=(heads, 2),
            in_specs=[
                ask, ask, keys, keys, vals, vals, ask, ask,
                part,
                pl.BlockSpec((1, 8, rows), lambda h, i, n: (first_head + h, 0, i)),
                pl.BlockSpec((1, 8, rows), lambda h, i, n: (p_base + h, 0, i)),
                pl.BlockSpec((1, 1, span, rows), lambda h, i, n: (p_base + h, i, 0, 0)),
            ] + extra_in,
            out_specs=([head_rows(0, 1, rows)] * 2 if last else [part]) + [pl.BlockSpec((2 * HEAD_DIM, rows), lambda h, i, n: (h, 0))] * 2,
            scratch_shapes=[
                pltpu.VMEM((span, 2 * HEAD_DIM), bf16),
                pltpu.VMEM((HEAD_DIM, span), f32),
                pltpu.VMEM((HEAD_DIM, span), f32),
            ],
        ),
        out_shape=[
            *([jax.ShapeDtypeStruct((heads * HEAD_DIM, rows), bf16)] * 2 if last else [jax.ShapeDtypeStruct((HEADS // 2 * HEAD_DIM, span), f32)]),
            *[jax.ShapeDtypeStruct((heads * 2 * HEAD_DIM, rows), bf16)] * 2,
        ],
        input_output_aliases=alias,
        cost_estimate=pl.CostEstimate(
            flops=32 * heads * span * span * HEAD_DIM, bytes_accessed=2 * heads * span * span, transcendentals=0
        ),
        name="attend_back",
    )(info, query_a, query_b, key_a, key_b, key_a, key_b, grad_a, grad_b, attended, stat, own, probs, *extra_args)


def middle_kernel(
    info_ref, mine_ref, theirs_ref, hidden_ref, cot_ref, vec_ref, *refs, ff, lows,
):
    own_stacks, other_stacks, refs = refs[:lows], refs[lows : 2 * lows], refs[2 * lows :]
    out_ref, grad_mid_ref, grad_mine_ref, grad_theirs_ref, keep_ref, send_ref, sums_ref, total, w_ref, act_s, slope_s, sems = refs
    step = pl.program_id(0)
    rows, width = hidden_ref.shape
    dp = w_ref.shape[0]
    part = w_ref.shape[1] // 2
    own_at, other_at = pl.multiple_of(info_ref[0] * part, part), pl.multiple_of((1 - info_ref[0]) * part, part)

    @pl.when(step == 0)
    def _():
        copies = []
        for j in range(lows):
            for k in range(dp // lows):
                at = info_ref[4] ^ (k * lows + j)
                for which, (stacks, row) in enumerate(((own_stacks, own_at), (other_stacks, other_at))):
                    copies.append(pltpu.make_async_copy(stacks[j].at[k], w_ref.at[at, pl.ds(row, part)], sems.at[which, j, k]))
        for copy in copies:
            copy.start()
        for copy in copies:
            copy.wait()

    shard = width // dp
    down_at, up_at = shard, shard + ff // dp
    own, other = info_ref[0], 1 - info_ref[0]
    halves = lambda which: (pl.ds(which * (dp // 2), dp // 2), pl.ds(0, shard), slice(None))
    down_rows = lambda j: (pl.ds(j * dp * width // ff, dp * width // ff), pl.ds(down_at, ff // dp), slice(None))
    up_rows = lambda j: (slice(None), pl.ds(up_at + j * shard, shard), slice(None))
    half = mine_ref.shape[0]
    blocks = ff // width

    @pl.when(step == 0)
    def _():
        total[...] = jnp.zeros_like(total)
        sums_ref[...] = jnp.zeros_like(sums_ref)

    w_mine = w_ref[halves(own)].reshape(half, width)
    w_theirs = w_ref[halves(other)].reshape(half, width)
    middle = hidden_ref[...].astype(f32) + dot(mine_ref[...], w_mine, 0, 0) + dot(theirs_ref[...], w_theirs, 0, 0) + vec_ref[0:1, 0:width]
    gain, shift, bias_down = [vec_ref[0:1, k * width : (k + 1) * width] for k in (1, 2, 3)]
    hat, scale = norm_parts(middle)
    normed = (hat * gain + shift).astype(bf16)
    out = middle + bias_down
    for j in range(blocks):
        cols = slice(j * width, (j + 1) * width)
        activated, slope = gelu_and_slope(dot(normed, w_ref[up_rows(j)].reshape(width, width), 1, 0) + vec_ref[1:2, cols])
        activated = activated.astype(bf16)
        act_s[:, cols] = activated
        slope_s[:, cols] = slope
        out = out + dot(activated, w_ref[down_rows(j)].reshape(width, width), 1, 0)
    out_ref[...] = out.astype(bf16)

    pos = step * rows + lax.broadcasted_iota(jnp.int32, (rows, width), 0)
    grad_z = jnp.where(pos < info_ref[1], cot_ref[...], jnp.zeros_like(cot_ref))
    grad_norm = jnp.zeros((rows, width), f32)
    for j in range(blocks):
        cols = slice(j * width, (j + 1) * width)
        grad_act = dot(grad_z, w_ref[down_rows(j)].reshape(width, width), 1, 1) * slope_s[:, cols]
        sums_ref[0:1, cols] += jnp.sum(grad_act, axis=0, keepdims=True)
        grad_pre = grad_act.astype(bf16)
        total[down_rows(j)] += dot(act_s[:, cols], grad_z, 0, 0).reshape(dp * width // ff, ff // dp, width)
        total[up_rows(j)] += dot(normed, grad_pre, 0, 0).reshape(dp, shard, width)
        grad_norm = grad_norm + dot(grad_pre, w_ref[up_rows(j)].reshape(width, width), 1, 1)
    grad_out = grad_z.astype(f32)
    grad_mid = grad_out + norm_back(grad_norm, hat, scale, gain)
    grad_mid_ref[...] = grad_mid
    branch = grad_mid.astype(bf16)
    for k, value in enumerate((branch.astype(f32), grad_norm * hat, grad_norm, grad_out)):
        sums_ref[1:2, k * width : (k + 1) * width] += jnp.sum(value, axis=0, keepdims=True)
    grad_mine_ref[...] = dot(w_mine, branch, 1, 1).astype(bf16)
    grad_theirs_ref[...] = dot(w_theirs, branch, 1, 1).astype(bf16)
    total[halves(own)] += dot(mine_ref[...], branch, 1, 0).reshape(dp // 2, shard, width)
    total[halves(other)] += dot(theirs_ref[...], branch, 1, 0).reshape(dp // 2, shard, width)

    @pl.when(step == pl.num_programs(0) - 1)
    def _():
        keep_ref[...] = total[:, pl.ds(own_at, part)].astype(bf16)
        send_ref[...] = total[:, pl.ds(other_at, part)].astype(bf16)


def middle_part(info, mine, theirs, hidden, cot, vectors, own, other, ff):
    half = mine.shape[0]
    rows, width = hidden.shape
    blk = min(512, rows)
    high, part, _ = own[0].shape
    lows = len(own)
    dp = high * lows
    tall = pl.BlockSpec((blk, width), lambda i, n: (i, 0))
    wide = pl.BlockSpec((half, blk), lambda i, n: (0, i))
    fixed = lambda shape: pl.BlockSpec(shape, lambda i, n: (0,) * len(shape))
    return pl.pallas_call(
        functools.partial(middle_kernel, ff=ff, lows=lows),
        grid_spec=pltpu.PrefetchScalarGridSpec(
            num_scalar_prefetch=1,
            grid=(rows // blk,),
            in_specs=[wide, wide, tall, tall, fixed(vectors.shape)] + [pl.BlockSpec(memory_space=pl.ANY)] * (2 * lows),
            out_specs=[tall, tall, wide, wide, fixed((dp, part, width)), fixed((dp, part, width)), fixed((8, ff))],
            scratch_shapes=[
                pltpu.VMEM((dp, 2 * part, width), f32),
                pltpu.VMEM((dp, 2 * part, width), bf16),
                pltpu.VMEM((blk, ff), bf16),
                pltpu.VMEM((blk, ff), f32),
                pltpu.SemaphoreType.DMA((2, lows, high)),
            ],
        ),
        out_shape=[
            jax.ShapeDtypeStruct((rows, width), bf16),
            jax.ShapeDtypeStruct((rows, width), f32),
            jax.ShapeDtypeStruct((half, rows), bf16),
            jax.ShapeDtypeStruct((half, rows), bf16),
            jax.ShapeDtypeStruct((dp, part, width), bf16),
            jax.ShapeDtypeStruct((dp, part, width), bf16),
            jax.ShapeDtypeStruct((8, ff), f32),
        ],
        cost_estimate=pl.CostEstimate(flops=12 * rows * width * (2 * ff + width) // 2, bytes_accessed=16 << 20, transcendentals=rows * ff),
        name="middle",
    )(info, mine, theirs, hidden, cot, vectors, *own, *other)


def pack_kernel(info_ref, out_ref, down_ref, up_ref, half_ref, whole):
    shard, width = out_ref.shape
    at = shard + down_ref.shape[0]
    whole[0:shard] = out_ref[...]
    whole[shard:at] = down_ref[...]
    for j in range(up_ref.shape[1] // width):
        whole[at + j * shard : at + (j + 1) * shard] = up_ref[:, j * width : (j + 1) * width]
    part = half_ref.shape[0]
    half_ref[...] = whole[pl.ds(pl.multiple_of(info_ref[0] * part, part), part)]


def pack_part(info, out_weight, down_weight, up_weight):
    shard, width = out_weight.shape
    total = shard + down_weight.shape[0] + up_weight.shape[1] // width * shard
    full = pl.BlockSpec(memory_space=pltpu.VMEM)
    return pl.pallas_call(
        pack_kernel,
        in_specs=[pl.BlockSpec(memory_space=pltpu.SMEM), full, full, full],
        out_specs=full,
        out_shape=jax.ShapeDtypeStruct((total // 2, width), bf16),
        scratch_shapes=[pltpu.VMEM((total, width), bf16)],
        name="pack",
    )(info, out_weight, down_weight, up_weight)


def place_kernel(info_ref, *refs, lows):
    own, other, out_ref = refs[:lows], refs[lows : 2 * lows], refs[2 * lows]
    for j in range(lows):
        for k in range(own[j].shape[0]):
            at = info_ref[4] ^ (k * lows + j)
            out_ref[:, pl.ds(at, 1), pl.ds(info_ref[0], 1)] = own[j][k][:, None, None]
            out_ref[:, pl.ds(at, 1), pl.ds(1 - info_ref[0], 1)] = other[j][k][:, None, None]


def place_part(info, own, other):
    count, _, rows, cols = own[0].shape
    full = pl.BlockSpec(memory_space=pltpu.VMEM)
    return pl.pallas_call(
        functools.partial(place_kernel, lows=len(own)),
        in_specs=[pl.BlockSpec(memory_space=pltpu.SMEM)] + [full] * (2 * len(own)),
        out_specs=full,
        out_shape=jax.ShapeDtypeStruct((2, count * len(own), 2, rows, cols), bf16),
        name="place",
    )(info, *own, *other)


def project_grad_kernel(*refs, groups, transposed):
    many_groups = len(groups)
    left_ref, dqs, dkvs, far = refs[0], *[refs[1 + i * many_groups : 1 + (i + 1) * many_groups] for i in range(3)]
    dw_ref, sum_ref, grads_ref, *left_out, total = refs[1 + 3 * many_groups :]
    step = pl.program_id(0)
    width = dw_ref.shape[0]
    half = width // 2

    @pl.when(step == 0)
    def _():
        total[...] = jnp.zeros_like(total)

    if transposed:
        left = left_ref[...]
    else:
        rows = left_ref.shape[0]
        ones = jnp.where(lax.broadcasted_iota(jnp.int32, (16, rows), 0) == 0, 1.0, 0.0).astype(bf16)
        left = jnp.concatenate([left_ref[...].T, ones], 0)
        left_out[0][...] = left
    for (at, many), dq_ref, dkv_ref, far_ref in zip(groups, dqs, dkvs, far):
        grads_ref[at * HEAD_DIM : (at + many) * HEAD_DIM] = dq_ref[...]
        where = slice(half + at * 2 * HEAD_DIM, half + (at + many) * 2 * HEAD_DIM)
        grads_ref[where] = (dkv_ref[...].astype(f32) + far_ref[...].astype(f32)).astype(bf16)
    total[...] += dot(left, grads_ref[...], 1, 1)

    @pl.when(step == pl.num_programs(0) - 1)
    def _():
        dw_ref[...] = total[0:width].astype(bf16)
        sum_ref[...] = jnp.broadcast_to(total[width : width + 1], sum_ref.shape)


def project_grad(left, dqs, dkvs, groups, far, transposed):
    rows = dqs[0].shape[1]
    half = HEADS // 2 * HEAD_DIM
    cols = 3 * half
    width = 2 * half
    blk = min(512, rows)
    wide = lambda n: pl.BlockSpec((n, blk), lambda i: (0, i))
    fixed = lambda shape: pl.BlockSpec(shape, lambda i: (0,) * len(shape))
    tall = pl.BlockSpec((blk, width), lambda i: (i, 0))
    out_specs = [fixed((width, cols)), fixed((8, cols)), wide(cols)]
    out_shape = [
        jax.ShapeDtypeStruct((width, cols), bf16),
        jax.ShapeDtypeStruct((8, cols), f32),
        jax.ShapeDtypeStruct((cols, rows), bf16),
    ]
    if not transposed:
        out_specs, out_shape = out_specs + [wide(width + 16)], out_shape + [jax.ShapeDtypeStruct((width + 16, rows), bf16)]
    return pl.pallas_call(
        functools.partial(project_grad_kernel, groups=groups, transposed=transposed),
        grid=(rows // blk,),
        in_specs=[wide(width + 16) if transposed else tall] + [wide(many * n * HEAD_DIM) for n in (1, 2, 2) for _, many in groups],
        out_specs=out_specs,
        out_shape=out_shape,
        scratch_shapes=[pltpu.VMEM((width + 16, cols), f32)],
        cost_estimate=pl.CostEstimate(flops=2 * rows * width * cols, bytes_accessed=6 << 20, transcendentals=0),
        name="project_grad",
    )(left, *dqs, *dkvs, *far)


def tail_kernel(info_ref, mine_ref, theirs_ref, hidden_ref, mid_ref, w_ref, vec_ref, out_ref, sums_ref):
    step = pl.program_id(0)
    width = hidden_ref.shape[1]
    cols = mine_ref.shape[0]

    @pl.when(step == 0)
    def _():
        sums_ref[...] = jnp.zeros_like(sums_ref)

    hat, scale = norm_parts(hidden_ref[...].astype(f32))
    grad_norm = dot(w_ref[pl.ds(info_ref[0], 1)].reshape(width, cols), mine_ref[...], 1, 0)
    grad_norm = (grad_norm + dot(w_ref[pl.ds(1 - info_ref[0], 1)].reshape(width, cols), theirs_ref[...], 1, 0)).T
    sums_ref[0:1] += jnp.sum(grad_norm * hat, axis=0, keepdims=True)
    sums_ref[1:2] += jnp.sum(grad_norm, axis=0, keepdims=True)
    out_ref[...] = (mid_ref[...] + norm_back(grad_norm, hat, scale, vec_ref[0:1])).astype(bf16)


def tail_part(info, mine, theirs, hidden, grad_mid, weights, vectors):
    cols = mine.shape[0]
    rows, width = hidden.shape
    blk = min(512, rows)
    tall = pl.BlockSpec((blk, width), lambda i, n: (i, 0))
    wide = pl.BlockSpec((cols, blk), lambda i, n: (0, i))
    fixed = lambda shape: pl.BlockSpec(shape, lambda i, n: (0,) * len(shape))
    return pl.pallas_call(
        tail_kernel,
        grid_spec=pltpu.PrefetchScalarGridSpec(
            num_scalar_prefetch=1,
            grid=(rows // blk,),
            in_specs=[wide, wide, tall, tall, fixed(weights.shape), fixed(vectors.shape)],
            out_specs=[tall, fixed((8, width))],
        ),
        out_shape=[jax.ShapeDtypeStruct((rows, width), bf16), jax.ShapeDtypeStruct((8, width), f32)],
        cost_estimate=pl.CostEstimate(flops=4 * rows * width * cols, bytes_accessed=8 << 20, transcendentals=rows),
        name="tail",
    )(info, mine, theirs, hidden, grad_mid, weights, vectors)


def swap(values, axis, flip):
    size = lax.axis_size(axis)
    return lax.ppermute(values, axis, [(i, i ^ flip) for i in range(size)])


def gelu_and_slope(u):
    a = 0.7978845608028654
    inner = a * (u + 0.044715 * u * u * u)
    t = jnp.tanh(inner)
    slope = 0.5 * (1 + t) + 0.5 * u * (1 - t * t) * a * (1 + 3 * 0.044715 * u * u)
    return 0.5 * u * (1 + t), slope


def norm_parts(inputs):
    center = inputs - jnp.mean(inputs, axis=-1, keepdims=True)
    scale = lax.rsqrt(jnp.mean(center * center, axis=-1, keepdims=True) + EPS)
    return center * scale, scale


def norm_back(grad, hat, scale, gain):
    e = grad * gain
    return scale * (e - jnp.mean(e, axis=-1, keepdims=True) - hat * jnp.mean(e * hat, axis=-1, keepdims=True))


def tie(*values):
    return lax.optimization_barrier(values)


def on_device(
    hidden_in, seq_lengths, out_cotangent, norm1_gain, norm1_shift, qkv_weight, qv_bias, out_weight, out_bias,
    norm2_gain, norm2_shift, up_weight, up_bias, down_weight, down_bias,
):
    rows, width = hidden_in.shape[1:]
    hidden_in, out_cotangent = hidden_in[0], out_cotangent[0]
    ff = up_weight.shape[1]
    dp, ctx = lax.axis_size("dp"), lax.axis_size("ctx")
    dp_low = 2 if dp == 8 else 4
    dp_high, high_at = dp // dp_low, dp_low.bit_length() - 1
    ring = ctx // 2
    me = lax.axis_index("ctx")
    core = me % 2
    heads = HEADS // 2
    half = heads * HEAD_DIM
    shard = width // dp
    length = seq_lengths[0]
    info = jnp.stack([core, jnp.clip(length - me * rows, 0, rows), length, me, lax.axis_index("dp")]).astype(jnp.int32)

    def by_core(cols):
        lead = cols.shape[:-1]
        cols = cols.reshape(lead + (3, 2, heads, HEAD_DIM))
        asks = cols[..., 0, :, :, :].reshape(lead + (2, half))
        pairs = jnp.moveaxis(cols[..., 1:, :, :, :], -4, -2).reshape(lead + (2, 2 * half))
        return jnp.concatenate([asks, pairs], -1)

    def from_core(cols):
        lead = cols.shape[:-2]
        asks = cols[..., :half].reshape(lead + (1, 2, heads, HEAD_DIM))
        pairs = jnp.moveaxis(cols[..., half:].reshape(lead + (2, heads, 2, HEAD_DIM)), -2, -4)
        return jnp.concatenate([asks, pairs], -4).reshape(lead + (6 * half,))

    high_stage = lambda x: [swap(x, "dp", k << high_at) for k in range(1, dp_high)]
    low_stage = lambda x: [swap(x, "dp", j) for j in range(1, dp_low)]

    piece = lax.dynamic_slice_in_dim(qkv_weight, core * (shard // 2), shard // 2, 0)
    piece = by_core(piece).swapaxes(0, 1)
    small = jnp.concatenate([norm1_gain, norm1_shift, qv_bias[0], qv_bias[1], out_bias, norm2_gain, norm2_shift, down_bias, up_bias])[None]
    pieces = [piece] + high_stage(piece)
    smalls = [small] + high_stage(small)
    pack = pack_part(info, out_weight, down_weight, up_weight)
    pieces, smalls, pack = tie(pieces, smalls, pack)
    packs = [pack] + high_stage(pack)
    stack = jnp.stack(pieces)
    own = [stack] + low_stage(stack)
    smalls = jnp.stack(smalls)
    smalls = [smalls] + low_stage(smalls)
    other = [swap(x, "ctx", 1) for x in own]
    w_qkv = place_part(info, own, other).reshape(2, width, 3 * half)

    smalls = jnp.stack(smalls, 1).reshape(dp, -1)
    small = jnp.take(smalls, lax.axis_index("dp") ^ jnp.arange(dp), axis=0).astype(f32)
    vector = lambda at: small[:, at * shard : (at + 1) * shard].reshape(width)
    gain_one, shift_one, bias_q, bias_v, bias_out, gain_two, shift_two, bias_down = [vector(at) for at in range(8)]
    bias_up = small[:, 8 * shard :].reshape(ff)
    second_rows = jnp.pad(jnp.stack([jnp.concatenate([bias_out, gain_two, shift_two, bias_down]), bias_up]), ((0, 6), (0, 0)))

    hat_one, _ = norm_parts(hidden_in.astype(f32))
    normed_one = (hat_one * gain_one + shift_one).astype(bf16)
    bias_full = by_core(jnp.concatenate([bias_q, jnp.zeros_like(bias_q), bias_v]))
    factors = jnp.where(jnp.arange(3 * half) < half, LOG2E * HEAD_DIM**-0.5, 1.0)

    def projected(which):
        pick = lambda x: lax.dynamic_index_in_dim(x, which, 0, keepdims=False)
        return ((dot(pick(w_qkv), normed_one, 0, 1) + pick(bias_full)[:, None]) * factors[:, None]).astype(bf16)

    foreign = projected(1 - core)
    mine = projected(core)
    theirs = swap(foreign, "ctx", 1)

    groups = [(0, 2), (2, 2)] if ring == 2 else [(0, heads)]
    far = []
    for k in range(1, ring):
        for at, many in groups:
            cut = slice(half + at * 2 * HEAD_DIM, half + (at + many) * 2 * HEAD_DIM)
            far.append((k, at, many, swap(mine[cut], "ctx", 2 * k), swap(foreign[cut], "ctx", 2 * k + 1)))
    call_info, packs, theirs = tie(info, packs, theirs)
    pack = jnp.stack(packs)
    own = [pack] + low_stage(pack)
    *sums, own_top, probs = attend(call_info, 0, mine, theirs, mine, theirs, heads, 0, heads, None, None, ring == 1)
    near = (own_top, probs)
    saved, low = [], None
    for n, (k, at, many, key_a, key_b) in enumerate(far):
        last = k == ring - 1
        call_info = info
        if n == 0:
            call_info, own = tie(info, own)
            other = [swap(x, "ctx", 1) for x in own]
        if n == 1:
            call_info, other = tie(info, other)
        out = attend(call_info, k, mine, theirs, key_a, key_b, 0, at, many, sums, low if last else None, last)
        if last:
            low, out = out[:2], out[2:]
        sums, own_top, probs = out[:2], out[2], out[3]
        saved.append((own_top, probs))
    attended, stat = sums
    low_theirs = swap(low[1], "ctx", 1)

    hidden_out, grad_mid, grad_mine, grad_theirs, keep, send, sums_two = middle_part(
        info, low[0], low_theirs, hidden_in, out_cotangent, second_rows, own, other, ff
    )
    grad_theirs = swap(grad_theirs, "ctx", 1)

    def pick_sum(total, axis, shift, count, sent_type=bf16):
        index = (lax.axis_index(axis) >> shift) & (count - 1)
        pick = lambda k: lax.dynamic_index_in_dim(total, index ^ k, 0, keepdims=False)
        return pick(0), [swap(pick(k).astype(sent_type), axis, k << shift) for k in range(1, count)]

    add = lambda first, rest: functools.reduce(lambda a, b: a + b.astype(f32), rest, first.astype(f32))

    def packed_chain():
        (got,) = yield [swap(send, "ctx", 1)]
        total = add(keep, [got]).reshape((dp_high, dp_low) + keep.shape[1:]).swapaxes(0, 1)
        first, sent = pick_sum(total, "dp", 0, dp_low)
        total = add(first, (yield sent))
        first, sent = pick_sum(total, "dp", high_at, dp_high)
        total = add(first, (yield sent))
        for flip in [2 << b for b in range(ring.bit_length() - 1)]:
            total = add(total, (yield [swap(total.astype(bf16), "ctx", flip)]))
        total = total.astype(bf16)
        (got,) = yield [swap(total, "ctx", 1)]
        yield [jnp.where(core == 0, total, got), jnp.where(core == 0, got, total)]

    chain = packed_chain()
    stage = next(chain)

    buffer, flying, back_mine, back_theirs = None, [], {}, {}
    shared = (grad_mine, grad_theirs, attended, stat)
    calls = [(k, at, many, key_a, key_b, 0, 0, kept) for (k, at, many, key_a, key_b), kept in zip(far, saved)]
    calls = calls + [(0, at, many, mine, theirs, heads + 2 * at, at, near) for at, many in groups]
    ends = []
    for n, (k, at, many, key_a, key_b, kv_base, p_base, kept) in enumerate(calls):
        call_info = info
        if n:
            call_info, stage = tie(info, stage)
            stage = chain.send(stage)
        if n > 1 and flying:
            call_info, (got_mine, got_theirs), where = *tie(call_info, flying[0][:2]), flying.pop(0)[2]
            back_mine.setdefault(where, []).append(got_mine)
            back_theirs.setdefault(where, []).append(got_theirs)
        outs = attend_back(call_info, k, mine, theirs, key_a, key_b, kv_base, p_base, at, many, *shared, *kept, (buffer, k == 0 or k > 1), k == 0)
        if k:
            buffer = outs[0]
            flying.append((swap(outs[1], "ctx", 2 * k), swap(outs[2], "ctx", 2 * k + 1), at))
        else:
            dq_a, dq_b, dkv_a, dkv_b = outs
            ends.append((dq_a, swap(dq_b, "ctx", 1), dkv_a, swap(dkv_b, "ctx", 1)))
    for got_mine, got_theirs, where in flying:
        back_mine.setdefault(where, []).append(got_mine)
        back_theirs.setdefault(where, []).append(got_theirs)
    dqs_mine, dqs_theirs, dkvs_mine, dkvs_theirs = zip(*ends)
    sum_far = lambda parts: [functools.reduce(lambda a, b: (a.astype(f32) + b.astype(f32)).astype(bf16), parts[at]) for at, _ in groups]

    dw_out, bias_mine, grads_mine, left = project_grad(normed_one, dqs_mine, dkvs_mine, groups, sum_far(back_mine), False)
    dw_in = swap(dw_out, "ctx", 1)
    dw, bias_theirs, grads_theirs = project_grad(left, dqs_theirs, dkvs_theirs, groups, sum_far(back_theirs), True)
    gains = jnp.broadcast_to(gain_one[None], (8, width))

    while True:
        try:
            stage = chain.send(stage)
        except StopIteration:
            break
    packed = jnp.concatenate(stage, 0).astype(f32)

    total = add(dw, [dw_in]).reshape(dp_high, dp_low, shard, 3 * half).swapaxes(0, 1)
    first, sent = pick_sum(total, "dp", 0, dp_low)
    grad_hidden, sums_one = tail_part(info, grads_mine, grads_theirs, hidden_in, grad_mid, w_qkv, gains)
    spread = lambda x: x.reshape(-1, dp, x.shape[-1] // dp).swapaxes(0, 1).reshape(dp, -1)
    bias_one = jnp.where(core == 0, bias_mine[0], bias_theirs[0])
    bias_two = jnp.where(core == 0, bias_theirs[0], bias_mine[0])
    bias_sums = from_core(jnp.stack([bias_one, bias_two])).reshape(3, width)
    smalls = jnp.concatenate(
        [spread(sums_one[0:2]), spread(bias_sums[0:1]), spread(bias_sums[2:3]), spread(sums_two[1].reshape(4, width)), spread(sums_two[0].reshape(1, ff))], 1
    )
    smalls = smalls + swap(smalls, "ctx", 1)
    for flip in [2 << b for b in range(ring.bit_length() - 1)]:
        smalls = smalls + swap(smalls, "ctx", flip)
    sent, smalls = tie(sent, smalls)
    total = add(first, sent)
    small_first, small_sent = pick_sum(smalls.reshape(dp_high, dp_low, 1, -1).swapaxes(0, 1), "dp", 0, dp_low, f32)
    smalls = functools.reduce(jnp.add, small_sent, small_first)
    first, sent = pick_sum(total, "dp", high_at, dp_high)
    sent, smalls = tie(sent, smalls)
    total = add(first, sent)
    small_first, small_sent = pick_sum(smalls, "dp", high_at, dp_high, f32)
    smalls = functools.reduce(jnp.add, small_sent, small_first)[0]
    for flip in [2 << b for b in range(ring.bit_length() - 1)]:
        total = add(total, [swap(total.astype(bf16), "ctx", flip)])
    total = total.astype(bf16)
    got = swap(total, "ctx", 1)
    grad_qkv = from_core(jnp.stack([jnp.where(core == 0, got, total), jnp.where(core == 0, total, got)], 1)).astype(f32)

    down_at, up_at = shard, shard + ff // dp
    grad_up = packed[up_at:].reshape(ff // width, shard, width).swapaxes(0, 1).reshape(shard, ff)
    small_out = lambda at: smalls[at * shard : (at + 1) * shard]
    return (
        hidden_out[None],
        grad_hidden[None],
        small_out(0),
        small_out(1),
        grad_qkv,
        jnp.stack([small_out(2), small_out(3)]),
        packed[:shard],
        small_out(4),
        small_out(5),
        small_out(6),
        grad_up,
        smalls[8 * shard :],
        packed[down_at:up_at],
        small_out(7),
    )


def solution(mesh):
    return jax.shard_map(
        on_device,
        mesh=mesh,
        in_specs=(
            P("dp", "ctx", None), P("dp"), P("dp", "ctx", None), P("dp"), P("dp"), P("dp", None), P(None, "dp"),
            P("dp", None), P("dp"), P("dp"), P("dp"), P("dp", None), P("dp"), P("dp", None), P("dp"),
        ),
        out_specs=(
            P("dp", "ctx", None), P("dp", "ctx", None), P("dp"), P("dp"), P("dp", None), P(None, "dp"), P("dp", None),
            P("dp"), P("dp"), P("dp"), P("dp", None), P("dp"), P("dp", None), P("dp"),
        ),
        check_vma=False,
    )
```

```python
import functools

import jax
import jax.numpy as jnp
from jax import lax
from jax.experimental import pallas as pl
from jax.experimental.pallas import tpu as pltpu
from jax.sharding import PartitionSpec as P

HEADS = 8
HEAD_DIM = 64
EPS = 1e-05
LOG2E = 1.4426950408889634
LN2 = 0.6931471805599453
LOW = -1e30
TOP = 1e30
f32 = jnp.float32
bf16 = jnp.bfloat16


def dot(left, right, left_dim, right_dim):
    return lax.dot_general(left, right, (((left_dim,), (right_dim,)), ((), ())), preferred_element_type=f32)


def split_three(values):
    one = values.astype(bf16)
    rest = values - one.astype(f32)
    two = rest.astype(bf16)
    return one, two, (rest - two.astype(f32)).astype(bf16)


def counts_of(info_ref, hop, rows):
    length, source = info_ref[2], info_ref[3] ^ (2 * hop)
    return jnp.clip(length - source * rows, 0, rows), jnp.clip(length - (source ^ 1) * rows, 0, rows), info_ref[0] * rows


def forward_kernel(info_ref, qa_ref, qb_ref, ka_ref, kb_ref, va_ref, vb_ref, *rest, blk, hop, first, last, aliases):
    prev, rest = ((None, None), rest) if first else (rest[:2], rest[2:])
    rest = rest[aliases:]
    low_refs, rest = (rest[:2], rest[2:]) if last else (None, rest)
    o_ref, stat_ref, own_ref, p_ref, keys, values = rest
    chunk = pl.program_id(1)
    rows = qa_ref.shape[1]
    span = keys.shape[0]
    *valid, start = counts_of(info_ref, hop, rows)
    alive = valid[0] + valid[1] > 0

    def finish(out, sums, top):
        own_ref[0] = jnp.broadcast_to(top, (8, rows))
        if not first:
            old_sums, old_top = prev[1][0, 0:1], prev[1][0, 1:2]
            new_top = jnp.maximum(top, old_top)
            scale, old_scale = jnp.exp2(top - new_top), jnp.exp2(old_top - new_top)
            out = out * scale + prev[0][...] * old_scale
            sums = sums * scale + old_sums * old_scale
            top = new_top
        stat_ref[0] = jnp.concatenate([sums, top, jnp.zeros((6, rows), f32)], 0)
        if last:
            out = out / sums
            for which, low_ref in enumerate(low_refs):

                @pl.when(chunk == which)
                def _():
                    low_ref[...] = out.astype(bf16)

        o_ref[...] = out

    @pl.when(jnp.logical_and(alive, chunk == 0))
    def _():
        pos = lax.broadcasted_iota(jnp.int32, (HEAD_DIM, rows), 1)
        row = lax.broadcasted_iota(jnp.int32, (HEAD_DIM, rows), 0)
        for part, (k_ref, v_ref) in enumerate(((ka_ref, va_ref), (kb_ref, vb_ref))):
            mask = jnp.where(pos < valid[part], 0.0, LOW)
            extra = jnp.where(row < 3, 1.0, jnp.where(row == 3, mask, 0.0)).astype(bf16)
            keys[pl.ds(part * rows, rows), :] = jnp.concatenate([k_ref[...], extra], 0).T
            values[:, pl.ds(part * rows, rows)] = v_ref[...]

    @pl.when(jnp.logical_not(alive))
    def _():
        finish(jnp.zeros((HEAD_DIM, rows), f32), jnp.zeros((1, rows), f32), jnp.full((1, rows), LOW, f32))

    @pl.when(alive)
    def _():
        query = jnp.where(chunk == 0, qa_ref[...], qb_ref[...])
        row = lax.broadcasted_iota(jnp.int32, (HEAD_DIM, rows), 0)
        head_blk = 64

        def extend(top):
            one, two, three = [jnp.broadcast_to(-x.astype(f32), (HEAD_DIM, rows)) for x in split_three(top)]
            extra = jnp.where(row == 0, one, jnp.where(row == 1, two, jnp.where(row == 2, three, jnp.where(row == 3, 1.0, 0.0))))
            return jnp.concatenate([query, extra.astype(bf16)], 0)

        plain = extend(jnp.zeros((1, rows), f32))
        guess = jnp.max(dot(keys[pl.ds(pl.multiple_of(start, head_blk), head_blk), :], plain, 1, 0), axis=0, keepdims=True)

        def run(top, unroll):
            query_ext = extend(top)

            def body(step, carry):
                total, sums = carry
                off = step * blk if isinstance(step, int) else pl.multiple_of(step * blk, blk)
                wide = jnp.exp2(dot(keys[pl.ds(off, blk), :], query_ext, 1, 0))
                probs = wide.astype(bf16)
                p_ref[0, 0, pl.ds(off, blk), :] = probs
                sums = sums + jnp.sum(wide.reshape(blk // 8, 8, rows), axis=0)
                return total + dot(values[:, pl.ds(off, blk)], probs, 1, 0), sums

            carry = jnp.zeros((HEAD_DIM, rows), f32), jnp.zeros((8, rows), f32)
            if unroll:
                for step in range(span // blk):
                    carry = body(step, carry)
            else:
                carry = lax.fori_loop(0, span // blk, body, carry)
            sums = jnp.sum(carry[1], axis=0, keepdims=True)
            finish(carry[0], sums, top)
            return jnp.max(sums)

        largest = run(guess, True)

        @pl.when(jnp.logical_not(largest < TOP))
        def _():
            def wider(step, top):
                off = pl.multiple_of(step * head_blk, head_blk)
                return jnp.maximum(top, jnp.max(dot(keys[pl.ds(off, head_blk), :], plain, 1, 0), axis=0, keepdims=True))

            run(lax.fori_loop(0, span // head_blk, wider, jnp.full((1, rows), LOW, f32)), False)


def head_rows(base, step, rows):
    return pl.BlockSpec((HEAD_DIM, rows), lambda h, i, n: (base + step * h, 0))


def attend(info, hop, query_a, query_b, key_a, key_b, kv_base, first_head, heads, prev, low, last):
    rows = query_a.shape[1]
    span = 2 * rows
    blk = min(512, rows)
    keys, vals, ask = head_rows(kv_base, 2, rows), head_rows(kv_base + 1, 2, rows), head_rows(first_head, 1, rows)
    out_spec = pl.BlockSpec((HEAD_DIM, rows), lambda h, i, n: (first_head + h, i))
    stat_spec = pl.BlockSpec((1, 8, rows), lambda h, i, n: (first_head + h, 0, i))
    all_heads = HEADS // 2
    extra_in = [out_spec, stat_spec] if prev else []
    extra_args = list(prev) if prev else []
    if low is not None:
        extra_in, extra_args = extra_in + [pl.BlockSpec(memory_space=pl.ANY)] * 2, extra_args + list(low)
    out_specs = [out_spec, stat_spec, pl.BlockSpec((1, 8, rows), lambda h, i, n: (h, 0, i)), pl.BlockSpec((1, 1, span, rows), lambda h, i, n: (h, i, 0, 0))]
    out_shape = [
        jax.ShapeDtypeStruct((all_heads * HEAD_DIM, span), f32),
        jax.ShapeDtypeStruct((all_heads, 8, span), f32),
        jax.ShapeDtypeStruct((heads, 8, span), f32),
        jax.ShapeDtypeStruct((heads, 2, span, rows), bf16),
    ]
    shift = 2 if last else 0
    if last:
        out_specs = [head_rows(first_head, 1, rows)] * 2 + out_specs
        out_shape = [jax.ShapeDtypeStruct((all_heads * HEAD_DIM, rows), bf16)] * 2 + out_shape
    alias = {7: shift, 8: shift + 1} if prev else {}
    if low is not None:
        alias = {**alias, 9: 0, 10: 1}
    return pl.pallas_call(
        functools.partial(forward_kernel, blk=blk, hop=hop, first=not prev, last=last, aliases=0 if low is None else 2),
        grid_spec=pltpu.PrefetchScalarGridSpec(
            num_scalar_prefetch=1,
            grid=(heads, 2),
            in_specs=[ask, ask, keys, keys, vals, vals] + extra_in,
            out_specs=out_specs,
            scratch_shapes=[pltpu.VMEM((span, 2 * HEAD_DIM), bf16), pltpu.VMEM((HEAD_DIM, span), bf16)],
        ),
        out_shape=out_shape,
        input_output_aliases=alias,
        cost_estimate=pl.CostEstimate(
            flops=16 * heads * span * span * HEAD_DIM, bytes_accessed=2 * heads * span * span, transcendentals=heads * span * span
        ),
        name="attend",
    )(info, query_a, query_b, key_a, key_b, key_a, key_b, *extra_args)


def backward_kernel(
    info_ref, qa_ref, qb_ref, ka_ref, kb_ref, va_ref, vb_ref, ga_ref, gb_ref, o_ref, stat_ref, own_ref, p_ref,
    *rest, blk, hop, adds, aliases, last,
):
    before_ref, rest = (rest[0], rest[1:]) if adds else (None, rest)
    rest = rest[aliases:]
    dq_refs, (*dkv_refs, values, dk_sum, dv_sum) = (rest[:2], rest[2:]) if last else (rest[:1], rest[1:])
    chunk = pl.program_id(1)
    rows = qa_ref.shape[1]
    span = values.shape[0]
    valid_a, valid_b, _ = counts_of(info_ref, hop, rows)
    alive = valid_a + valid_b > 0
    row = lax.broadcasted_iota(jnp.int32, (HEAD_DIM, rows), 0)

    def finish(dq):
        if adds:
            dq = dq + before_ref[...]
        if not last:
            dq_refs[0][...] = dq
            return
        for which, dq_ref in enumerate(dq_refs):

            @pl.when(chunk == which)
            def _():
                dq_ref[...] = (dq * HEAD_DIM**-0.5).astype(bf16)

    @pl.when(chunk == 0)
    def _():
        extra = jnp.where(row < 3, 1.0, 0.0).astype(bf16)
        for part, v_ref in enumerate((va_ref, vb_ref)):
            values[pl.ds(part * rows, rows), :] = jnp.concatenate([v_ref[...], extra], 0).T
        dk_sum[...] = jnp.zeros_like(dk_sum)
        dv_sum[...] = jnp.zeros_like(dv_sum)

    @pl.when(jnp.logical_not(alive))
    def _():
        finish(jnp.zeros((HEAD_DIM, rows), f32))

    @pl.when(alive)
    def _():
        query = jnp.where(chunk == 0, qa_ref[...], qb_ref[...])
        grad = jnp.where(chunk == 0, ga_ref[...], gb_ref[...])
        factor = jnp.exp2(own_ref[0, 0:1] - stat_ref[0, 1:2]) / stat_ref[0, 0:1]
        grad = (grad.astype(f32) * factor).astype(bf16)
        delta = jnp.sum(grad.astype(f32) * o_ref[...], axis=0, keepdims=True)
        one, two, three = [jnp.broadcast_to(-x.astype(f32), (HEAD_DIM, rows)) for x in split_three(delta)]
        extra = jnp.where(row == 0, one, jnp.where(row == 1, two, jnp.where(row == 2, three, 0.0))).astype(bf16)
        grad_ext = jnp.concatenate([grad, extra], 0)
        dq = jnp.zeros((HEAD_DIM, rows), f32)
        for step in range(span // blk):
            off = step * blk
            probs = p_ref[0, 0, pl.ds(off, blk), :]
            grad_scores = (probs.astype(f32) * dot(values[pl.ds(off, blk), :], grad_ext, 1, 0)).astype(bf16)
            k_ref = (ka_ref, kb_ref)[off // rows]
            dq = dq + dot(k_ref[:, pl.ds(off % rows, blk)], grad_scores, 1, 0)
            dv_sum[:, pl.ds(off, blk)] += dot(grad, probs, 1, 1)
            dk_sum[:, pl.ds(off, blk)] += dot(query, grad_scores, 1, 1)
        finish(dq)

    @pl.when(chunk == pl.num_programs(1) - 1)
    def _():
        for which, dkv_ref in enumerate(dkv_refs):
            dkv_ref[0:HEAD_DIM] = (dk_sum[:, which * rows : (which + 1) * rows] * LN2).astype(bf16)
            dkv_ref[HEAD_DIM:] = dv_sum[:, which * rows : (which + 1) * rows].astype(bf16)


def attend_back(info, hop, query_a, query_b, key_a, key_b, kv_base, p_base, first_head, heads, grad_a, grad_b, attended, stat, own, probs, before, last):
    rows = query_a.shape[1]
    span = 2 * rows
    blk = min(512, rows)
    keys, vals, ask = head_rows(kv_base, 2, rows), head_rows(kv_base + 1, 2, rows), head_rows(first_head, 1, rows)
    part = pl.BlockSpec((HEAD_DIM, rows), lambda h, i, n: (first_head + h, i))
    buffer, adds = before
    alias, extra_in, extra_args = {}, [], []
    if adds:
        extra_in, extra_args = [part], [buffer]
        alias = {} if last else {13: 0}
    elif buffer is not None:
        extra_in, extra_args, alias = [pl.BlockSpec(memory_space=pl.ANY)], [buffer], {13: 0}
    return pl.pallas_call(
        functools.partial(backward_kernel, blk=blk, adds=adds, hop=hop, aliases=len(extra_in) - int(adds), last=last),
        grid_spec=pltpu.PrefetchScalarGridSpec(
            num_scalar_prefetch=1,
            grid=(heads, 2),
            in_specs=[
                ask, ask, keys, keys, vals, vals, ask, ask,
                part,
                pl.BlockSpec((1, 8, rows), lambda h, i, n: (first_head + h, 0, i)),
                pl.BlockSpec((1, 8, rows), lambda h, i, n: (p_base + h, 0, i)),
                pl.BlockSpec((1, 1, span, rows), lambda h, i, n: (p_base + h, i, 0, 0)),
            ] + extra_in,
            out_specs=([head_rows(0, 1, rows)] * 2 if last else [part]) + [pl.BlockSpec((2 * HEAD_DIM, rows), lambda h, i, n: (h, 0))] * 2,
            scratch_shapes=[
                pltpu.VMEM((span, 2 * HEAD_DIM), bf16),
                pltpu.VMEM((HEAD_DIM, span), f32),
                pltpu.VMEM((HEAD_DIM, span), f32),
            ],
        ),
        out_shape=[
            *([jax.ShapeDtypeStruct((heads * HEAD_DIM, rows), bf16)] * 2 if last else [jax.ShapeDtypeStruct((HEADS // 2 * HEAD_DIM, span), f32)]),
            *[jax.ShapeDtypeStruct((heads * 2 * HEAD_DIM, rows), bf16)] * 2,
        ],
        input_output_aliases=alias,
        cost_estimate=pl.CostEstimate(
            flops=32 * heads * span * span * HEAD_DIM, bytes_accessed=2 * heads * span * span, transcendentals=0
        ),
        name="attend_back",
    )(info, query_a, query_b, key_a, key_b, key_a, key_b, grad_a, grad_b, attended, stat, own, probs, *extra_args)


def middle_kernel(
    info_ref, mine_ref, theirs_ref, hidden_ref, cot_ref, w_ref, vec_ref,
    out_ref, grad_mid_ref, grad_mine_ref, grad_theirs_ref, packed_ref, sums_ref,
    total, act_s, slope_s, *, ff,
):
    step = pl.program_id(0)
    rows, width = hidden_ref.shape
    dp = w_ref.shape[0]
    shard = width // dp
    down_at, up_at = shard, shard + ff // dp
    own, other = info_ref[0], 1 - info_ref[0]
    halves = lambda which: (pl.ds(which * (dp // 2), dp // 2), pl.ds(0, shard), slice(None))
    down_rows = lambda j: (pl.ds(j * dp * width // ff, dp * width // ff), pl.ds(down_at, ff // dp), slice(None))
    up_rows = lambda j: (slice(None), pl.ds(up_at + j * shard, shard), slice(None))
    half = mine_ref.shape[0]
    blocks = ff // width

    @pl.when(step == 0)
    def _():
        total[...] = jnp.zeros_like(total)
        sums_ref[...] = jnp.zeros_like(sums_ref)

    w_mine = w_ref[halves(own)].reshape(half, width)
    w_theirs = w_ref[halves(other)].reshape(half, width)
    middle = hidden_ref[...].astype(f32) + dot(mine_ref[...], w_mine, 0, 0) + dot(theirs_ref[...], w_theirs, 0, 0) + vec_ref[0:1, 0:width]
    gain, shift, bias_down = [vec_ref[0:1, k * width : (k + 1) * width] for k in (1, 2, 3)]
    hat, scale = norm_parts(middle)
    normed = (hat * gain + shift).astype(bf16)
    out = middle + bias_down
    for j in range(blocks):
        cols = slice(j * width, (j + 1) * width)
        activated, slope = gelu_and_slope(dot(normed, w_ref[up_rows(j)].reshape(width, width), 1, 0) + vec_ref[1:2, cols])
        activated = activated.astype(bf16)
        act_s[:, cols] = activated
        slope_s[:, cols] = slope
        out = out + dot(activated, w_ref[down_rows(j)].reshape(width, width), 1, 0)
    out_ref[...] = out.astype(bf16)

    pos = step * rows + lax.broadcasted_iota(jnp.int32, (rows, width), 0)
    grad_z = jnp.where(pos < info_ref[1], cot_ref[...], jnp.zeros_like(cot_ref))
    grad_norm = jnp.zeros((rows, width), f32)
    for j in range(blocks):
        cols = slice(j * width, (j + 1) * width)
        grad_act = dot(grad_z, w_ref[down_rows(j)].reshape(width, width), 1, 1) * slope_s[:, cols]
        sums_ref[0:1, cols] += jnp.sum(grad_act, axis=0, keepdims=True)
        grad_pre = grad_act.astype(bf16)
        total[down_rows(j)] += dot(act_s[:, cols], grad_z, 0, 0).reshape(dp * width // ff, ff // dp, width)
        total[up_rows(j)] += dot(normed, grad_pre, 0, 0).reshape(dp, shard, width)
        grad_norm = grad_norm + dot(grad_pre, w_ref[up_rows(j)].reshape(width, width), 1, 1)
    grad_out = grad_z.astype(f32)
    grad_mid = grad_out + norm_back(grad_norm, hat, scale, gain)
    grad_mid_ref[...] = grad_mid
    branch = grad_mid.astype(bf16)
    for k, value in enumerate((branch.astype(f32), grad_norm * hat, grad_norm, grad_out)):
        sums_ref[1:2, k * width : (k + 1) * width] += jnp.sum(value, axis=0, keepdims=True)
    grad_mine_ref[...] = dot(w_mine, branch, 1, 1).astype(bf16)
    grad_theirs_ref[...] = dot(w_theirs, branch, 1, 1).astype(bf16)
    total[halves(own)] += dot(mine_ref[...], branch, 1, 0).reshape(dp // 2, shard, width)
    total[halves(other)] += dot(theirs_ref[...], branch, 1, 0).reshape(dp // 2, shard, width)

    @pl.when(step == pl.num_programs(0) - 1)
    def _():
        packed_ref[:, 0 : total.shape[1]] = total[...].astype(bf16)


def middle_part(info, mine, theirs, hidden, cot, weights, vectors, ff):
    half = mine.shape[0]
    rows, width = hidden.shape
    blk = min(512, rows)
    packed = weights.shape
    tall = pl.BlockSpec((blk, width), lambda i, n: (i, 0))
    wide = pl.BlockSpec((half, blk), lambda i, n: (0, i))
    fixed = lambda shape: pl.BlockSpec(shape, lambda i, n: (0,) * len(shape))
    return pl.pallas_call(
        functools.partial(middle_kernel, ff=ff),
        grid_spec=pltpu.PrefetchScalarGridSpec(
            num_scalar_prefetch=1,
            grid=(rows // blk,),
            in_specs=[wide, wide, tall, tall, fixed(packed), fixed(vectors.shape)],
            out_specs=[tall, tall, wide, wide, fixed(packed), fixed((8, ff))],
            scratch_shapes=[pltpu.VMEM((packed[0], packed[1] - 16, width), f32), pltpu.VMEM((blk, ff), bf16), pltpu.VMEM((blk, ff), f32)],
        ),
        out_shape=[
            jax.ShapeDtypeStruct((rows, width), bf16),
            jax.ShapeDtypeStruct((rows, width), f32),
            jax.ShapeDtypeStruct((half, rows), bf16),
            jax.ShapeDtypeStruct((half, rows), bf16),
            jax.ShapeDtypeStruct(packed, bf16),
            jax.ShapeDtypeStruct((8, ff), f32),
        ],
        cost_estimate=pl.CostEstimate(flops=12 * rows * width * (2 * ff + width) // 2, bytes_accessed=16 << 20, transcendentals=rows * ff),
        name="middle",
    )(info, mine, theirs, hidden, cot, weights, vectors)


def pack_kernel(out_ref, down_ref, up_ref, row_ref, packed_ref):
    shard, width = out_ref.shape
    at = shard + down_ref.shape[0]
    packed_ref[0:shard] = out_ref[...]
    packed_ref[shard:at] = down_ref[...]
    for j in range(up_ref.shape[1] // width):
        packed_ref[at + j * shard : at + (j + 1) * shard] = up_ref[:, j * width : (j + 1) * width]
    end = at + up_ref.shape[1] // width * shard
    packed_ref[end:] = jnp.broadcast_to(row_ref[...], (packed_ref.shape[0] - end, width))


def pack_part(out_weight, down_weight, up_weight, row):
    shard, width = out_weight.shape
    total = shard + down_weight.shape[0] + up_weight.shape[1] // width * shard + 16
    return pl.pallas_call(pack_kernel, out_shape=jax.ShapeDtypeStruct((total, width), bf16), name="pack")(out_weight, down_weight, up_weight, row)


def shape_kernel(info_ref, w_ref, small_ref, out_ref):
    part = w_ref.shape[0] // 2
    heads = HEADS // 2
    half = heads * HEAD_DIM
    block = w_ref[pl.ds(pl.multiple_of(info_ref[0] * part, part), part)]
    for which in range(2):
        cols = [block[:, which * half : (which + 1) * half]]
        for head in range(heads):
            for kind in (1, 2):
                at = (2 * kind + which) * half + head * HEAD_DIM
                cols.append(block[:, at : at + HEAD_DIM])
        out_ref[which * part : (which + 1) * part] = jnp.concatenate(cols, 1)
    out_ref[2 * part :] = jnp.broadcast_to(small_ref[...], (8, 3 * half))


def shape_part(info, weight, small):
    shard, cols = weight.shape
    full = pl.BlockSpec(memory_space=pltpu.VMEM)
    return pl.pallas_call(
        shape_kernel,
        in_specs=[pl.BlockSpec(memory_space=pltpu.SMEM), full, full],
        out_specs=full,
        out_shape=jax.ShapeDtypeStruct((shard + 8, cols // 2), bf16),
        name="shape",
    )(info, weight, small)


def place_kernel(info_ref, *refs, lows):
    own, other, out_ref, small_ref = refs[:lows], refs[lows : 2 * lows], refs[2 * lows], refs[2 * lows + 1]
    part, cols = out_ref.shape[3:]
    for j in range(lows):
        for k in range(own[j].shape[0]):
            at = info_ref[4] ^ (k * lows + j)
            out_ref[:, pl.ds(at, 1), pl.ds(info_ref[0], 1)] = own[j][k, 0 : 2 * part].reshape(2, part, cols)[:, None, None]
            out_ref[:, pl.ds(at, 1), pl.ds(1 - info_ref[0], 1)] = other[j][k, 0 : 2 * part].reshape(2, part, cols)[:, None, None]
            small_ref[pl.ds(at, 1)] = own[j][k, 2 * part :][None]


def place_part(info, own, other):
    count, rows, cols = own[0].shape
    full = pl.BlockSpec(memory_space=pltpu.VMEM)
    return pl.pallas_call(
        functools.partial(place_kernel, lows=len(own)),
        in_specs=[pl.BlockSpec(memory_space=pltpu.SMEM)] + [full] * (2 * len(own)),
        out_specs=[full, full],
        out_shape=[
            jax.ShapeDtypeStruct((2, count * len(own), 2, rows // 2 - 4, cols), bf16),
            jax.ShapeDtypeStruct((count * len(own), 8, cols), bf16),
        ],
        name="place",
    )(info, *own, *other)


def project_grad_kernel(*refs, groups, transposed):
    many_groups = len(groups)
    left_ref, dqs, dkvs, far = refs[0], *[refs[1 + i * many_groups : 1 + (i + 1) * many_groups] for i in range(3)]
    dw_ref, sum_ref, grads_ref, *left_out, total = refs[1 + 3 * many_groups :]
    step = pl.program_id(0)
    width = dw_ref.shape[0]
    half = width // 2

    @pl.when(step == 0)
    def _():
        total[...] = jnp.zeros_like(total)

    if transposed:
        left = left_ref[...]
    else:
        rows = left_ref.shape[0]
        ones = jnp.where(lax.broadcasted_iota(jnp.int32, (16, rows), 0) == 0, 1.0, 0.0).astype(bf16)
        left = jnp.concatenate([left_ref[...].T, ones], 0)
        left_out[0][...] = left
    for (at, many), dq_ref, dkv_ref, far_ref in zip(groups, dqs, dkvs, far):
        grads_ref[at * HEAD_DIM : (at + many) * HEAD_DIM] = dq_ref[...]
        where = slice(half + at * 2 * HEAD_DIM, half + (at + many) * 2 * HEAD_DIM)
        grads_ref[where] = (dkv_ref[...].astype(f32) + far_ref[...].astype(f32)).astype(bf16)
    total[...] += dot(left, grads_ref[...], 1, 1)

    @pl.when(step == pl.num_programs(0) - 1)
    def _():
        dw_ref[...] = total[0:width].astype(bf16)
        sum_ref[...] = jnp.broadcast_to(total[width : width + 1], sum_ref.shape)


def project_grad(left, dqs, dkvs, groups, far, transposed):
    rows = dqs[0].shape[1]
    half = HEADS // 2 * HEAD_DIM
    cols = 3 * half
    width = 2 * half
    blk = min(512, rows)
    wide = lambda n: pl.BlockSpec((n, blk), lambda i: (0, i))
    fixed = lambda shape: pl.BlockSpec(shape, lambda i: (0,) * len(shape))
    tall = pl.BlockSpec((blk, width), lambda i: (i, 0))
    out_specs = [fixed((width, cols)), fixed((8, cols)), wide(cols)]
    out_shape = [
        jax.ShapeDtypeStruct((width, cols), bf16),
        jax.ShapeDtypeStruct((8, cols), f32),
        jax.ShapeDtypeStruct((cols, rows), bf16),
    ]
    if not transposed:
        out_specs, out_shape = out_specs + [wide(width + 16)], out_shape + [jax.ShapeDtypeStruct((width + 16, rows), bf16)]
    return pl.pallas_call(
        functools.partial(project_grad_kernel, groups=groups, transposed=transposed),
        grid=(rows // blk,),
        in_specs=[wide(width + 16) if transposed else tall] + [wide(many * n * HEAD_DIM) for n in (1, 2, 2) for _, many in groups],
        out_specs=out_specs,
        out_shape=out_shape,
        scratch_shapes=[pltpu.VMEM((width + 16, cols), f32)],
        cost_estimate=pl.CostEstimate(flops=2 * rows * width * cols, bytes_accessed=6 << 20, transcendentals=0),
        name="project_grad",
    )(left, *dqs, *dkvs, *far)


def tail_kernel(info_ref, mine_ref, theirs_ref, hidden_ref, mid_ref, w_ref, vec_ref, out_ref, sums_ref):
    step = pl.program_id(0)
    width = hidden_ref.shape[1]
    cols = mine_ref.shape[0]

    @pl.when(step == 0)
    def _():
        sums_ref[...] = jnp.zeros_like(sums_ref)

    hat, scale = norm_parts(hidden_ref[...].astype(f32))
    grad_norm = dot(w_ref[pl.ds(info_ref[0], 1)].reshape(width, cols), mine_ref[...], 1, 0)
    grad_norm = (grad_norm + dot(w_ref[pl.ds(1 - info_ref[0], 1)].reshape(width, cols), theirs_ref[...], 1, 0)).T
    sums_ref[0:1] += jnp.sum(grad_norm * hat, axis=0, keepdims=True)
    sums_ref[1:2] += jnp.sum(grad_norm, axis=0, keepdims=True)
    out_ref[...] = (mid_ref[...] + norm_back(grad_norm, hat, scale, vec_ref[0:1])).astype(bf16)


def tail_part(info, mine, theirs, hidden, grad_mid, weights, vectors):
    cols = mine.shape[0]
    rows, width = hidden.shape
    blk = min(512, rows)
    tall = pl.BlockSpec((blk, width), lambda i, n: (i, 0))
    wide = pl.BlockSpec((cols, blk), lambda i, n: (0, i))
    fixed = lambda shape: pl.BlockSpec(shape, lambda i, n: (0,) * len(shape))
    return pl.pallas_call(
        tail_kernel,
        grid_spec=pltpu.PrefetchScalarGridSpec(
            num_scalar_prefetch=1,
            grid=(rows // blk,),
            in_specs=[wide, wide, tall, tall, fixed(weights.shape), fixed(vectors.shape)],
            out_specs=[tall, fixed((8, width))],
        ),
        out_shape=[jax.ShapeDtypeStruct((rows, width), bf16), jax.ShapeDtypeStruct((8, width), f32)],
        cost_estimate=pl.CostEstimate(flops=4 * rows * width * cols, bytes_accessed=8 << 20, transcendentals=rows),
        name="tail",
    )(info, mine, theirs, hidden, grad_mid, weights, vectors)


def swap(values, axis, flip):
    size = lax.axis_size(axis)
    return lax.ppermute(values, axis, [(i, i ^ flip) for i in range(size)])


def gelu_and_slope(u):
    a = 0.7978845608028654
    inner = a * (u + 0.044715 * u * u * u)
    t = jnp.tanh(inner)
    slope = 0.5 * (1 + t) + 0.5 * u * (1 - t * t) * a * (1 + 3 * 0.044715 * u * u)
    return 0.5 * u * (1 + t), slope


def norm_parts(inputs):
    center = inputs - jnp.mean(inputs, axis=-1, keepdims=True)
    scale = lax.rsqrt(jnp.mean(center * center, axis=-1, keepdims=True) + EPS)
    return center * scale, scale


def norm_back(grad, hat, scale, gain):
    e = grad * gain
    return scale * (e - jnp.mean(e, axis=-1, keepdims=True) - hat * jnp.mean(e * hat, axis=-1, keepdims=True))


def tie(*values):
    return lax.optimization_barrier(values)


def on_device(
    hidden_in, seq_lengths, out_cotangent, norm1_gain, norm1_shift, qkv_weight, qv_bias, out_weight, out_bias,
    norm2_gain, norm2_shift, up_weight, up_bias, down_weight, down_bias,
):
    rows, width = hidden_in.shape[1:]
    hidden_in, out_cotangent = hidden_in[0], out_cotangent[0]
    ff = up_weight.shape[1]
    dp, ctx = lax.axis_size("dp"), lax.axis_size("ctx")
    dp_low = 2 if dp == 8 else 4
    dp_high, high_at = dp // dp_low, dp_low.bit_length() - 1
    ring = ctx // 2
    me = lax.axis_index("ctx")
    core = me % 2
    heads = HEADS // 2
    half = heads * HEAD_DIM
    shard = width // dp
    length = seq_lengths[0]
    info = jnp.stack([core, jnp.clip(length - me * rows, 0, rows), length, me, lax.axis_index("dp")]).astype(jnp.int32)

    def by_core(cols):
        lead = cols.shape[:-1]
        cols = cols.reshape(lead + (3, 2, heads, HEAD_DIM))
        asks = cols[..., 0, :, :, :].reshape(lead + (2, half))
        pairs = jnp.moveaxis(cols[..., 1:, :, :, :], -4, -2).reshape(lead + (2, 2 * half))
        return jnp.concatenate([asks, pairs], -1)

    def from_core(cols):
        lead = cols.shape[:-2]
        asks = cols[..., :half].reshape(lead + (1, 2, heads, HEAD_DIM))
        pairs = jnp.moveaxis(cols[..., half:].reshape(lead + (2, heads, 2, HEAD_DIM)), -2, -4)
        return jnp.concatenate([asks, pairs], -4).reshape(lead + (6 * half,))

    high_stage = lambda x: [swap(x, "dp", k << high_at) for k in range(1, dp_high)]
    low_stage = lambda x: [swap(x, "dp", j) for j in range(1, dp_low)]

    early = jnp.concatenate([norm1_gain, norm1_shift, qv_bias[0], qv_bias[1]])
    early = jnp.pad(early, (0, 3 * half - early.shape[0]))[None]
    piece = shape_part(info, qkv_weight, early)
    pieces = [piece] + high_stage(piece)
    late = jnp.concatenate([out_bias, norm2_gain, norm2_shift, down_bias, up_bias])
    late = jnp.pad(late, (0, width - late.shape[0]))[None]
    others = pack_part(out_weight, down_weight, up_weight, late)
    others, pieces = tie(others, pieces)
    others = lax.all_gather(others, "dp", axis=0, tiled=False)
    stack = jnp.stack(pieces)
    own = [stack] + low_stage(stack)
    other = [swap(x, "ctx", 1) for x in own]
    w_qkv, early = place_part(info, own, other)
    w_qkv = w_qkv.reshape(2, width, 3 * half)
    early = early[:, 0, : 4 * shard].reshape(dp, 4, shard).swapaxes(0, 1).reshape(4, width).astype(f32)
    gain_one, shift_one, bias_q, bias_v = early

    hat_one, _ = norm_parts(hidden_in.astype(f32))
    normed_one = (hat_one * gain_one + shift_one).astype(bf16)
    bias_full = by_core(jnp.concatenate([bias_q, jnp.zeros_like(bias_q), bias_v]))
    factors = jnp.where(jnp.arange(3 * half) < half, LOG2E * HEAD_DIM**-0.5, 1.0)

    def projected(which):
        pick = lambda x: lax.dynamic_index_in_dim(x, which, 0, keepdims=False)
        return ((dot(pick(w_qkv), normed_one, 0, 1) + pick(bias_full)[:, None]) * factors[:, None]).astype(bf16)

    foreign = projected(1 - core)
    mine = projected(core)
    theirs = swap(foreign, "ctx", 1)

    groups = [(0, 2), (2, 2)] if ring == 2 else [(0, heads)]
    far = []
    for k in range(1, ring):
        for at, many in groups:
            cut = slice(half + at * 2 * HEAD_DIM, half + (at + many) * 2 * HEAD_DIM)
            far.append((k, at, many, swap(mine[cut], "ctx", 2 * k), swap(foreign[cut], "ctx", 2 * k + 1)))
    *sums, own_top, probs = attend(info, 0, mine, theirs, mine, theirs, heads, 0, heads, None, None, ring == 1)
    near = (own_top, probs)
    saved, low = [], None
    for k, at, many, key_a, key_b in far:
        last = k == ring - 1
        out = attend(info, k, mine, theirs, key_a, key_b, 0, at, many, sums, low if last else None, last)
        if last:
            low, out = out[:2], out[2:]
        sums, own_top, probs = out[:2], out[2], out[3]
        saved.append((own_top, probs))
    attended, stat = sums
    low_theirs = swap(low[1], "ctx", 1)

    rest = others[:, -16].astype(f32)
    vector = lambda at: rest[:, at * shard : (at + 1) * shard].reshape(width)
    second_rows = jnp.pad(
        jnp.stack([jnp.concatenate([vector(0), vector(1), vector(2), vector(3)]), rest[:, 4 * shard : 4 * shard + ff // dp].reshape(ff)]), ((0, 6), (0, 0))
    )
    hidden_out, grad_mid, grad_mine, grad_theirs, packed, sums_two = middle_part(
        info, low[0], low_theirs, hidden_in, out_cotangent, others, second_rows, ff
    )
    grad_theirs = swap(grad_theirs, "ctx", 1)

    spread = lambda x: x.reshape(-1, dp, x.shape[-1] // dp).swapaxes(0, 1).reshape(dp, -1)
    late = jnp.concatenate([spread(sums_two[1].reshape(4, width)), spread(sums_two[0].reshape(1, ff))], 1)
    late = jnp.pad(late, ((0, 0), (0, width - late.shape[1])))[:, None].astype(bf16)
    packed = lax.dynamic_update_slice(packed, jnp.broadcast_to(late, (dp, 16, width)), (0, packed.shape[1] - 16, 0))
    packed = lax.psum_scatter(packed, "dp", scatter_dimension=0, tiled=False)

    buffer, flying, back_mine, back_theirs = None, [], {}, {}
    shared = (grad_mine, grad_theirs, attended, stat)
    calls = [(k, at, many, key_a, key_b, 0, 0, kept) for (k, at, many, key_a, key_b), kept in zip(far, saved)]
    calls = calls + [(0, at, many, mine, theirs, heads + 2 * at, at, near) for at, many in groups]
    ends = []
    for n, (k, at, many, key_a, key_b, kv_base, p_base, kept) in enumerate(calls):
        call_info = info
        if ends:
            call_info, kept_back = tie(info, ends[-1][2])
            ends[-1] = ends[-1][:2] + (kept_back,) + ends[-1][3:]
        if n > 1 and flying:
            call_info, (got_mine, got_theirs), where = *tie(call_info, flying[0][:2]), flying.pop(0)[2]
            back_mine.setdefault(where, []).append(got_mine)
            back_theirs.setdefault(where, []).append(got_theirs)
        outs = attend_back(call_info, k, mine, theirs, key_a, key_b, kv_base, p_base, at, many, *shared, *kept, (buffer, k == 0 or k > 1), k == 0)
        if k:
            buffer = outs[0]
            flying.append((swap(outs[1], "ctx", 2 * k), swap(outs[2], "ctx", 2 * k + 1), at))
        else:
            dq_a, dq_b, dkv_a, dkv_b = outs
            ends.append((dq_a, swap(dq_b, "ctx", 1), dkv_a, swap(dkv_b, "ctx", 1)))
    for got_mine, got_theirs, where in flying:
        back_mine.setdefault(where, []).append(got_mine)
        back_theirs.setdefault(where, []).append(got_theirs)
    dqs_mine, dqs_theirs, dkvs_mine, dkvs_theirs = zip(*ends)
    sum_far = lambda parts: [functools.reduce(lambda a, b: (a.astype(f32) + b.astype(f32)).astype(bf16), parts[at]) for at, _ in groups]

    dw_out, bias_mine, grads_mine, left = project_grad(normed_one, dqs_mine, dkvs_mine, groups, sum_far(back_mine), False)
    dw_in = swap(dw_out, "ctx", 1)
    dw, bias_theirs, grads_theirs = project_grad(left, dqs_theirs, dkvs_theirs, groups, sum_far(back_theirs), True)
    gains = jnp.broadcast_to(gain_one[None], (8, width))

    grad_hidden, sums_one = tail_part(info, grads_mine, grads_theirs, hidden_in, grad_mid, w_qkv, gains)

    def halve(total, axis, shift, count, dim):
        index = (lax.axis_index(axis) >> shift) & (count - 1)
        pick = lambda k: lax.dynamic_index_in_dim(total, index ^ k, dim, keepdims=False)
        return pick(0).astype(f32), [swap(pick(k).astype(bf16), axis, k << shift) for k in range(1, count)]

    add = lambda first, rest: functools.reduce(lambda a, b: a + b.astype(f32), rest, first.astype(f32))
    flips = [2 << b for b in range(ring.bit_length() - 1)]

    def sum_chips(total):
        for flip in flips:
            total = total.astype(bf16)
            total = add(total, [swap(total, "ctx", flip)])
        return total.astype(bf16)

    bias_one = jnp.where(core == 0, bias_mine[0], bias_theirs[0])
    bias_two = jnp.where(core == 0, bias_theirs[0], bias_mine[0])
    bias_sums = from_core(jnp.stack([bias_one, bias_two])).reshape(3, width)
    smalls = jnp.concatenate([spread(sums_one[0:2]), spread(bias_sums[0:1]), spread(bias_sums[2:3])], 1)
    smalls = jnp.pad(smalls[:, None], ((0, 0), (0, 7), (0, 3 * half - smalls.shape[1])))
    total = jnp.concatenate([add(dw, [dw_in]).reshape(dp, shard, 3 * half), smalls], 1)
    first, sent = halve(total.reshape((dp_high, dp_low) + total.shape[1:]), "dp", 0, dp_low, 1)
    packed_first, packed_sent = halve(packed.reshape((2, -1) + packed.shape[1:]), "ctx", 0, 2, 0)
    sent, packed_sent = tie(sent, packed_sent)
    packed = add(packed_first, packed_sent)
    first, sent = halve(add(first, sent), "dp", high_at, dp_high, 0)
    packed = sum_chips(packed)
    sent, packed = tie(sent, packed)
    total = sum_chips(add(first, sent))
    packed_got = swap(packed, "ctx", 1)
    total, packed_got = tie(total, packed_got)
    got = swap(total, "ctx", 1)
    by_index = lambda a, b: [jnp.where(core == 0, a, b), jnp.where(core == 0, b, a)]
    packed = jnp.concatenate(by_index(packed, packed_got), 0).astype(f32)
    grad_qkv = from_core(jnp.stack(by_index(total[:shard], got[:shard])[::-1], 1)).astype(f32)
    smalls = total[shard].astype(f32) + got[shard].astype(f32)

    down_at, up_at, end = shard, shard + ff // dp, shard + 2 * (ff // dp)
    grad_up = packed[up_at:end].reshape(ff // width, shard, width).swapaxes(0, 1).reshape(shard, ff)
    small_out = lambda at: smalls[at * shard : (at + 1) * shard]
    late_out = lambda at: packed[-16, at * shard : (at + 1) * shard]
    return (
        hidden_out[None],
        grad_hidden[None],
        small_out(0),
        small_out(1),
        grad_qkv,
        jnp.stack([small_out(2), small_out(3)]),
        packed[:shard],
        late_out(0),
        late_out(1),
        late_out(2),
        grad_up,
        packed[-16, 4 * shard : 4 * shard + ff // dp],
        packed[down_at:up_at],
        late_out(3),
    )


def solution(mesh):
    return jax.shard_map(
        on_device,
        mesh=mesh,
        in_specs=(
            P("dp", "ctx", None), P("dp"), P("dp", "ctx", None), P("dp"), P("dp"), P("dp", None), P(None, "dp"),
            P("dp", None), P("dp"), P("dp"), P("dp"), P("dp", None), P("dp"), P("dp", None), P("dp"),
        ),
        out_specs=(
            P("dp", "ctx", None), P("dp", "ctx", None), P("dp"), P("dp"), P("dp", None), P(None, "dp"), P("dp", None),
            P("dp"), P("dp"), P("dp"), P("dp", None), P("dp"), P("dp", None), P("dp"),
        ),
        check_vma=False,
    )
```

```python
import functools

import jax
import jax.numpy as jnp
from jax import lax
from jax.experimental import pallas as pl
from jax.experimental.pallas import tpu as pltpu
from jax.sharding import PartitionSpec as P

HEADS = 8
HEAD_DIM = 64
EPS = 1e-05
LOG2E = 1.4426950408889634
LN2 = 0.6931471805599453
LOW = -1e30
TOP = 1e30
f32 = jnp.float32
bf16 = jnp.bfloat16


def dot(left, right, left_dim, right_dim):
    return lax.dot_general(left, right, (((left_dim,), (right_dim,)), ((), ())), preferred_element_type=f32)


def split_three(values):
    one = values.astype(bf16)
    rest = values - one.astype(f32)
    two = rest.astype(bf16)
    return one, two, (rest - two.astype(f32)).astype(bf16)


def counts_of(info_ref, hop, rows):
    length, source = info_ref[2], info_ref[3] ^ (2 * hop)
    return jnp.clip(length - source * rows, 0, rows), jnp.clip(length - (source ^ 1) * rows, 0, rows), info_ref[0] * rows


def forward_kernel(info_ref, qa_ref, qb_ref, ka_ref, kb_ref, va_ref, vb_ref, *rest, blk, hop, first, last, aliases):
    prev, rest = ((None, None), rest) if first else (rest[:2], rest[2:])
    rest = rest[aliases:]
    low_refs, rest = (rest[:2], rest[2:]) if last else (None, rest)
    o_ref, stat_ref, own_ref, p_ref, keys, values = rest
    chunk = pl.program_id(1)
    rows = qa_ref.shape[1]
    span = keys.shape[0]
    *valid, start = counts_of(info_ref, hop, rows)
    alive = valid[0] + valid[1] > 0

    def finish(out, sums, top):
        own_ref[0] = jnp.broadcast_to(top, (8, rows))
        if not first:
            old_sums, old_top = prev[1][0, 0:1], prev[1][0, 1:2]
            new_top = jnp.maximum(top, old_top)
            scale, old_scale = jnp.exp2(top - new_top), jnp.exp2(old_top - new_top)
            out = out * scale + prev[0][...] * old_scale
            sums = sums * scale + old_sums * old_scale
            top = new_top
        stat_ref[0] = jnp.concatenate([sums, top, jnp.zeros((6, rows), f32)], 0)
        if last:
            out = out / sums
            for which, low_ref in enumerate(low_refs):

                @pl.when(chunk == which)
                def _():
                    low_ref[...] = out.astype(bf16)

        o_ref[...] = out

    @pl.when(jnp.logical_and(alive, chunk == 0))
    def _():
        pos = lax.broadcasted_iota(jnp.int32, (HEAD_DIM, rows), 1)
        row = lax.broadcasted_iota(jnp.int32, (HEAD_DIM, rows), 0)
        for part, (k_ref, v_ref) in enumerate(((ka_ref, va_ref), (kb_ref, vb_ref))):
            mask = jnp.where(pos < valid[part], 0.0, LOW)
            extra = jnp.where(row < 3, 1.0, jnp.where(row == 3, mask, 0.0)).astype(bf16)
            keys[pl.ds(part * rows, rows), :] = jnp.concatenate([k_ref[...], extra], 0).T
            values[:, pl.ds(part * rows, rows)] = v_ref[...]

    @pl.when(jnp.logical_not(alive))
    def _():
        finish(jnp.zeros((HEAD_DIM, rows), f32), jnp.zeros((1, rows), f32), jnp.full((1, rows), LOW, f32))

    @pl.when(alive)
    def _():
        query = jnp.where(chunk == 0, qa_ref[...], qb_ref[...])
        row = lax.broadcasted_iota(jnp.int32, (HEAD_DIM, rows), 0)
        head_blk = 64

        def extend(top):
            one, two, three = [jnp.broadcast_to(-x.astype(f32), (HEAD_DIM, rows)) for x in split_three(top)]
            extra = jnp.where(row == 0, one, jnp.where(row == 1, two, jnp.where(row == 2, three, jnp.where(row == 3, 1.0, 0.0))))
            return jnp.concatenate([query, extra.astype(bf16)], 0)

        plain = extend(jnp.zeros((1, rows), f32))
        guess = jnp.max(dot(keys[pl.ds(pl.multiple_of(start, head_blk), head_blk), :], plain, 1, 0), axis=0, keepdims=True)

        def run(top, unroll):
            query_ext = extend(top)

            def body(step, carry):
                total, sums = carry
                off = step * blk if isinstance(step, int) else pl.multiple_of(step * blk, blk)
                wide = jnp.exp2(dot(keys[pl.ds(off, blk), :], query_ext, 1, 0))
                probs = wide.astype(bf16)
                p_ref[0, 0, pl.ds(off, blk), :] = probs
                sums = sums + jnp.sum(wide.reshape(blk // 8, 8, rows), axis=0)
                return total + dot(values[:, pl.ds(off, blk)], probs, 1, 0), sums

            carry = jnp.zeros((HEAD_DIM, rows), f32), jnp.zeros((8, rows), f32)
            if unroll:
                for step in range(span // blk):
                    carry = body(step, carry)
            else:
                carry = lax.fori_loop(0, span // blk, body, carry)
            sums = jnp.sum(carry[1], axis=0, keepdims=True)
            finish(carry[0], sums, top)
            return jnp.max(sums)

        largest = run(guess, True)

        @pl.when(jnp.logical_not(largest < TOP))
        def _():
            def wider(step, top):
                off = pl.multiple_of(step * head_blk, head_blk)
                return jnp.maximum(top, jnp.max(dot(keys[pl.ds(off, head_blk), :], plain, 1, 0), axis=0, keepdims=True))

            run(lax.fori_loop(0, span // head_blk, wider, jnp.full((1, rows), LOW, f32)), False)


def head_rows(base, step, rows):
    return pl.BlockSpec((HEAD_DIM, rows), lambda h, i, n: (base + step * h, 0))


def attend(info, hop, query_a, query_b, key_a, key_b, kv_base, first_head, heads, prev, low, last):
    rows = query_a.shape[1]
    span = 2 * rows
    blk = min(512, rows)
    keys, vals, ask = head_rows(kv_base, 2, rows), head_rows(kv_base + 1, 2, rows), head_rows(first_head, 1, rows)
    out_spec = pl.BlockSpec((HEAD_DIM, rows), lambda h, i, n: (first_head + h, i))
    stat_spec = pl.BlockSpec((1, 8, rows), lambda h, i, n: (first_head + h, 0, i))
    all_heads = HEADS // 2
    extra_in = [out_spec, stat_spec] if prev else []
    extra_args = list(prev) if prev else []
    if low is not None:
        extra_in, extra_args = extra_in + [pl.BlockSpec(memory_space=pl.ANY)] * 2, extra_args + list(low)
    out_specs = [out_spec, stat_spec, pl.BlockSpec((1, 8, rows), lambda h, i, n: (h, 0, i)), pl.BlockSpec((1, 1, span, rows), lambda h, i, n: (h, i, 0, 0))]
    out_shape = [
        jax.ShapeDtypeStruct((all_heads * HEAD_DIM, span), f32),
        jax.ShapeDtypeStruct((all_heads, 8, span), f32),
        jax.ShapeDtypeStruct((heads, 8, span), f32),
        jax.ShapeDtypeStruct((heads, 2, span, rows), bf16),
    ]
    shift = 2 if last else 0
    if last:
        out_specs = [head_rows(first_head, 1, rows)] * 2 + out_specs
        out_shape = [jax.ShapeDtypeStruct((all_heads * HEAD_DIM, rows), bf16)] * 2 + out_shape
    alias = {7: shift, 8: shift + 1} if prev else {}
    if low is not None:
        alias = {**alias, 9: 0, 10: 1}
    return pl.pallas_call(
        functools.partial(forward_kernel, blk=blk, hop=hop, first=not prev, last=last, aliases=0 if low is None else 2),
        grid_spec=pltpu.PrefetchScalarGridSpec(
            num_scalar_prefetch=1,
            grid=(heads, 2),
            in_specs=[ask, ask, keys, keys, vals, vals] + extra_in,
            out_specs=out_specs,
            scratch_shapes=[pltpu.VMEM((span, 2 * HEAD_DIM), bf16), pltpu.VMEM((HEAD_DIM, span), bf16)],
        ),
        out_shape=out_shape,
        input_output_aliases=alias,
        cost_estimate=pl.CostEstimate(
            flops=16 * heads * span * span * HEAD_DIM, bytes_accessed=2 * heads * span * span, transcendentals=heads * span * span
        ),
        name="attend",
    )(info, query_a, query_b, key_a, key_b, key_a, key_b, *extra_args)


def backward_kernel(
    info_ref, qa_ref, qb_ref, ka_ref, kb_ref, va_ref, vb_ref, ga_ref, gb_ref, o_ref, stat_ref, own_ref, p_ref,
    *rest, blk, hop, adds, aliases, last,
):
    before_ref, rest = (rest[0], rest[1:]) if adds else (None, rest)
    rest = rest[aliases:]
    dq_refs, (*dkv_refs, values, dk_sum, dv_sum) = (rest[:2], rest[2:]) if last else (rest[:1], rest[1:])
    chunk = pl.program_id(1)
    rows = qa_ref.shape[1]
    span = values.shape[0]
    valid_a, valid_b, _ = counts_of(info_ref, hop, rows)
    alive = valid_a + valid_b > 0
    row = lax.broadcasted_iota(jnp.int32, (HEAD_DIM, rows), 0)

    def finish(dq):
        if adds:
            dq = dq + before_ref[...]
        if not last:
            dq_refs[0][...] = dq
            return
        for which, dq_ref in enumerate(dq_refs):

            @pl.when(chunk == which)
            def _():
                dq_ref[...] = (dq * HEAD_DIM**-0.5).astype(bf16)

    @pl.when(chunk == 0)
    def _():
        extra = jnp.where(row < 3, 1.0, 0.0).astype(bf16)
        for part, v_ref in enumerate((va_ref, vb_ref)):
            values[pl.ds(part * rows, rows), :] = jnp.concatenate([v_ref[...], extra], 0).T
        dk_sum[...] = jnp.zeros_like(dk_sum)
        dv_sum[...] = jnp.zeros_like(dv_sum)

    @pl.when(jnp.logical_not(alive))
    def _():
        finish(jnp.zeros((HEAD_DIM, rows), f32))

    @pl.when(alive)
    def _():
        query = jnp.where(chunk == 0, qa_ref[...], qb_ref[...])
        grad = jnp.where(chunk == 0, ga_ref[...], gb_ref[...])
        factor = jnp.exp2(own_ref[0, 0:1] - stat_ref[0, 1:2]) / stat_ref[0, 0:1]
        grad = (grad.astype(f32) * factor).astype(bf16)
        delta = jnp.sum(grad.astype(f32) * o_ref[...], axis=0, keepdims=True)
        one, two, three = [jnp.broadcast_to(-x.astype(f32), (HEAD_DIM, rows)) for x in split_three(delta)]
        extra = jnp.where(row == 0, one, jnp.where(row == 1, two, jnp.where(row == 2, three, 0.0))).astype(bf16)
        grad_ext = jnp.concatenate([grad, extra], 0)
        dq = jnp.zeros((HEAD_DIM, rows), f32)
        for step in range(span // blk):
            off = step * blk
            probs = p_ref[0, 0, pl.ds(off, blk), :]
            grad_scores = (probs.astype(f32) * dot(values[pl.ds(off, blk), :], grad_ext, 1, 0)).astype(bf16)
            k_ref = (ka_ref, kb_ref)[off // rows]
            dq = dq + dot(k_ref[:, pl.ds(off % rows, blk)], grad_scores, 1, 0)
            dv_sum[:, pl.ds(off, blk)] += dot(grad, probs, 1, 1)
            dk_sum[:, pl.ds(off, blk)] += dot(query, grad_scores, 1, 1)
        finish(dq)

    @pl.when(chunk == pl.num_programs(1) - 1)
    def _():
        for which, dkv_ref in enumerate(dkv_refs):
            dkv_ref[0:HEAD_DIM] = (dk_sum[:, which * rows : (which + 1) * rows] * LN2).astype(bf16)
            dkv_ref[HEAD_DIM:] = dv_sum[:, which * rows : (which + 1) * rows].astype(bf16)


def attend_back(info, hop, query_a, query_b, key_a, key_b, kv_base, p_base, first_head, heads, grad_a, grad_b, attended, stat, own, probs, before, last):
    rows = query_a.shape[1]
    span = 2 * rows
    blk = min(512, rows)
    keys, vals, ask = head_rows(kv_base, 2, rows), head_rows(kv_base + 1, 2, rows), head_rows(first_head, 1, rows)
    part = pl.BlockSpec((HEAD_DIM, rows), lambda h, i, n: (first_head + h, i))
    buffer, adds = before
    alias, extra_in, extra_args = {}, [], []
    if adds:
        extra_in, extra_args = [part], [buffer]
        alias = {} if last else {13: 0}
    elif buffer is not None:
        extra_in, extra_args, alias = [pl.BlockSpec(memory_space=pl.ANY)], [buffer], {13: 0}
    return pl.pallas_call(
        functools.partial(backward_kernel, blk=blk, adds=adds, hop=hop, aliases=len(extra_in) - int(adds), last=last),
        grid_spec=pltpu.PrefetchScalarGridSpec(
            num_scalar_prefetch=1,
            grid=(heads, 2),
            in_specs=[
                ask, ask, keys, keys, vals, vals, ask, ask,
                part,
                pl.BlockSpec((1, 8, rows), lambda h, i, n: (first_head + h, 0, i)),
                pl.BlockSpec((1, 8, rows), lambda h, i, n: (p_base + h, 0, i)),
                pl.BlockSpec((1, 1, span, rows), lambda h, i, n: (p_base + h, i, 0, 0)),
            ] + extra_in,
            out_specs=([head_rows(0, 1, rows)] * 2 if last else [part]) + [pl.BlockSpec((2 * HEAD_DIM, rows), lambda h, i, n: (h, 0))] * 2,
            scratch_shapes=[
                pltpu.VMEM((span, 2 * HEAD_DIM), bf16),
                pltpu.VMEM((HEAD_DIM, span), f32),
                pltpu.VMEM((HEAD_DIM, span), f32),
            ],
        ),
        out_shape=[
            *([jax.ShapeDtypeStruct((heads * HEAD_DIM, rows), bf16)] * 2 if last else [jax.ShapeDtypeStruct((HEADS // 2 * HEAD_DIM, span), f32)]),
            *[jax.ShapeDtypeStruct((heads * 2 * HEAD_DIM, rows), bf16)] * 2,
        ],
        input_output_aliases=alias,
        cost_estimate=pl.CostEstimate(
            flops=32 * heads * span * span * HEAD_DIM, bytes_accessed=2 * heads * span * span, transcendentals=0
        ),
        name="attend_back",
    )(info, query_a, query_b, key_a, key_b, key_a, key_b, grad_a, grad_b, attended, stat, own, probs, *extra_args)


def middle_kernel(
    info_ref, mine_ref, theirs_ref, hidden_ref, cot_ref, w_ref, vec_ref,
    out_ref, grad_mid_ref, grad_mine_ref, grad_theirs_ref, packed_ref, sums_ref,
    total, act_s, slope_s, *, ff,
):
    step = pl.program_id(0)
    rows, width = hidden_ref.shape
    dp = w_ref.shape[0]
    shard = width // dp
    down_at, up_at = shard, shard + ff // dp
    own, other = info_ref[0], 1 - info_ref[0]
    halves = lambda which: (pl.ds(which * (dp // 2), dp // 2), pl.ds(0, shard), slice(None))
    down_rows = lambda j: (pl.ds(j * dp * width // ff, dp * width // ff), pl.ds(down_at, ff // dp), slice(None))
    up_rows = lambda j: (slice(None), pl.ds(up_at + j * shard, shard), slice(None))
    half = mine_ref.shape[0]
    blocks = ff // width

    @pl.when(step == 0)
    def _():
        total[...] = jnp.zeros_like(total)
        sums_ref[...] = jnp.zeros_like(sums_ref)

    w_mine = w_ref[halves(own)].reshape(half, width)
    w_theirs = w_ref[halves(other)].reshape(half, width)
    middle = hidden_ref[...].astype(f32) + dot(mine_ref[...], w_mine, 0, 0) + dot(theirs_ref[...], w_theirs, 0, 0) + vec_ref[0:1, 0:width]
    gain, shift, bias_down = [vec_ref[0:1, k * width : (k + 1) * width] for k in (1, 2, 3)]
    hat, scale = norm_parts(middle)
    normed = (hat * gain + shift).astype(bf16)
    out = middle + bias_down
    for j in range(blocks):
        cols = slice(j * width, (j + 1) * width)
        activated, slope = gelu_and_slope(dot(normed, w_ref[up_rows(j)].reshape(width, width), 1, 0) + vec_ref[1:2, cols])
        activated = activated.astype(bf16)
        act_s[:, cols] = activated
        slope_s[:, cols] = slope
        out = out + dot(activated, w_ref[down_rows(j)].reshape(width, width), 1, 0)
    out_ref[...] = out.astype(bf16)

    pos = step * rows + lax.broadcasted_iota(jnp.int32, (rows, width), 0)
    grad_z = jnp.where(pos < info_ref[1], cot_ref[...], jnp.zeros_like(cot_ref))
    grad_norm = jnp.zeros((rows, width), f32)
    for j in range(blocks):
        cols = slice(j * width, (j + 1) * width)
        grad_act = dot(grad_z, w_ref[down_rows(j)].reshape(width, width), 1, 1) * slope_s[:, cols]
        sums_ref[0:1, cols] += jnp.sum(grad_act, axis=0, keepdims=True)
        grad_pre = grad_act.astype(bf16)
        total[down_rows(j)] += dot(act_s[:, cols], grad_z, 0, 0).reshape(dp * width // ff, ff // dp, width)
        total[up_rows(j)] += dot(normed, grad_pre, 0, 0).reshape(dp, shard, width)
        grad_norm = grad_norm + dot(grad_pre, w_ref[up_rows(j)].reshape(width, width), 1, 1)
    grad_out = grad_z.astype(f32)
    grad_mid = grad_out + norm_back(grad_norm, hat, scale, gain)
    grad_mid_ref[...] = grad_mid
    branch = grad_mid.astype(bf16)
    for k, value in enumerate((branch.astype(f32), grad_norm * hat, grad_norm, grad_out)):
        sums_ref[1:2, k * width : (k + 1) * width] += jnp.sum(value, axis=0, keepdims=True)
    grad_mine_ref[...] = dot(w_mine, branch, 1, 1).astype(bf16)
    grad_theirs_ref[...] = dot(w_theirs, branch, 1, 1).astype(bf16)
    total[halves(own)] += dot(mine_ref[...], branch, 1, 0).reshape(dp // 2, shard, width)
    total[halves(other)] += dot(theirs_ref[...], branch, 1, 0).reshape(dp // 2, shard, width)

    @pl.when(step == pl.num_programs(0) - 1)
    def _():
        packed_ref[:, 0 : total.shape[1]] = total[...].astype(bf16)


def middle_part(info, mine, theirs, hidden, cot, weights, vectors, ff):
    half = mine.shape[0]
    rows, width = hidden.shape
    blk = min(256, rows)
    packed = weights.shape
    tall = pl.BlockSpec((blk, width), lambda i, n: (i, 0))
    wide = pl.BlockSpec((half, blk), lambda i, n: (0, i))
    fixed = lambda shape: pl.BlockSpec(shape, lambda i, n: (0,) * len(shape))
    return pl.pallas_call(
        functools.partial(middle_kernel, ff=ff),
        grid_spec=pltpu.PrefetchScalarGridSpec(
            num_scalar_prefetch=1,
            grid=(rows // blk,),
            in_specs=[wide, wide, tall, tall, fixed(packed), fixed(vectors.shape)],
            out_specs=[tall, tall, wide, wide, fixed(packed), fixed((8, ff))],
            scratch_shapes=[pltpu.VMEM((packed[0], packed[1] - 16, width), f32), pltpu.VMEM((blk, ff), bf16), pltpu.VMEM((blk, ff), f32)],
        ),
        out_shape=[
            jax.ShapeDtypeStruct((rows, width), bf16),
            jax.ShapeDtypeStruct((rows, width), f32),
            jax.ShapeDtypeStruct((half, rows), bf16),
            jax.ShapeDtypeStruct((half, rows), bf16),
            jax.ShapeDtypeStruct(packed, bf16),
            jax.ShapeDtypeStruct((8, ff), f32),
        ],
        cost_estimate=pl.CostEstimate(flops=12 * rows * width * (2 * ff + width) // 2, bytes_accessed=16 << 20, transcendentals=rows * ff),
        name="middle",
    )(info, mine, theirs, hidden, cot, weights, vectors)


def pack_kernel(out_ref, down_ref, up_ref, row_ref, packed_ref):
    shard, width = out_ref.shape
    at = shard + down_ref.shape[0]
    packed_ref[0:shard] = out_ref[...]
    packed_ref[shard:at] = down_ref[...]
    for j in range(up_ref.shape[1] // width):
        packed_ref[at + j * shard : at + (j + 1) * shard] = up_ref[:, j * width : (j + 1) * width]
    end = at + up_ref.shape[1] // width * shard
    packed_ref[end:] = jnp.broadcast_to(row_ref[...], (packed_ref.shape[0] - end, width))


def pack_part(out_weight, down_weight, up_weight, row):
    shard, width = out_weight.shape
    total = shard + down_weight.shape[0] + up_weight.shape[1] // width * shard + 16
    return pl.pallas_call(pack_kernel, out_shape=jax.ShapeDtypeStruct((total, width), bf16), name="pack")(out_weight, down_weight, up_weight, row)


def shape_kernel(info_ref, w_ref, small_ref, out_ref):
    part = w_ref.shape[0] // 2
    heads = HEADS // 2
    half = heads * HEAD_DIM
    block = w_ref[pl.ds(pl.multiple_of(info_ref[0] * part, part), part)]
    for which in range(2):
        cols = [block[:, which * half : (which + 1) * half]]
        for head in range(heads):
            for kind in (1, 2):
                at = (2 * kind + which) * half + head * HEAD_DIM
                cols.append(block[:, at : at + HEAD_DIM])
        out_ref[which * part : (which + 1) * part] = jnp.concatenate(cols, 1)
    out_ref[2 * part :] = jnp.broadcast_to(small_ref[...], (8, 3 * half))


def shape_part(info, weight, small):
    shard, cols = weight.shape
    full = pl.BlockSpec(memory_space=pltpu.VMEM)
    return pl.pallas_call(
        shape_kernel,
        in_specs=[pl.BlockSpec(memory_space=pltpu.SMEM), full, full],
        out_specs=full,
        out_shape=jax.ShapeDtypeStruct((shard + 8, cols // 2), bf16),
        name="shape",
    )(info, weight, small)


def place_kernel(info_ref, *refs, lows):
    own, other, out_ref, small_ref = refs[:lows], refs[lows : 2 * lows], refs[2 * lows], refs[2 * lows + 1]
    part, cols = out_ref.shape[3:]
    for j in range(lows):
        for k in range(own[j].shape[0]):
            at = info_ref[4] ^ (k * lows + j)
            out_ref[:, pl.ds(at, 1), pl.ds(info_ref[0], 1)] = own[j][k, 0 : 2 * part].reshape(2, part, cols)[:, None, None]
            out_ref[:, pl.ds(at, 1), pl.ds(1 - info_ref[0], 1)] = other[j][k, 0 : 2 * part].reshape(2, part, cols)[:, None, None]
            small_ref[pl.ds(at, 1)] = own[j][k, 2 * part :][None]


def place_part(info, own, other):
    count, rows, cols = own[0].shape
    full = pl.BlockSpec(memory_space=pltpu.VMEM)
    return pl.pallas_call(
        functools.partial(place_kernel, lows=len(own)),
        in_specs=[pl.BlockSpec(memory_space=pltpu.SMEM)] + [full] * (2 * len(own)),
        out_specs=[full, full],
        out_shape=[
            jax.ShapeDtypeStruct((2, count * len(own), 2, rows // 2 - 4, cols), bf16),
            jax.ShapeDtypeStruct((count * len(own), 8, cols), bf16),
        ],
        name="place",
    )(info, *own, *other)


def finish_kernel(info_ref, hidden_ref, mid_ref, w_ref, vec_ref, *refs, groups):
    many_groups = len(groups)
    parts, (mine_ref, theirs_ref, bias_ref, out_ref, sums_ref, total, grads) = refs[: 6 * many_groups], refs[6 * many_groups :]
    step = pl.program_id(0)
    rows, width = hidden_ref.shape
    half = width // 2

    @pl.when(step == 0)
    def _():
        total[...] = jnp.zeros_like(total)
        sums_ref[...] = jnp.zeros_like(sums_ref)

    ones = jnp.where(lax.broadcasted_iota(jnp.int32, (16, rows), 0) == 0, 1.0, 0.0).astype(bf16)
    hat, scale = norm_parts(hidden_ref[...].astype(f32))
    gain, shift = vec_ref[0:1], vec_ref[1:2]
    left = jnp.concatenate([(hat * gain + shift).astype(bf16).T, ones], 0)
    grad_norm = jnp.zeros((width, rows), f32)
    for which in range(2):
        dqs, dkvs, far = [parts[(3 * which + n) * many_groups : (3 * which + n + 1) * many_groups] for n in range(3)]
        for (at, many), dq_ref, dkv_ref, far_ref in zip(groups, dqs, dkvs, far):
            grads[which, at * HEAD_DIM : (at + many) * HEAD_DIM] = dq_ref[...]
            where = slice(half + at * 2 * HEAD_DIM, half + (at + many) * 2 * HEAD_DIM)
            grads[which, where] = (dkv_ref[...].astype(f32) + far_ref[...].astype(f32)).astype(bf16)
        total[which] += dot(left, grads[which], 1, 1)
        weights = w_ref[pl.ds(info_ref[0] ^ which, 1)].reshape(width, 3 * half)
        grad_norm = grad_norm + dot(weights, grads[which], 1, 0)
    grad_norm = grad_norm.T
    sums_ref[0:1] += jnp.sum(grad_norm * hat, axis=0, keepdims=True)
    sums_ref[1:2] += jnp.sum(grad_norm, axis=0, keepdims=True)
    out_ref[...] = (mid_ref[...] + norm_back(grad_norm, hat, scale, gain)).astype(bf16)

    @pl.when(step == pl.num_programs(0) - 1)
    def _():
        mine_ref[...] = total[0, 0:width].astype(bf16)
        theirs_ref[...] = total[1, 0:width].astype(bf16)
        for which in range(2):
            bias_ref[which] = jnp.broadcast_to(total[which, width : width + 1], bias_ref.shape[1:])


def finish_part(info, hidden, grad_mid, weights, vectors, mine, theirs, groups):
    rows, width = hidden.shape
    cols = 3 * width // 2
    blk = min(512, rows)
    wide = lambda n: pl.BlockSpec((n, blk), lambda i, n_: (0, i))
    tall = pl.BlockSpec((blk, width), lambda i, n: (i, 0))
    fixed = lambda shape: pl.BlockSpec(shape, lambda i, n: (0,) * len(shape))
    parts = [x for side in (mine, theirs) for kind in side for x in kind]
    return pl.pallas_call(
        functools.partial(finish_kernel, groups=groups),
        grid_spec=pltpu.PrefetchScalarGridSpec(
            num_scalar_prefetch=1,
            grid=(rows // blk,),
            in_specs=[tall, tall, fixed(weights.shape), fixed(vectors.shape)] + [wide(x.shape[0]) for x in parts],
            out_specs=[fixed((width, cols)), fixed((width, cols)), fixed((2, 8, cols)), tall, fixed((8, width))],
            scratch_shapes=[pltpu.VMEM((2, width + 16, cols), f32), pltpu.VMEM((2, cols, blk), bf16)],
        ),
        out_shape=[
            jax.ShapeDtypeStruct((width, cols), bf16),
            jax.ShapeDtypeStruct((width, cols), bf16),
            jax.ShapeDtypeStruct((2, 8, cols), f32),
            jax.ShapeDtypeStruct((rows, width), bf16),
            jax.ShapeDtypeStruct((8, width), f32),
        ],
        cost_estimate=pl.CostEstimate(flops=8 * rows * width * cols, bytes_accessed=16 << 20, transcendentals=rows),
        name="finish",
    )(info, hidden, grad_mid, weights, vectors, *parts)


def join_kernel(info_ref, held_ref, got_ref, out_ref, small_ref):
    shard = out_ref.shape[0]
    heads = HEADS // 2
    half = heads * HEAD_DIM
    held, got = held_ref[...].astype(f32), got_ref[...].astype(f32)
    for which in range(2):
        block = jnp.where(info_ref[0] == which, got[:shard], held[:shard])
        out_ref[:, which * half : (which + 1) * half] = block[:, :half]
        for kind in (1, 2):
            at = (2 * kind + which) * half
            starts = [half + (2 * head + kind - 1) * HEAD_DIM for head in range(heads)]
            out_ref[:, at : at + half] = jnp.concatenate([block[:, start : start + HEAD_DIM] for start in starts], 1)
    small_ref[...] = held[shard:] + got[shard:]


def join_part(info, held, got):
    rows, cols = held.shape
    full = pl.BlockSpec(memory_space=pltpu.VMEM)
    return pl.pallas_call(
        join_kernel,
        in_specs=[pl.BlockSpec(memory_space=pltpu.SMEM), full, full],
        out_specs=[full, full],
        out_shape=[jax.ShapeDtypeStruct((rows - 8, 2 * cols), f32), jax.ShapeDtypeStruct((8, cols), f32)],
        name="join",
    )(info, held, got)


def swap(values, axis, flip):
    size = lax.axis_size(axis)
    return lax.ppermute(values, axis, [(i, i ^ flip) for i in range(size)])


def gelu_and_slope(u):
    a = 0.7978845608028654
    inner = a * (u + 0.044715 * u * u * u)
    t = jnp.tanh(inner)
    slope = 0.5 * (1 + t) + 0.5 * u * (1 - t * t) * a * (1 + 3 * 0.044715 * u * u)
    return 0.5 * u * (1 + t), slope


def norm_parts(inputs):
    center = inputs - jnp.mean(inputs, axis=-1, keepdims=True)
    scale = lax.rsqrt(jnp.mean(center * center, axis=-1, keepdims=True) + EPS)
    return center * scale, scale


def norm_back(grad, hat, scale, gain):
    e = grad * gain
    return scale * (e - jnp.mean(e, axis=-1, keepdims=True) - hat * jnp.mean(e * hat, axis=-1, keepdims=True))


def tie(*values):
    return lax.optimization_barrier(values)


def on_device(
    hidden_in, seq_lengths, out_cotangent, norm1_gain, norm1_shift, qkv_weight, qv_bias, out_weight, out_bias,
    norm2_gain, norm2_shift, up_weight, up_bias, down_weight, down_bias,
):
    rows, width = hidden_in.shape[1:]
    hidden_in, out_cotangent = hidden_in[0], out_cotangent[0]
    ff = up_weight.shape[1]
    dp, ctx = lax.axis_size("dp"), lax.axis_size("ctx")
    dp_low = 2 if dp == 8 else 4
    dp_high, high_at = dp // dp_low, dp_low.bit_length() - 1
    ring = ctx // 2
    me = lax.axis_index("ctx")
    core = me % 2
    heads = HEADS // 2
    half = heads * HEAD_DIM
    shard = width // dp
    length = seq_lengths[0]
    info = jnp.stack([core, jnp.clip(length - me * rows, 0, rows), length, me, lax.axis_index("dp")]).astype(jnp.int32)

    def by_core(cols):
        lead = cols.shape[:-1]
        cols = cols.reshape(lead + (3, 2, heads, HEAD_DIM))
        asks = cols[..., 0, :, :, :].reshape(lead + (2, half))
        pairs = jnp.moveaxis(cols[..., 1:, :, :, :], -4, -2).reshape(lead + (2, 2 * half))
        return jnp.concatenate([asks, pairs], -1)

    def from_core(cols):
        lead = cols.shape[:-2]
        asks = cols[..., :half].reshape(lead + (1, 2, heads, HEAD_DIM))
        pairs = jnp.moveaxis(cols[..., half:].reshape(lead + (2, heads, 2, HEAD_DIM)), -2, -4)
        return jnp.concatenate([asks, pairs], -4).reshape(lead + (6 * half,))

    high_stage = lambda x: [swap(x, "dp", k << high_at) for k in range(1, dp_high)]
    low_stage = lambda x: [swap(x, "dp", j) for j in range(1, dp_low)]

    early = jnp.concatenate([norm1_gain, norm1_shift, qv_bias[0], qv_bias[1]])
    early = jnp.pad(early, (0, 3 * half - early.shape[0]))[None]
    piece = shape_part(info, qkv_weight, early)
    pieces = [piece] + high_stage(piece)
    late = jnp.concatenate([out_bias, norm2_gain, norm2_shift, down_bias, up_bias])
    late = jnp.pad(late, (0, width - late.shape[0]))[None]
    others = pack_part(out_weight, down_weight, up_weight, late)
    others, pieces = tie(others, pieces)
    others = lax.all_gather(others, "dp", axis=0, tiled=False)
    stack = jnp.stack(pieces)
    own = [stack] + low_stage(stack)
    other = [swap(x, "ctx", 1) for x in own]
    w_qkv, early = place_part(info, own, other)
    w_qkv = w_qkv.reshape(2, width, 3 * half)
    early = early[:, 0, : 4 * shard].reshape(dp, 4, shard).swapaxes(0, 1).reshape(4, width).astype(f32)
    gain_one, shift_one, bias_q, bias_v = early

    hat_one, _ = norm_parts(hidden_in.astype(f32))
    normed_one = (hat_one * gain_one + shift_one).astype(bf16)
    bias_full = by_core(jnp.concatenate([bias_q, jnp.zeros_like(bias_q), bias_v]))
    factors = jnp.where(jnp.arange(3 * half) < half, LOG2E * HEAD_DIM**-0.5, 1.0)

    def projected(which):
        pick = lambda x: lax.dynamic_index_in_dim(x, which, 0, keepdims=False)
        return ((dot(pick(w_qkv), normed_one, 0, 1) + pick(bias_full)[:, None]) * factors[:, None]).astype(bf16)

    foreign = projected(1 - core)
    mine = projected(core)
    theirs = swap(foreign, "ctx", 1)

    groups = [(0, 2), (2, 2)] if ring == 2 else [(0, heads)]
    far = []
    for k in range(1, ring):
        for at, many in groups:
            cut = slice(half + at * 2 * HEAD_DIM, half + (at + many) * 2 * HEAD_DIM)
            far.append((k, at, many, swap(mine[cut], "ctx", 2 * k), swap(foreign[cut], "ctx", 2 * k + 1)))
    *sums, own_top, probs = attend(info, 0, mine, theirs, mine, theirs, heads, 0, heads, None, None, ring == 1)
    near = (own_top, probs)
    saved, low = [], None
    for k, at, many, key_a, key_b in far:
        last = k == ring - 1
        out = attend(info, k, mine, theirs, key_a, key_b, 0, at, many, sums, low if last else None, last)
        if last:
            low, out = out[:2], out[2:]
        sums, own_top, probs = out[:2], out[2], out[3]
        saved.append((own_top, probs))
    attended, stat = sums
    low_theirs = swap(low[1], "ctx", 1)

    rest = others[:, -16].astype(f32)
    vector = lambda at: rest[:, at * shard : (at + 1) * shard].reshape(width)
    second_rows = jnp.pad(
        jnp.stack([jnp.concatenate([vector(0), vector(1), vector(2), vector(3)]), rest[:, 4 * shard : 4 * shard + ff // dp].reshape(ff)]), ((0, 6), (0, 0))
    )
    hidden_out, grad_mid, grad_mine, grad_theirs, packed, sums_two = middle_part(
        info, low[0], low_theirs, hidden_in, out_cotangent, others, second_rows, ff
    )
    grad_theirs = swap(grad_theirs, "ctx", 1)

    spread = lambda x: x.reshape(-1, dp, x.shape[-1] // dp).swapaxes(0, 1).reshape(dp, -1)
    late = jnp.concatenate([spread(sums_two[1].reshape(4, width)), spread(sums_two[0].reshape(1, ff))], 1)
    late = jnp.pad(late, ((0, 0), (0, width - late.shape[1])))[:, None].astype(bf16)
    packed = lax.dynamic_update_slice(packed, jnp.broadcast_to(late, (dp, 16, width)), (0, packed.shape[1] - 16, 0))
    packed = lax.psum_scatter(packed, "dp", scatter_dimension=0, tiled=False)

    buffer, flying, back_mine, back_theirs = None, [], {}, {}
    shared = (grad_mine, grad_theirs, attended, stat)
    calls = [(k, at, many, key_a, key_b, 0, 0, kept) for (k, at, many, key_a, key_b), kept in zip(far, saved)]
    calls = calls + [(0, at, many, mine, theirs, heads + 2 * at, at, near) for at, many in groups]
    ends = []
    for n, (k, at, many, key_a, key_b, kv_base, p_base, kept) in enumerate(calls):
        call_info = info
        if ends:
            call_info, kept_back = tie(info, ends[-1][2])
            ends[-1] = ends[-1][:2] + (kept_back,) + ends[-1][3:]
        if n > 1 and flying:
            call_info, (got_mine, got_theirs), where = *tie(call_info, flying[0][:2]), flying.pop(0)[2]
            back_mine.setdefault(where, []).append(got_mine)
            back_theirs.setdefault(where, []).append(got_theirs)
        outs = attend_back(call_info, k, mine, theirs, key_a, key_b, kv_base, p_base, at, many, *shared, *kept, (buffer, k == 0 or k > 1), k == 0)
        if k:
            buffer = outs[0]
            flying.append((swap(outs[1], "ctx", 2 * k), swap(outs[2], "ctx", 2 * k + 1), at))
        else:
            dq_a, dq_b, dkv_a, dkv_b = outs
            ends.append((dq_a, swap(dq_b, "ctx", 1), dkv_a, swap(dkv_b, "ctx", 1)))
    for got_mine, got_theirs, where in flying:
        back_mine.setdefault(where, []).append(got_mine)
        back_theirs.setdefault(where, []).append(got_theirs)
    dqs_mine, dqs_theirs, dkvs_mine, dkvs_theirs = zip(*ends)
    sum_far = lambda parts: [functools.reduce(lambda a, b: (a.astype(f32) + b.astype(f32)).astype(bf16), parts[at]) for at, _ in groups]

    sides = [(dqs_mine, dkvs_mine, sum_far(back_mine)), (dqs_theirs, dkvs_theirs, sum_far(back_theirs))]
    dw_out, dw, bias_sides, grad_hidden, sums_one = finish_part(info, hidden_in, grad_mid, w_qkv, early, *sides, groups)
    dw_in = swap(dw_out, "ctx", 1)

    def halves(total, axis, shift, count, dim):
        index = (lax.axis_index(axis) >> shift) & (count - 1)
        pick = lambda k: lax.dynamic_index_in_dim(total, index ^ k, dim, keepdims=False)
        return pick(0).astype(f32), [pick(k).astype(bf16) for k in range(1, count)]

    swaps = lambda parts, axis, shift: [swap(part, axis, k << shift) for k, part in enumerate(parts, 1)]
    add = lambda first, rest: functools.reduce(lambda a, b: a + b.astype(f32), rest, first.astype(f32))

    def sum_chips(total, covers=None):
        for flip in [2 << b for b in range(ring.bit_length() - 1)]:
            total = total.astype(bf16)
            got = swap(total, "ctx", flip)
            if covers is not None:
                got, _ = tie(got, covers)
            total = add(total, [got])
        return total.astype(bf16)

    bias_one = jnp.where(core == 0, bias_sides[0, 0], bias_sides[1, 0])
    bias_two = jnp.where(core == 0, bias_sides[1, 0], bias_sides[0, 0])
    bias_sums = from_core(jnp.stack([bias_one, bias_two])).reshape(3, width)
    smalls = jnp.concatenate([spread(sums_one[0:2]), spread(bias_sums[0:1]), spread(bias_sums[2:3])], 1)
    smalls = jnp.pad(smalls[:, None], ((0, 0), (0, 7), (0, 3 * half - smalls.shape[1])))
    total = jnp.concatenate([add(dw, [dw_in]).reshape(dp, shard, 3 * half), smalls], 1)
    first, sent, packed = tie(*halves(total.reshape((dp_high, dp_low) + total.shape[1:]), "dp", 0, dp_low, 1), packed)
    sent = swaps(sent, "dp", 0)
    packed_first, packed_sent = halves(packed.reshape((2, -1) + packed.shape[1:]), "ctx", 0, 2, 0)
    packed = add(packed_first, swaps(packed_sent, "ctx", 0)).astype(bf16)
    sent, _ = tie(sent, packed)
    packed = sum_chips(packed)
    first, sent = halves(add(first, sent), "dp", high_at, dp_high, 0)
    sent = swaps(sent, "dp", high_at)
    sent, _ = tie(sent, packed)
    packed_got = swap(packed, "ctx", 1)
    by_index = lambda a, b: [jnp.where(core == 0, a, b), jnp.where(core == 0, b, a)]
    packed = jnp.concatenate(by_index(packed, packed_got), 0).astype(f32)
    down_at, up_at, end = shard, shard + ff // dp, shard + 2 * (ff // dp)
    grad_up = packed[up_at:end].reshape(ff // width, shard, width).swapaxes(0, 1).reshape(shard, ff)
    grad_out_weight, grad_down, last_row = packed[:shard], packed[down_at:up_at], packed[-16]
    total = sum_chips(add(first, sent), (grad_out_weight, grad_down, grad_up, last_row))
    grad_qkv, smalls = join_part(info, total, swap(total, "ctx", 1))
    smalls = smalls[0]
    small_out = lambda at: smalls[at * shard : (at + 1) * shard]
    late_out = lambda at: last_row[at * shard : (at + 1) * shard]
    return (
        hidden_out[None],
        grad_hidden[None],
        small_out(0),
        small_out(1),
        grad_qkv,
        jnp.stack([small_out(2), small_out(3)]),
        grad_out_weight,
        late_out(0),
        late_out(1),
        late_out(2),
        grad_up,
        last_row[4 * shard : 4 * shard + ff // dp],
        grad_down,
        late_out(3),
    )


def solution(mesh):
    return jax.shard_map(
        on_device,
        mesh=mesh,
        in_specs=(
            P("dp", "ctx", None), P("dp"), P("dp", "ctx", None), P("dp"), P("dp"), P("dp", None), P(None, "dp"),
            P("dp", None), P("dp"), P("dp"), P("dp"), P("dp", None), P("dp"), P("dp", None), P("dp"),
        ),
        out_specs=(
            P("dp", "ctx", None), P("dp", "ctx", None), P("dp"), P("dp"), P("dp", None), P(None, "dp"), P("dp", None),
            P("dp"), P("dp"), P("dp"), P("dp", None), P("dp"), P("dp", None), P("dp"),
        ),
        check_vma=False,
    )
```

```python
import functools

import jax
import jax.numpy as jnp
from jax import lax
from jax.experimental import pallas as pl
from jax.experimental.pallas import tpu as pltpu
from jax.sharding import PartitionSpec as P

HEADS = 8
HEAD_DIM = 64
EPS = 1e-05
LOG2E = 1.4426950408889634
LN2 = 0.6931471805599453
LOW = -1e30
TOP = 1e30
f32 = jnp.float32
bf16 = jnp.bfloat16


def dot(left, right, left_dim, right_dim):
    return lax.dot_general(left, right, (((left_dim,), (right_dim,)), ((), ())), preferred_element_type=f32)


def split_three(values):
    one = values.astype(bf16)
    rest = values - one.astype(f32)
    two = rest.astype(bf16)
    return one, two, (rest - two.astype(f32)).astype(bf16)


def counts_of(info_ref, hop, rows):
    length, source = info_ref[2], info_ref[3] ^ (2 * hop)
    return jnp.clip(length - source * rows, 0, rows), jnp.clip(length - (source ^ 1) * rows, 0, rows), info_ref[0] * rows


def forward_kernel(info_ref, qa_ref, qb_ref, ka_ref, kb_ref, va_ref, vb_ref, *rest, blk, hop, first, last, aliases):
    prev, rest = ((None, None), rest) if first else (rest[:2], rest[2:])
    rest = rest[aliases:]
    low_refs, rest = (rest[:2], rest[2:]) if last else (None, rest)
    o_ref, stat_ref, own_ref, p_ref, keys, values = rest
    chunk = pl.program_id(1)
    rows = qa_ref.shape[1]
    span = keys.shape[0]
    *valid, start = counts_of(info_ref, hop, rows)
    alive = valid[0] + valid[1] > 0

    def finish(out, sums, top):
        own_ref[0] = jnp.broadcast_to(top, (8, rows))
        if not first:
            old_sums, old_top = prev[1][0, 0:1], prev[1][0, 1:2]
            new_top = jnp.maximum(top, old_top)
            scale, old_scale = jnp.exp2(top - new_top), jnp.exp2(old_top - new_top)
            out = out * scale + prev[0][...] * old_scale
            sums = sums * scale + old_sums * old_scale
            top = new_top
        stat_ref[0] = jnp.concatenate([sums, top, jnp.zeros((6, rows), f32)], 0)
        if last:
            out = out / sums
            for which, low_ref in enumerate(low_refs):

                @pl.when(chunk == which)
                def _():
                    low_ref[...] = out.astype(bf16)

        o_ref[...] = out

    @pl.when(jnp.logical_and(alive, chunk == 0))
    def _():
        pos = lax.broadcasted_iota(jnp.int32, (HEAD_DIM, rows), 1)
        row = lax.broadcasted_iota(jnp.int32, (HEAD_DIM, rows), 0)
        for part, (k_ref, v_ref) in enumerate(((ka_ref, va_ref), (kb_ref, vb_ref))):
            mask = jnp.where(pos < valid[part], 0.0, LOW)
            extra = jnp.where(row < 3, 1.0, jnp.where(row == 3, mask, 0.0)).astype(bf16)
            keys[pl.ds(part * rows, rows), :] = jnp.concatenate([k_ref[...], extra], 0).T
            values[:, pl.ds(part * rows, rows)] = v_ref[...]

    @pl.when(jnp.logical_not(alive))
    def _():
        finish(jnp.zeros((HEAD_DIM, rows), f32), jnp.zeros((1, rows), f32), jnp.full((1, rows), LOW, f32))

    @pl.when(alive)
    def _():
        query = jnp.where(chunk == 0, qa_ref[...], qb_ref[...])
        row = lax.broadcasted_iota(jnp.int32, (HEAD_DIM, rows), 0)
        head_blk = 64

        def extend(top):
            one, two, three = [jnp.broadcast_to(-x.astype(f32), (HEAD_DIM, rows)) for x in split_three(top)]
            extra = jnp.where(row == 0, one, jnp.where(row == 1, two, jnp.where(row == 2, three, jnp.where(row == 3, 1.0, 0.0))))
            return jnp.concatenate([query, extra.astype(bf16)], 0)

        plain = extend(jnp.zeros((1, rows), f32))
        guess = jnp.max(dot(keys[pl.ds(pl.multiple_of(start, head_blk), head_blk), :], plain, 1, 0), axis=0, keepdims=True)

        def run(top, unroll):
            query_ext = extend(top)

            def body(step, carry):
                total, sums = carry
                off = step * blk if isinstance(step, int) else pl.multiple_of(step * blk, blk)
                wide = jnp.exp2(dot(keys[pl.ds(off, blk), :], query_ext, 1, 0))
                probs = wide.astype(bf16)
                p_ref[0, 0, pl.ds(off, blk), :] = probs
                sums = sums + jnp.sum(wide.reshape(blk // 8, 8, rows), axis=0)
                return total + dot(values[:, pl.ds(off, blk)], probs, 1, 0), sums

            carry = jnp.zeros((HEAD_DIM, rows), f32), jnp.zeros((8, rows), f32)
            if unroll:
                for step in range(span // blk):
                    carry = body(step, carry)
            else:
                carry = lax.fori_loop(0, span // blk, body, carry)
            sums = jnp.sum(carry[1], axis=0, keepdims=True)
            finish(carry[0], sums, top)
            return jnp.max(sums)

        largest = run(guess, True)

        @pl.when(jnp.logical_not(largest < TOP))
        def _():
            def wider(step, top):
                off = pl.multiple_of(step * head_blk, head_blk)
                return jnp.maximum(top, jnp.max(dot(keys[pl.ds(off, head_blk), :], plain, 1, 0), axis=0, keepdims=True))

            run(lax.fori_loop(0, span // head_blk, wider, jnp.full((1, rows), LOW, f32)), False)


def head_rows(base, step, rows):
    return pl.BlockSpec((HEAD_DIM, rows), lambda h, i, n: (base + step * h, 0))


def attend(info, hop, query_a, query_b, key_a, key_b, kv_base, first_head, heads, prev, low, last):
    rows = query_a.shape[1]
    span = 2 * rows
    blk = min(512, rows)
    keys, vals, ask = head_rows(kv_base, 2, rows), head_rows(kv_base + 1, 2, rows), head_rows(first_head, 1, rows)
    out_spec = pl.BlockSpec((HEAD_DIM, rows), lambda h, i, n: (first_head + h, i))
    stat_spec = pl.BlockSpec((1, 8, rows), lambda h, i, n: (first_head + h, 0, i))
    all_heads = HEADS // 2
    extra_in = [out_spec, stat_spec] if prev else []
    extra_args = list(prev) if prev else []
    if low is not None:
        extra_in, extra_args = extra_in + [pl.BlockSpec(memory_space=pl.ANY)] * 2, extra_args + list(low)
    out_specs = [out_spec, stat_spec, pl.BlockSpec((1, 8, rows), lambda h, i, n: (h, 0, i)), pl.BlockSpec((1, 1, span, rows), lambda h, i, n: (h, i, 0, 0))]
    out_shape = [
        jax.ShapeDtypeStruct((all_heads * HEAD_DIM, span), f32),
        jax.ShapeDtypeStruct((all_heads, 8, span), f32),
        jax.ShapeDtypeStruct((heads, 8, span), f32),
        jax.ShapeDtypeStruct((heads, 2, span, rows), bf16),
    ]
    shift = 2 if last else 0
    if last:
        out_specs = [head_rows(first_head, 1, rows)] * 2 + out_specs
        out_shape = [jax.ShapeDtypeStruct((all_heads * HEAD_DIM, rows), bf16)] * 2 + out_shape
    alias = {7: shift, 8: shift + 1} if prev else {}
    if low is not None:
        alias = {**alias, 9: 0, 10: 1}
    return pl.pallas_call(
        functools.partial(forward_kernel, blk=blk, hop=hop, first=not prev, last=last, aliases=0 if low is None else 2),
        grid_spec=pltpu.PrefetchScalarGridSpec(
            num_scalar_prefetch=1,
            grid=(heads, 2),
            in_specs=[ask, ask, keys, keys, vals, vals] + extra_in,
            out_specs=out_specs,
            scratch_shapes=[pltpu.VMEM((span, 2 * HEAD_DIM), bf16), pltpu.VMEM((HEAD_DIM, span), bf16)],
        ),
        out_shape=out_shape,
        input_output_aliases=alias,
        cost_estimate=pl.CostEstimate(
            flops=16 * heads * span * span * HEAD_DIM, bytes_accessed=2 * heads * span * span, transcendentals=heads * span * span
        ),
        name="attend",
    )(info, query_a, query_b, key_a, key_b, key_a, key_b, *extra_args)


def backward_kernel(
    info_ref, qa_ref, qb_ref, ka_ref, kb_ref, va_ref, vb_ref, ga_ref, gb_ref, o_ref, stat_ref, own_ref, p_ref,
    *rest, blk, hop, adds, aliases, last,
):
    before_ref, rest = (rest[0], rest[1:]) if adds else (None, rest)
    rest = rest[aliases:]
    dq_refs, (*dkv_refs, values, dk_sum, dv_sum) = (rest[:2], rest[2:]) if last else (rest[:1], rest[1:])
    chunk = pl.program_id(1)
    rows = qa_ref.shape[1]
    span = values.shape[0]
    valid_a, valid_b, _ = counts_of(info_ref, hop, rows)
    alive = valid_a + valid_b > 0
    row = lax.broadcasted_iota(jnp.int32, (HEAD_DIM, rows), 0)

    def finish(dq):
        if adds:
            dq = dq + before_ref[...]
        if not last:
            dq_refs[0][...] = dq
            return
        for which, dq_ref in enumerate(dq_refs):

            @pl.when(chunk == which)
            def _():
                dq_ref[...] = (dq * HEAD_DIM**-0.5).astype(bf16)

    @pl.when(chunk == 0)
    def _():
        extra = jnp.where(row < 3, 1.0, 0.0).astype(bf16)
        for part, v_ref in enumerate((va_ref, vb_ref)):
            values[pl.ds(part * rows, rows), :] = jnp.concatenate([v_ref[...], extra], 0).T
        dk_sum[...] = jnp.zeros_like(dk_sum)
        dv_sum[...] = jnp.zeros_like(dv_sum)

    @pl.when(jnp.logical_not(alive))
    def _():
        finish(jnp.zeros((HEAD_DIM, rows), f32))

    @pl.when(alive)
    def _():
        query = jnp.where(chunk == 0, qa_ref[...], qb_ref[...])
        grad = jnp.where(chunk == 0, ga_ref[...], gb_ref[...])
        factor = jnp.exp2(own_ref[0, 0:1] - stat_ref[0, 1:2]) / stat_ref[0, 0:1]
        grad = (grad.astype(f32) * factor).astype(bf16)
        delta = jnp.sum(grad.astype(f32) * o_ref[...], axis=0, keepdims=True)
        one, two, three = [jnp.broadcast_to(-x.astype(f32), (HEAD_DIM, rows)) for x in split_three(delta)]
        extra = jnp.where(row == 0, one, jnp.where(row == 1, two, jnp.where(row == 2, three, 0.0))).astype(bf16)
        grad_ext = jnp.concatenate([grad, extra], 0)
        dq = jnp.zeros((HEAD_DIM, rows), f32)
        for step in range(span // blk):
            off = step * blk
            probs = p_ref[0, 0, pl.ds(off, blk), :]
            grad_scores = (probs.astype(f32) * dot(values[pl.ds(off, blk), :], grad_ext, 1, 0)).astype(bf16)
            k_ref = (ka_ref, kb_ref)[off // rows]
            dq = dq + dot(k_ref[:, pl.ds(off % rows, blk)], grad_scores, 1, 0)
            dv_sum[:, pl.ds(off, blk)] += dot(grad, probs, 1, 1)
            dk_sum[:, pl.ds(off, blk)] += dot(query, grad_scores, 1, 1)
        finish(dq)

    @pl.when(chunk == pl.num_programs(1) - 1)
    def _():
        for which, dkv_ref in enumerate(dkv_refs):
            dkv_ref[0:HEAD_DIM] = (dk_sum[:, which * rows : (which + 1) * rows] * LN2).astype(bf16)
            dkv_ref[HEAD_DIM:] = dv_sum[:, which * rows : (which + 1) * rows].astype(bf16)


def attend_back(info, hop, query_a, query_b, key_a, key_b, kv_base, p_base, first_head, heads, grad_a, grad_b, attended, stat, own, probs, before, last):
    rows = query_a.shape[1]
    span = 2 * rows
    blk = min(512, rows)
    keys, vals, ask = head_rows(kv_base, 2, rows), head_rows(kv_base + 1, 2, rows), head_rows(first_head, 1, rows)
    part = pl.BlockSpec((HEAD_DIM, rows), lambda h, i, n: (first_head + h, i))
    buffer, adds = before
    alias, extra_in, extra_args = {}, [], []
    if adds:
        extra_in, extra_args = [part], [buffer]
        alias = {} if last else {13: 0}
    elif buffer is not None:
        extra_in, extra_args, alias = [pl.BlockSpec(memory_space=pl.ANY)], [buffer], {13: 0}
    return pl.pallas_call(
        functools.partial(backward_kernel, blk=blk, adds=adds, hop=hop, aliases=len(extra_in) - int(adds), last=last),
        grid_spec=pltpu.PrefetchScalarGridSpec(
            num_scalar_prefetch=1,
            grid=(heads, 2),
            in_specs=[
                ask, ask, keys, keys, vals, vals, ask, ask,
                part,
                pl.BlockSpec((1, 8, rows), lambda h, i, n: (first_head + h, 0, i)),
                pl.BlockSpec((1, 8, rows), lambda h, i, n: (p_base + h, 0, i)),
                pl.BlockSpec((1, 1, span, rows), lambda h, i, n: (p_base + h, i, 0, 0)),
            ] + extra_in,
            out_specs=([head_rows(0, 1, rows)] * 2 if last else [part]) + [pl.BlockSpec((2 * HEAD_DIM, rows), lambda h, i, n: (h, 0))] * 2,
            scratch_shapes=[
                pltpu.VMEM((span, 2 * HEAD_DIM), bf16),
                pltpu.VMEM((HEAD_DIM, span), f32),
                pltpu.VMEM((HEAD_DIM, span), f32),
            ],
        ),
        out_shape=[
            *([jax.ShapeDtypeStruct((heads * HEAD_DIM, rows), bf16)] * 2 if last else [jax.ShapeDtypeStruct((HEADS // 2 * HEAD_DIM, span), f32)]),
            *[jax.ShapeDtypeStruct((heads * 2 * HEAD_DIM, rows), bf16)] * 2,
        ],
        input_output_aliases=alias,
        cost_estimate=pl.CostEstimate(
            flops=32 * heads * span * span * HEAD_DIM, bytes_accessed=2 * heads * span * span, transcendentals=0
        ),
        name="attend_back",
    )(info, query_a, query_b, key_a, key_b, key_a, key_b, grad_a, grad_b, attended, stat, own, probs, *extra_args)


def middle_kernel(
    info_ref, mine_ref, theirs_ref, hidden_ref, cot_ref, w_ref, vec_ref,
    out_ref, grad_mid_ref, grad_mine_ref, grad_theirs_ref, packed_ref, sums_ref,
    total, act_s, slope_s, *, ff,
):
    step = pl.program_id(0)
    rows, width = hidden_ref.shape
    dp = w_ref.shape[0]
    shard = width // dp
    down_at, up_at = shard, shard + ff // dp
    own, other = info_ref[0], 1 - info_ref[0]
    halves = lambda which: (pl.ds(which * (dp // 2), dp // 2), pl.ds(0, shard), slice(None))
    down_rows = lambda j: (pl.ds(j * dp * width // ff, dp * width // ff), pl.ds(down_at, ff // dp), slice(None))
    up_rows = lambda j: (slice(None), pl.ds(up_at + j * shard, shard), slice(None))
    half = mine_ref.shape[0]
    blocks = ff // width

    @pl.when(step == 0)
    def _():
        total[...] = jnp.zeros_like(total)
        sums_ref[...] = jnp.zeros_like(sums_ref)

    w_mine = w_ref[halves(own)].reshape(half, width)
    w_theirs = w_ref[halves(other)].reshape(half, width)
    middle = hidden_ref[...].astype(f32) + dot(mine_ref[...], w_mine, 0, 0) + dot(theirs_ref[...], w_theirs, 0, 0) + vec_ref[0:1, 0:width]
    gain, shift, bias_down = [vec_ref[0:1, k * width : (k + 1) * width] for k in (1, 2, 3)]
    hat, scale = norm_parts(middle)
    normed = (hat * gain + shift).astype(bf16)
    out = middle + bias_down
    for j in range(blocks):
        cols = slice(j * width, (j + 1) * width)
        activated, slope = gelu_and_slope(dot(normed, w_ref[up_rows(j)].reshape(width, width), 1, 0) + vec_ref[1:2, cols])
        activated = activated.astype(bf16)
        act_s[:, cols] = activated
        slope_s[:, cols] = slope
        out = out + dot(activated, w_ref[down_rows(j)].reshape(width, width), 1, 0)
    out_ref[...] = out.astype(bf16)

    pos = step * rows + lax.broadcasted_iota(jnp.int32, (rows, width), 0)
    grad_z = jnp.where(pos < info_ref[1], cot_ref[...], jnp.zeros_like(cot_ref))
    grad_norm = jnp.zeros((rows, width), f32)
    for j in range(blocks):
        cols = slice(j * width, (j + 1) * width)
        grad_act = dot(grad_z, w_ref[down_rows(j)].reshape(width, width), 1, 1) * slope_s[:, cols]
        sums_ref[0:1, cols] += jnp.sum(grad_act, axis=0, keepdims=True)
        grad_pre = grad_act.astype(bf16)
        total[down_rows(j)] += dot(act_s[:, cols], grad_z, 0, 0).reshape(dp * width // ff, ff // dp, width)
        total[up_rows(j)] += dot(normed, grad_pre, 0, 0).reshape(dp, shard, width)
        grad_norm = grad_norm + dot(grad_pre, w_ref[up_rows(j)].reshape(width, width), 1, 1)
    grad_out = grad_z.astype(f32)
    grad_mid = grad_out + norm_back(grad_norm, hat, scale, gain)
    grad_mid_ref[...] = grad_mid
    branch = grad_mid.astype(bf16)
    for k, value in enumerate((branch.astype(f32), grad_norm * hat, grad_norm, grad_out)):
        sums_ref[1:2, k * width : (k + 1) * width] += jnp.sum(value, axis=0, keepdims=True)
    grad_mine_ref[...] = dot(w_mine, branch, 1, 1).astype(bf16)
    grad_theirs_ref[...] = dot(w_theirs, branch, 1, 1).astype(bf16)
    total[halves(own)] += dot(mine_ref[...], branch, 1, 0).reshape(dp // 2, shard, width)
    total[halves(other)] += dot(theirs_ref[...], branch, 1, 0).reshape(dp // 2, shard, width)

    @pl.when(step == pl.num_programs(0) - 1)
    def _():
        packed_ref[:, 0 : total.shape[1]] = total[...].astype(bf16)


def middle_part(info, mine, theirs, hidden, cot, weights, vectors, ff):
    half = mine.shape[0]
    rows, width = hidden.shape
    blk = min(256, rows)
    packed = weights.shape
    tall = pl.BlockSpec((blk, width), lambda i, n: (i, 0))
    wide = pl.BlockSpec((half, blk), lambda i, n: (0, i))
    fixed = lambda shape: pl.BlockSpec(shape, lambda i, n: (0,) * len(shape))
    return pl.pallas_call(
        functools.partial(middle_kernel, ff=ff),
        grid_spec=pltpu.PrefetchScalarGridSpec(
            num_scalar_prefetch=1,
            grid=(rows // blk,),
            in_specs=[wide, wide, tall, tall, fixed(packed), fixed(vectors.shape)],
            out_specs=[tall, tall, wide, wide, fixed(packed), fixed((8, ff))],
            scratch_shapes=[pltpu.VMEM((packed[0], packed[1] - 16, width), f32), pltpu.VMEM((blk, ff), bf16), pltpu.VMEM((blk, ff), f32)],
        ),
        out_shape=[
            jax.ShapeDtypeStruct((rows, width), bf16),
            jax.ShapeDtypeStruct((rows, width), f32),
            jax.ShapeDtypeStruct((half, rows), bf16),
            jax.ShapeDtypeStruct((half, rows), bf16),
            jax.ShapeDtypeStruct(packed, bf16),
            jax.ShapeDtypeStruct((8, ff), f32),
        ],
        cost_estimate=pl.CostEstimate(flops=12 * rows * width * (2 * ff + width) // 2, bytes_accessed=16 << 20, transcendentals=rows * ff),
        name="middle",
    )(info, mine, theirs, hidden, cot, weights, vectors)


def pack_kernel(out_ref, down_ref, up_ref, row_ref, packed_ref):
    shard, width = out_ref.shape
    at = shard + down_ref.shape[0]
    packed_ref[0:shard] = out_ref[...]
    packed_ref[shard:at] = down_ref[...]
    for j in range(up_ref.shape[1] // width):
        packed_ref[at + j * shard : at + (j + 1) * shard] = up_ref[:, j * width : (j + 1) * width]
    end = at + up_ref.shape[1] // width * shard
    packed_ref[end:] = jnp.broadcast_to(row_ref[...], (packed_ref.shape[0] - end, width))


def pack_part(out_weight, down_weight, up_weight, row):
    shard, width = out_weight.shape
    total = shard + down_weight.shape[0] + up_weight.shape[1] // width * shard + 16
    return pl.pallas_call(pack_kernel, out_shape=jax.ShapeDtypeStruct((total, width), bf16), name="pack")(out_weight, down_weight, up_weight, row)


def shape_kernel(info_ref, w_ref, small_ref, out_ref):
    part = w_ref.shape[0] // 2
    heads = HEADS // 2
    half = heads * HEAD_DIM
    block = w_ref[pl.ds(pl.multiple_of(info_ref[0] * part, part), part)]
    for which in range(2):
        cols = [block[:, which * half : (which + 1) * half]]
        for head in range(heads):
            for kind in (1, 2):
                at = (2 * kind + which) * half + head * HEAD_DIM
                cols.append(block[:, at : at + HEAD_DIM])
        out_ref[which * part : (which + 1) * part] = jnp.concatenate(cols, 1)
    out_ref[2 * part :] = jnp.broadcast_to(small_ref[...], (8, 3 * half))


def shape_part(info, weight, small):
    shard, cols = weight.shape
    full = pl.BlockSpec(memory_space=pltpu.VMEM)
    return pl.pallas_call(
        shape_kernel,
        in_specs=[pl.BlockSpec(memory_space=pltpu.SMEM), full, full],
        out_specs=full,
        out_shape=jax.ShapeDtypeStruct((shard + 8, cols // 2), bf16),
        name="shape",
    )(info, weight, small)


def place_kernel(info_ref, *refs, lows):
    own, other, out_ref, small_ref = refs[:lows], refs[lows : 2 * lows], refs[2 * lows], refs[2 * lows + 1]
    part, cols = out_ref.shape[3:]
    for j in range(lows):
        for k in range(own[j].shape[0]):
            at = info_ref[4] ^ (k * lows + j)
            out_ref[:, pl.ds(at, 1), pl.ds(info_ref[0], 1)] = own[j][k, 0 : 2 * part].reshape(2, part, cols)[:, None, None]
            out_ref[:, pl.ds(at, 1), pl.ds(1 - info_ref[0], 1)] = other[j][k, 0 : 2 * part].reshape(2, part, cols)[:, None, None]
            small_ref[pl.ds(at, 1)] = own[j][k, 2 * part :][None]


def place_part(info, own, other):
    count, rows, cols = own[0].shape
    full = pl.BlockSpec(memory_space=pltpu.VMEM)
    return pl.pallas_call(
        functools.partial(place_kernel, lows=len(own)),
        in_specs=[pl.BlockSpec(memory_space=pltpu.SMEM)] + [full] * (2 * len(own)),
        out_specs=[full, full],
        out_shape=[
            jax.ShapeDtypeStruct((2, count * len(own), 2, rows // 2 - 4, cols), bf16),
            jax.ShapeDtypeStruct((count * len(own), 8, cols), bf16),
        ],
        name="place",
    )(info, *own, *other)


def finish_kernel(info_ref, hidden_ref, mid_ref, w_ref, vec_ref, *refs, groups):
    many_groups = len(groups)
    parts, (mine_ref, theirs_ref, bias_ref, out_ref, sums_ref, total, grads) = refs[: 6 * many_groups], refs[6 * many_groups :]
    step = pl.program_id(0)
    rows, width = hidden_ref.shape
    half = width // 2

    @pl.when(step == 0)
    def _():
        total[...] = jnp.zeros_like(total)
        sums_ref[...] = jnp.zeros_like(sums_ref)

    ones = jnp.where(lax.broadcasted_iota(jnp.int32, (16, rows), 0) == 0, 1.0, 0.0).astype(bf16)
    hat, scale = norm_parts(hidden_ref[...].astype(f32))
    gain, shift = vec_ref[0:1], vec_ref[1:2]
    left = jnp.concatenate([(hat * gain + shift).astype(bf16).T, ones], 0)
    grad_norm = jnp.zeros((width, rows), f32)
    for which in range(2):
        dqs, dkvs, far = [parts[(3 * which + n) * many_groups : (3 * which + n + 1) * many_groups] for n in range(3)]
        for (at, many), dq_ref, dkv_ref, far_ref in zip(groups, dqs, dkvs, far):
            grads[which, at * HEAD_DIM : (at + many) * HEAD_DIM] = dq_ref[...]
            where = slice(half + at * 2 * HEAD_DIM, half + (at + many) * 2 * HEAD_DIM)
            grads[which, where] = (dkv_ref[...].astype(f32) + far_ref[...].astype(f32)).astype(bf16)
        total[which] += dot(left, grads[which], 1, 1)
        weights = w_ref[pl.ds(info_ref[0] ^ which, 1)].reshape(width, 3 * half)
        grad_norm = grad_norm + dot(weights, grads[which], 1, 0)
    grad_norm = grad_norm.T
    sums_ref[0:1] += jnp.sum(grad_norm * hat, axis=0, keepdims=True)
    sums_ref[1:2] += jnp.sum(grad_norm, axis=0, keepdims=True)
    out_ref[...] = (mid_ref[...] + norm_back(grad_norm, hat, scale, gain)).astype(bf16)

    @pl.when(step == pl.num_programs(0) - 1)
    def _():
        mine_ref[...] = total[0, 0:width].astype(bf16)
        theirs_ref[...] = total[1, 0:width].astype(bf16)
        for which in range(2):
            bias_ref[which] = jnp.broadcast_to(total[which, width : width + 1], bias_ref.shape[1:])


def finish_part(info, hidden, grad_mid, weights, vectors, mine, theirs, groups):
    rows, width = hidden.shape
    cols = 3 * width // 2
    blk = min(512, rows)
    wide = lambda n: pl.BlockSpec((n, blk), lambda i, n_: (0, i))
    tall = pl.BlockSpec((blk, width), lambda i, n: (i, 0))
    fixed = lambda shape: pl.BlockSpec(shape, lambda i, n: (0,) * len(shape))
    parts = [x for side in (mine, theirs) for kind in side for x in kind]
    return pl.pallas_call(
        functools.partial(finish_kernel, groups=groups),
        grid_spec=pltpu.PrefetchScalarGridSpec(
            num_scalar_prefetch=1,
            grid=(rows // blk,),
            in_specs=[tall, tall, fixed(weights.shape), fixed(vectors.shape)] + [wide(x.shape[0]) for x in parts],
            out_specs=[fixed((width, cols)), fixed((width, cols)), fixed((2, 8, cols)), tall, fixed((8, width))],
            scratch_shapes=[pltpu.VMEM((2, width + 16, cols), f32), pltpu.VMEM((2, cols, blk), bf16)],
        ),
        out_shape=[
            jax.ShapeDtypeStruct((width, cols), bf16),
            jax.ShapeDtypeStruct((width, cols), bf16),
            jax.ShapeDtypeStruct((2, 8, cols), f32),
            jax.ShapeDtypeStruct((rows, width), bf16),
            jax.ShapeDtypeStruct((8, width), f32),
        ],
        cost_estimate=pl.CostEstimate(flops=8 * rows * width * cols, bytes_accessed=16 << 20, transcendentals=rows),
        name="finish",
    )(info, hidden, grad_mid, weights, vectors, *parts)


def join_kernel(info_ref, held_ref, got_ref, out_ref, small_ref):
    shard = out_ref.shape[0]
    heads = HEADS // 2
    half = heads * HEAD_DIM
    held, got = held_ref[...].astype(f32), got_ref[...].astype(f32)
    for which in range(2):
        block = jnp.where(info_ref[0] == which, got[:shard], held[:shard])
        out_ref[:, which * half : (which + 1) * half] = block[:, :half]
        for kind in (1, 2):
            at = (2 * kind + which) * half
            starts = [half + (2 * head + kind - 1) * HEAD_DIM for head in range(heads)]
            out_ref[:, at : at + half] = jnp.concatenate([block[:, start : start + HEAD_DIM] for start in starts], 1)
    small_ref[...] = held[shard:] + got[shard:]


def join_part(info, held, got):
    rows, cols = held.shape
    full = pl.BlockSpec(memory_space=pltpu.VMEM)
    return pl.pallas_call(
        join_kernel,
        in_specs=[pl.BlockSpec(memory_space=pltpu.SMEM), full, full],
        out_specs=[full, full],
        out_shape=[jax.ShapeDtypeStruct((rows - 8, 2 * cols), f32), jax.ShapeDtypeStruct((8, cols), f32)],
        name="join",
    )(info, held, got)


def swap(values, axis, flip):
    size = lax.axis_size(axis)
    return lax.ppermute(values, axis, [(i, i ^ flip) for i in range(size)])


def gelu_and_slope(u):
    a = 0.7978845608028654
    inner = a * (u + 0.044715 * u * u * u)
    t = jnp.tanh(inner)
    slope = 0.5 * (1 + t) + 0.5 * u * (1 - t * t) * a * (1 + 3 * 0.044715 * u * u)
    return 0.5 * u * (1 + t), slope


def norm_parts(inputs):
    center = inputs - jnp.mean(inputs, axis=-1, keepdims=True)
    scale = lax.rsqrt(jnp.mean(center * center, axis=-1, keepdims=True) + EPS)
    return center * scale, scale


def norm_back(grad, hat, scale, gain):
    e = grad * gain
    return scale * (e - jnp.mean(e, axis=-1, keepdims=True) - hat * jnp.mean(e * hat, axis=-1, keepdims=True))


def tie(*values):
    return lax.optimization_barrier(values)


def on_device(
    hidden_in, seq_lengths, out_cotangent, norm1_gain, norm1_shift, qkv_weight, qv_bias, out_weight, out_bias,
    norm2_gain, norm2_shift, up_weight, up_bias, down_weight, down_bias,
):
    rows, width = hidden_in.shape[1:]
    hidden_in, out_cotangent = hidden_in[0], out_cotangent[0]
    ff = up_weight.shape[1]
    dp, ctx = lax.axis_size("dp"), lax.axis_size("ctx")
    dp_low = 2 if dp == 8 else 4
    dp_high, high_at = dp // dp_low, dp_low.bit_length() - 1
    ring = ctx // 2
    me = lax.axis_index("ctx")
    core = me % 2
    heads = HEADS // 2
    half = heads * HEAD_DIM
    shard = width // dp
    length = seq_lengths[0]
    info = jnp.stack([core, jnp.clip(length - me * rows, 0, rows), length, me, lax.axis_index("dp")]).astype(jnp.int32)

    def by_core(cols):
        lead = cols.shape[:-1]
        cols = cols.reshape(lead + (3, 2, heads, HEAD_DIM))
        asks = cols[..., 0, :, :, :].reshape(lead + (2, half))
        pairs = jnp.moveaxis(cols[..., 1:, :, :, :], -4, -2).reshape(lead + (2, 2 * half))
        return jnp.concatenate([asks, pairs], -1)

    def from_core(cols):
        lead = cols.shape[:-2]
        asks = cols[..., :half].reshape(lead + (1, 2, heads, HEAD_DIM))
        pairs = jnp.moveaxis(cols[..., half:].reshape(lead + (2, heads, 2, HEAD_DIM)), -2, -4)
        return jnp.concatenate([asks, pairs], -4).reshape(lead + (6 * half,))

    high_stage = lambda x: [swap(x, "dp", k << high_at) for k in range(1, dp_high)]
    low_stage = lambda x: [swap(x, "dp", j) for j in range(1, dp_low)]

    early = jnp.concatenate([norm1_gain, norm1_shift, qv_bias[0], qv_bias[1]])
    early = jnp.pad(early, (0, 3 * half - early.shape[0]))[None]
    piece = shape_part(info, qkv_weight, early)
    pieces = [piece] + high_stage(piece)
    late = jnp.concatenate([out_bias, norm2_gain, norm2_shift, down_bias, up_bias])
    late = jnp.pad(late, (0, width - late.shape[0]))[None]
    others = pack_part(out_weight, down_weight, up_weight, late)
    others, pieces = tie(others, pieces)
    others = lax.all_gather(others, "dp", axis=0, tiled=False)
    stack = jnp.stack(pieces)
    own = [stack] + low_stage(stack)
    other = [swap(x, "ctx", 1) for x in own]
    w_qkv, early = place_part(info, own, other)
    w_qkv = w_qkv.reshape(2, width, 3 * half)
    early = early[:, 0, : 4 * shard].reshape(dp, 4, shard).swapaxes(0, 1).reshape(4, width).astype(f32)
    gain_one, shift_one, bias_q, bias_v = early

    hat_one, _ = norm_parts(hidden_in.astype(f32))
    normed_one = (hat_one * gain_one + shift_one).astype(bf16)
    bias_full = by_core(jnp.concatenate([bias_q, jnp.zeros_like(bias_q), bias_v]))
    factors = jnp.where(jnp.arange(3 * half) < half, LOG2E * HEAD_DIM**-0.5, 1.0)

    def projected(which):
        pick = lambda x: lax.dynamic_index_in_dim(x, which, 0, keepdims=False)
        return ((dot(pick(w_qkv), normed_one, 0, 1) + pick(bias_full)[:, None]) * factors[:, None]).astype(bf16)

    foreign = projected(1 - core)
    mine = projected(core)
    theirs = swap(foreign, "ctx", 1)

    groups = [(0, 2), (2, 2)] if ring == 2 else [(0, heads)]
    far = []
    for k in range(1, ring):
        for at, many in groups:
            cut = slice(half + at * 2 * HEAD_DIM, half + (at + many) * 2 * HEAD_DIM)
            there = tie(foreign[cut], mine, theirs)[0] if at else foreign[cut]
            far.append((k, at, many, swap(mine[cut], "ctx", 2 * k), swap(there, "ctx", 2 * k + 1)))
    *sums, own_top, probs = attend(info, 0, mine, theirs, mine, theirs, heads, 0, heads, None, None, ring == 1)
    near = (own_top, probs)
    saved, low = [], None
    for k, at, many, key_a, key_b in far:
        last = k == ring - 1
        out = attend(info, k, mine, theirs, key_a, key_b, 0, at, many, sums, low if last else None, last)
        if last:
            low, out = out[:2], out[2:]
        sums, own_top, probs = out[:2], out[2], out[3]
        saved.append((own_top, probs))
    attended, stat = sums
    low_theirs = swap(low[1], "ctx", 1)

    rest = others[:, -16].astype(f32)
    vector = lambda at: rest[:, at * shard : (at + 1) * shard].reshape(width)
    second_rows = jnp.pad(
        jnp.stack([jnp.concatenate([vector(0), vector(1), vector(2), vector(3)]), rest[:, 4 * shard : 4 * shard + ff // dp].reshape(ff)]), ((0, 6), (0, 0))
    )
    hidden_out, grad_mid, grad_mine, grad_theirs, packed, sums_two = middle_part(
        info, low[0], low_theirs, hidden_in, out_cotangent, others, second_rows, ff
    )
    grad_theirs = swap(grad_theirs, "ctx", 1)

    spread = lambda x: x.reshape(-1, dp, x.shape[-1] // dp).swapaxes(0, 1).reshape(dp, -1)
    late = jnp.concatenate([spread(sums_two[1].reshape(4, width)), spread(sums_two[0].reshape(1, ff))], 1)
    late = jnp.pad(late, ((0, 0), (0, width - late.shape[1])))[:, None].astype(bf16)
    packed = lax.dynamic_update_slice(packed, jnp.broadcast_to(late, (dp, 16, width)), (0, packed.shape[1] - 16, 0))
    packed = lax.psum_scatter(packed, "dp", scatter_dimension=0, tiled=False)

    buffer, flying, back_mine, back_theirs = None, [], {}, {}
    shared = (grad_mine, grad_theirs, attended, stat)
    calls = [(k, at, many, key_a, key_b, 0, 0, kept) for (k, at, many, key_a, key_b), kept in zip(far, saved)]
    calls = calls + [(0, at, many, mine, theirs, heads + 2 * at, at, near) for at, many in groups]
    ends = []
    for n, (k, at, many, key_a, key_b, kv_base, p_base, kept) in enumerate(calls):
        call_info = info
        if ends:
            call_info, kept_back = tie(info, ends[-1][2])
            ends[-1] = ends[-1][:2] + (kept_back,) + ends[-1][3:]
        if n > 1 and flying:
            call_info, (got_mine, got_theirs), where = *tie(call_info, flying[0][:2]), flying.pop(0)[2]
            back_mine.setdefault(where, []).append(got_mine)
            back_theirs.setdefault(where, []).append(got_theirs)
        outs = attend_back(call_info, k, mine, theirs, key_a, key_b, kv_base, p_base, at, many, *shared, *kept, (buffer, k == 0 or k > 1), k == 0)
        if k:
            buffer = outs[0]
            flying.append((swap(outs[1], "ctx", 2 * k), swap(outs[2], "ctx", 2 * k + 1), at))
        else:
            dq_a, dq_b, dkv_a, dkv_b = outs
            ends.append((dq_a, swap(dq_b, "ctx", 1), dkv_a, swap(dkv_b, "ctx", 1)))
    for got_mine, got_theirs, where in flying:
        back_mine.setdefault(where, []).append(got_mine)
        back_theirs.setdefault(where, []).append(got_theirs)
    dqs_mine, dqs_theirs, dkvs_mine, dkvs_theirs = zip(*ends)
    sum_far = lambda parts: [functools.reduce(lambda a, b: (a.astype(f32) + b.astype(f32)).astype(bf16), parts[at]) for at, _ in groups]

    sides = [(dqs_mine, dkvs_mine, sum_far(back_mine)), (dqs_theirs, dkvs_theirs, sum_far(back_theirs))]
    packed = packed.reshape((2, -1) + packed.shape[1:])
    packed_first, packed_send = [lax.dynamic_index_in_dim(packed, core ^ k, 0, keepdims=False) for k in range(2)]
    call_info, packed_send = tie(info, packed_send)
    dw_out, dw, bias_sides, grad_hidden, sums_one = finish_part(call_info, hidden_in, grad_mid, w_qkv, early, *sides, groups)
    dw_in = swap(dw_out, "ctx", 1)

    def halves(total, axis, shift, count, dim):
        index = (lax.axis_index(axis) >> shift) & (count - 1)
        pick = lambda k: lax.dynamic_index_in_dim(total, index ^ k, dim, keepdims=False)
        return pick(0).astype(f32), [pick(k).astype(bf16) for k in range(1, count)]

    swaps = lambda parts, axis, shift: [swap(part, axis, k << shift) for k, part in enumerate(parts, 1)]
    add = lambda first, rest: functools.reduce(lambda a, b: a + b.astype(f32), rest, first.astype(f32))

    def sum_chips(total, covers=None):
        for flip in [2 << b for b in range(ring.bit_length() - 1)]:
            total = total.astype(bf16)
            got = swap(total, "ctx", flip)
            if covers is not None:
                got, _ = tie(got, covers)
            total = add(total, [got])
        return total.astype(bf16)

    bias_one = jnp.where(core == 0, bias_sides[0, 0], bias_sides[1, 0])
    bias_two = jnp.where(core == 0, bias_sides[1, 0], bias_sides[0, 0])
    bias_sums = from_core(jnp.stack([bias_one, bias_two])).reshape(3, width)
    smalls = jnp.concatenate([spread(sums_one[0:2]), spread(bias_sums[0:1]), spread(bias_sums[2:3])], 1)
    smalls = jnp.pad(smalls[:, None], ((0, 0), (0, 7), (0, 3 * half - smalls.shape[1])))
    total = jnp.concatenate([add(dw, [dw_in]).reshape(dp, shard, 3 * half), smalls], 1)
    first, sent = halves(total.reshape((dp_high, dp_low) + total.shape[1:]), "dp", 0, dp_low, 1)
    sent, packed_send = tie(sent, packed_send)
    sent = swaps(sent, "dp", 0)
    packed = add(packed_first, [swap(packed_send, "ctx", 1)]).astype(bf16)
    sent, _ = tie(sent, packed)
    packed = sum_chips(packed)
    first, sent = halves(add(first, sent), "dp", high_at, dp_high, 0)
    sent = swaps(sent, "dp", high_at)
    sent, _ = tie(sent, packed)
    packed_got = swap(packed, "ctx", 1)
    by_index = lambda a, b: [jnp.where(core == 0, a, b), jnp.where(core == 0, b, a)]
    packed = jnp.concatenate(by_index(packed, packed_got), 0).astype(f32)
    down_at, up_at, end = shard, shard + ff // dp, shard + 2 * (ff // dp)
    grad_up = packed[up_at:end].reshape(ff // width, shard, width).swapaxes(0, 1).reshape(shard, ff)
    grad_out_weight, grad_down, last_row = packed[:shard], packed[down_at:up_at], packed[-16]
    total = sum_chips(add(first, sent), (grad_out_weight, grad_down, grad_up, last_row))
    grad_qkv, smalls = join_part(info, total, swap(total, "ctx", 1))
    smalls = smalls[0]
    small_out = lambda at: smalls[at * shard : (at + 1) * shard]
    late_out = lambda at: last_row[at * shard : (at + 1) * shard]
    return (
        hidden_out[None],
        grad_hidden[None],
        small_out(0),
        small_out(1),
        grad_qkv,
        jnp.stack([small_out(2), small_out(3)]),
        grad_out_weight,
        late_out(0),
        late_out(1),
        late_out(2),
        grad_up,
        last_row[4 * shard : 4 * shard + ff // dp],
        grad_down,
        late_out(3),
    )


def solution(mesh):
    return jax.shard_map(
        on_device,
        mesh=mesh,
        in_specs=(
            P("dp", "ctx", None), P("dp"), P("dp", "ctx", None), P("dp"), P("dp"), P("dp", None), P(None, "dp"),
            P("dp", None), P("dp"), P("dp"), P("dp"), P("dp", None), P("dp"), P("dp", None), P("dp"),
        ),
        out_specs=(
            P("dp", "ctx", None), P("dp", "ctx", None), P("dp"), P("dp"), P("dp", None), P(None, "dp"), P("dp", None),
            P("dp"), P("dp"), P("dp"), P("dp", None), P("dp"), P("dp", None), P("dp"),
        ),
        check_vma=False,
    )
```

```python
import functools

import jax
import jax.numpy as jnp
from jax import lax
from jax.experimental import pallas as pl
from jax.experimental.pallas import tpu as pltpu
from jax.sharding import PartitionSpec as P

HEADS = 8
HEAD_DIM = 64
EPS = 1e-05
LOG2E = 1.4426950408889634
LN2 = 0.6931471805599453
LOW = -1e30
TOP = 1e30
f32 = jnp.float32
bf16 = jnp.bfloat16


def dot(left, right, left_dim, right_dim):
    return lax.dot_general(left, right, (((left_dim,), (right_dim,)), ((), ())), preferred_element_type=f32)


def split_three(values):
    one = values.astype(bf16)
    rest = values - one.astype(f32)
    two = rest.astype(bf16)
    return one, two, (rest - two.astype(f32)).astype(bf16)


def counts_of(info_ref, hop, rows):
    length, source = info_ref[2], info_ref[3] ^ (2 * hop)
    return jnp.clip(length - source * rows, 0, rows), jnp.clip(length - (source ^ 1) * rows, 0, rows), info_ref[0] * rows


def forward_kernel(info_ref, qa_ref, qb_ref, ka_ref, kb_ref, va_ref, vb_ref, *rest, blk, hop, first, last, aliases):
    prev, rest = ((None, None), rest) if first else (rest[:2], rest[2:])
    rest = rest[aliases:]
    low_refs, rest = (rest[:2], rest[2:]) if last else (None, rest)
    o_ref, stat_ref, own_ref, p_ref, keys, values = rest
    chunk = pl.program_id(1)
    rows = qa_ref.shape[1]
    span = keys.shape[0]
    *valid, start = counts_of(info_ref, hop, rows)
    alive = valid[0] + valid[1] > 0

    def finish(out, sums, top):
        own_ref[0] = jnp.broadcast_to(top, (8, rows))
        if not first:
            old_sums, old_top = prev[1][0, 0:1], prev[1][0, 1:2]
            new_top = jnp.maximum(top, old_top)
            scale, old_scale = jnp.exp2(top - new_top), jnp.exp2(old_top - new_top)
            out = out * scale + prev[0][...] * old_scale
            sums = sums * scale + old_sums * old_scale
            top = new_top
        stat_ref[0] = jnp.concatenate([sums, top, jnp.zeros((6, rows), f32)], 0)
        if last:
            out = out / sums
            for which, low_ref in enumerate(low_refs):

                @pl.when(chunk == which)
                def _():
                    low_ref[...] = out.astype(bf16)

        o_ref[...] = out

    @pl.when(jnp.logical_and(alive, chunk == 0))
    def _():
        pos = lax.broadcasted_iota(jnp.int32, (HEAD_DIM, rows), 1)
        row = lax.broadcasted_iota(jnp.int32, (HEAD_DIM, rows), 0)
        for part, (k_ref, v_ref) in enumerate(((ka_ref, va_ref), (kb_ref, vb_ref))):
            mask = jnp.where(pos < valid[part], 0.0, LOW)
            extra = jnp.where(row < 3, 1.0, jnp.where(row == 3, mask, 0.0)).astype(bf16)
            keys[pl.ds(part * rows, rows), :] = jnp.concatenate([k_ref[...], extra], 0).T
            values[:, pl.ds(part * rows, rows)] = v_ref[...]

    @pl.when(jnp.logical_not(alive))
    def _():
        finish(jnp.zeros((HEAD_DIM, rows), f32), jnp.zeros((1, rows), f32), jnp.full((1, rows), LOW, f32))

    @pl.when(alive)
    def _():
        query = jnp.where(chunk == 0, qa_ref[...], qb_ref[...])
        row = lax.broadcasted_iota(jnp.int32, (HEAD_DIM, rows), 0)
        head_blk = 64

        def extend(top):
            one, two, three = [jnp.broadcast_to(-x.astype(f32), (HEAD_DIM, rows)) for x in split_three(top)]
            extra = jnp.where(row == 0, one, jnp.where(row == 1, two, jnp.where(row == 2, three, jnp.where(row == 3, 1.0, 0.0))))
            return jnp.concatenate([query, extra.astype(bf16)], 0)

        plain = extend(jnp.zeros((1, rows), f32))
        guess = jnp.max(dot(keys[pl.ds(pl.multiple_of(start, head_blk), head_blk), :], plain, 1, 0), axis=0, keepdims=True)

        def run(top, unroll):
            query_ext = extend(top)

            def body(step, carry):
                total, sums = carry
                off = step * blk if isinstance(step, int) else pl.multiple_of(step * blk, blk)
                wide = jnp.exp2(dot(keys[pl.ds(off, blk), :], query_ext, 1, 0))
                probs = wide.astype(bf16)
                p_ref[0, 0, pl.ds(off, blk), :] = probs
                sums = sums + jnp.sum(wide.reshape(blk // 8, 8, rows), axis=0)
                return total + dot(values[:, pl.ds(off, blk)], probs, 1, 0), sums

            carry = jnp.zeros((HEAD_DIM, rows), f32), jnp.zeros((8, rows), f32)
            if unroll:
                for step in range(span // blk):
                    carry = body(step, carry)
            else:
                carry = lax.fori_loop(0, span // blk, body, carry)
            sums = jnp.sum(carry[1], axis=0, keepdims=True)
            finish(carry[0], sums, top)
            return jnp.max(sums)

        largest = run(guess, True)

        @pl.when(jnp.logical_not(largest < TOP))
        def _():
            def wider(step, top):
                off = pl.multiple_of(step * head_blk, head_blk)
                return jnp.maximum(top, jnp.max(dot(keys[pl.ds(off, head_blk), :], plain, 1, 0), axis=0, keepdims=True))

            run(lax.fori_loop(0, span // head_blk, wider, jnp.full((1, rows), LOW, f32)), False)


def head_rows(base, step, rows):
    return pl.BlockSpec((HEAD_DIM, rows), lambda h, i, n: (base + step * h, 0))


def attend(info, hop, query_a, query_b, key_a, key_b, kv_base, first_head, heads, prev, low, last):
    rows = query_a.shape[1]
    span = 2 * rows
    blk = min(512, rows)
    keys, vals, ask = head_rows(kv_base, 2, rows), head_rows(kv_base + 1, 2, rows), head_rows(first_head, 1, rows)
    out_spec = pl.BlockSpec((HEAD_DIM, rows), lambda h, i, n: (first_head + h, i))
    stat_spec = pl.BlockSpec((1, 8, rows), lambda h, i, n: (first_head + h, 0, i))
    all_heads = HEADS // 2
    extra_in = [out_spec, stat_spec] if prev else []
    extra_args = list(prev) if prev else []
    if low is not None:
        extra_in, extra_args = extra_in + [pl.BlockSpec(memory_space=pl.ANY)] * 2, extra_args + list(low)
    out_specs = [out_spec, stat_spec, pl.BlockSpec((1, 8, rows), lambda h, i, n: (h, 0, i)), pl.BlockSpec((1, 1, span, rows), lambda h, i, n: (h, i, 0, 0))]
    out_shape = [
        jax.ShapeDtypeStruct((all_heads * HEAD_DIM, span), f32),
        jax.ShapeDtypeStruct((all_heads, 8, span), f32),
        jax.ShapeDtypeStruct((heads, 8, span), f32),
        jax.ShapeDtypeStruct((heads, 2, span, rows), bf16),
    ]
    shift = 2 if last else 0
    if last:
        out_specs = [head_rows(first_head, 1, rows)] * 2 + out_specs
        out_shape = [jax.ShapeDtypeStruct((all_heads * HEAD_DIM, rows), bf16)] * 2 + out_shape
    alias = {7: shift, 8: shift + 1} if prev else {}
    if low is not None:
        alias = {**alias, 9: 0, 10: 1}
    return pl.pallas_call(
        functools.partial(forward_kernel, blk=blk, hop=hop, first=not prev, last=last, aliases=0 if low is None else 2),
        grid_spec=pltpu.PrefetchScalarGridSpec(
            num_scalar_prefetch=1,
            grid=(heads, 2),
            in_specs=[ask, ask, keys, keys, vals, vals] + extra_in,
            out_specs=out_specs,
            scratch_shapes=[pltpu.VMEM((span, 2 * HEAD_DIM), bf16), pltpu.VMEM((HEAD_DIM, span), bf16)],
        ),
        out_shape=out_shape,
        input_output_aliases=alias,
        cost_estimate=pl.CostEstimate(
            flops=16 * heads * span * span * HEAD_DIM, bytes_accessed=2 * heads * span * span, transcendentals=heads * span * span
        ),
        name="attend",
    )(info, query_a, query_b, key_a, key_b, key_a, key_b, *extra_args)


def backward_kernel(
    info_ref, qa_ref, qb_ref, ka_ref, kb_ref, va_ref, vb_ref, ga_ref, gb_ref, o_ref, stat_ref, own_ref, p_ref,
    *rest, blk, hop, adds, aliases, last,
):
    before_ref, rest = (rest[0], rest[1:]) if adds else (None, rest)
    rest = rest[aliases:]
    dq_refs, (*dkv_refs, values, dk_sum, dv_sum) = (rest[:2], rest[2:]) if last else (rest[:1], rest[1:])
    chunk = pl.program_id(1)
    rows = qa_ref.shape[1]
    span = values.shape[0]
    valid_a, valid_b, _ = counts_of(info_ref, hop, rows)
    alive = valid_a + valid_b > 0
    row = lax.broadcasted_iota(jnp.int32, (HEAD_DIM, rows), 0)

    def finish(dq):
        if adds:
            dq = dq + before_ref[...]
        if not last:
            dq_refs[0][...] = dq
            return
        for which, dq_ref in enumerate(dq_refs):

            @pl.when(chunk == which)
            def _():
                dq_ref[...] = (dq * HEAD_DIM**-0.5).astype(bf16)

    @pl.when(chunk == 0)
    def _():
        extra = jnp.where(row < 3, 1.0, 0.0).astype(bf16)
        for part, v_ref in enumerate((va_ref, vb_ref)):
            values[pl.ds(part * rows, rows), :] = jnp.concatenate([v_ref[...], extra], 0).T
        dk_sum[...] = jnp.zeros_like(dk_sum)
        dv_sum[...] = jnp.zeros_like(dv_sum)

    @pl.when(jnp.logical_not(alive))
    def _():
        finish(jnp.zeros((HEAD_DIM, rows), f32))

    @pl.when(alive)
    def _():
        query = jnp.where(chunk == 0, qa_ref[...], qb_ref[...])
        grad = jnp.where(chunk == 0, ga_ref[...], gb_ref[...])
        factor = jnp.exp2(own_ref[0, 0:1] - stat_ref[0, 1:2]) / stat_ref[0, 0:1]
        grad = (grad.astype(f32) * factor).astype(bf16)
        delta = jnp.sum(grad.astype(f32) * o_ref[...], axis=0, keepdims=True)
        one, two, three = [jnp.broadcast_to(-x.astype(f32), (HEAD_DIM, rows)) for x in split_three(delta)]
        extra = jnp.where(row == 0, one, jnp.where(row == 1, two, jnp.where(row == 2, three, 0.0))).astype(bf16)
        grad_ext = jnp.concatenate([grad, extra], 0)
        dq = jnp.zeros((HEAD_DIM, rows), f32)
        for step in range(span // blk):
            off = step * blk
            probs = p_ref[0, 0, pl.ds(off, blk), :]
            grad_scores = (probs.astype(f32) * dot(values[pl.ds(off, blk), :], grad_ext, 1, 0)).astype(bf16)
            k_ref = (ka_ref, kb_ref)[off // rows]
            dq = dq + dot(k_ref[:, pl.ds(off % rows, blk)], grad_scores, 1, 0)
            dv_sum[:, pl.ds(off, blk)] += dot(grad, probs, 1, 1)
            dk_sum[:, pl.ds(off, blk)] += dot(query, grad_scores, 1, 1)
        finish(dq)

    @pl.when(chunk == pl.num_programs(1) - 1)
    def _():
        for which, dkv_ref in enumerate(dkv_refs):
            dkv_ref[0:HEAD_DIM] = (dk_sum[:, which * rows : (which + 1) * rows] * LN2).astype(bf16)
            dkv_ref[HEAD_DIM:] = dv_sum[:, which * rows : (which + 1) * rows].astype(bf16)


def attend_back(info, hop, query_a, query_b, key_a, key_b, kv_base, p_base, first_head, heads, grad_a, grad_b, attended, stat, own, probs, before, last):
    rows = query_a.shape[1]
    span = 2 * rows
    blk = min(512, rows)
    keys, vals, ask = head_rows(kv_base, 2, rows), head_rows(kv_base + 1, 2, rows), head_rows(first_head, 1, rows)
    part = pl.BlockSpec((HEAD_DIM, rows), lambda h, i, n: (first_head + h, i))
    buffer, adds = before
    alias, extra_in, extra_args = {}, [], []
    if adds:
        extra_in, extra_args = [part], [buffer]
        alias = {} if last else {13: 0}
    elif buffer is not None:
        extra_in, extra_args, alias = [pl.BlockSpec(memory_space=pl.ANY)], [buffer], {13: 0}
    return pl.pallas_call(
        functools.partial(backward_kernel, blk=blk, adds=adds, hop=hop, aliases=len(extra_in) - int(adds), last=last),
        grid_spec=pltpu.PrefetchScalarGridSpec(
            num_scalar_prefetch=1,
            grid=(heads, 2),
            in_specs=[
                ask, ask, keys, keys, vals, vals, ask, ask,
                part,
                pl.BlockSpec((1, 8, rows), lambda h, i, n: (first_head + h, 0, i)),
                pl.BlockSpec((1, 8, rows), lambda h, i, n: (p_base + h, 0, i)),
                pl.BlockSpec((1, 1, span, rows), lambda h, i, n: (p_base + h, i, 0, 0)),
            ] + extra_in,
            out_specs=([head_rows(0, 1, rows)] * 2 if last else [part]) + [pl.BlockSpec((2 * HEAD_DIM, rows), lambda h, i, n: (h, 0))] * 2,
            scratch_shapes=[
                pltpu.VMEM((span, 2 * HEAD_DIM), bf16),
                pltpu.VMEM((HEAD_DIM, span), f32),
                pltpu.VMEM((HEAD_DIM, span), f32),
            ],
        ),
        out_shape=[
            *([jax.ShapeDtypeStruct((heads * HEAD_DIM, rows), bf16)] * 2 if last else [jax.ShapeDtypeStruct((HEADS // 2 * HEAD_DIM, span), f32)]),
            *[jax.ShapeDtypeStruct((heads * 2 * HEAD_DIM, rows), bf16)] * 2,
        ],
        input_output_aliases=alias,
        cost_estimate=pl.CostEstimate(
            flops=32 * heads * span * span * HEAD_DIM, bytes_accessed=2 * heads * span * span, transcendentals=0
        ),
        name="attend_back",
    )(info, query_a, query_b, key_a, key_b, key_a, key_b, grad_a, grad_b, attended, stat, own, probs, *extra_args)


def middle_kernel(
    info_ref, mine_ref, theirs_ref, hidden_ref, cot_ref, w_ref, vec_ref,
    out_ref, grad_mid_ref, grad_mine_ref, grad_theirs_ref, packed_ref, sums_ref,
    total, act_s, slope_s, *, ff,
):
    step = pl.program_id(0)
    rows, width = hidden_ref.shape
    dp = w_ref.shape[0]
    shard = width // dp
    down_at, up_at = shard, shard + ff // dp
    own, other = info_ref[0], 1 - info_ref[0]
    halves = lambda which: (pl.ds(which * (dp // 2), dp // 2), pl.ds(0, shard), slice(None))
    down_rows = lambda j: (pl.ds(j * dp * width // ff, dp * width // ff), pl.ds(down_at, ff // dp), slice(None))
    up_rows = lambda j: (slice(None), pl.ds(up_at + j * shard, shard), slice(None))
    half = mine_ref.shape[0]
    blocks = ff // width

    @pl.when(step == 0)
    def _():
        total[...] = jnp.zeros_like(total)
        sums_ref[...] = jnp.zeros_like(sums_ref)

    w_mine = w_ref[halves(own)].reshape(half, width)
    w_theirs = w_ref[halves(other)].reshape(half, width)
    middle = hidden_ref[...].astype(f32) + dot(mine_ref[...], w_mine, 0, 0) + dot(theirs_ref[...], w_theirs, 0, 0) + vec_ref[0:1, 0:width]
    gain, shift, bias_down = [vec_ref[0:1, k * width : (k + 1) * width] for k in (1, 2, 3)]
    hat, scale = norm_parts(middle)
    normed = (hat * gain + shift).astype(bf16)
    out = middle + bias_down
    for j in range(blocks):
        cols = slice(j * width, (j + 1) * width)
        activated, slope = gelu_and_slope(dot(normed, w_ref[up_rows(j)].reshape(width, width), 1, 0) + vec_ref[1:2, cols])
        activated = activated.astype(bf16)
        act_s[:, cols] = activated
        slope_s[:, cols] = slope
        out = out + dot(activated, w_ref[down_rows(j)].reshape(width, width), 1, 0)
    out_ref[...] = out.astype(bf16)

    pos = step * rows + lax.broadcasted_iota(jnp.int32, (rows, width), 0)
    grad_z = jnp.where(pos < info_ref[1], cot_ref[...], jnp.zeros_like(cot_ref))
    grad_norm = jnp.zeros((rows, width), f32)
    for j in range(blocks):
        cols = slice(j * width, (j + 1) * width)
        grad_act = dot(grad_z, w_ref[down_rows(j)].reshape(width, width), 1, 1) * slope_s[:, cols]
        sums_ref[0:1, cols] += jnp.sum(grad_act, axis=0, keepdims=True)
        grad_pre = grad_act.astype(bf16)
        total[down_rows(j)] += dot(act_s[:, cols], grad_z, 0, 0).reshape(dp * width // ff, ff // dp, width)
        total[up_rows(j)] += dot(normed, grad_pre, 0, 0).reshape(dp, shard, width)
        grad_norm = grad_norm + dot(grad_pre, w_ref[up_rows(j)].reshape(width, width), 1, 1)
    grad_out = grad_z.astype(f32)
    grad_mid = grad_out + norm_back(grad_norm, hat, scale, gain)
    grad_mid_ref[...] = grad_mid
    branch = grad_mid.astype(bf16)
    for k, value in enumerate((branch.astype(f32), grad_norm * hat, grad_norm, grad_out)):
        sums_ref[1:2, k * width : (k + 1) * width] += jnp.sum(value, axis=0, keepdims=True)
    grad_mine_ref[...] = dot(w_mine, branch, 1, 1).astype(bf16)
    grad_theirs_ref[...] = dot(w_theirs, branch, 1, 1).astype(bf16)
    total[halves(own)] += dot(mine_ref[...], branch, 1, 0).reshape(dp // 2, shard, width)
    total[halves(other)] += dot(theirs_ref[...], branch, 1, 0).reshape(dp // 2, shard, width)

    @pl.when(step == pl.num_programs(0) - 1)
    def _():
        packed_ref[:, 0 : total.shape[1]] = total[...].astype(bf16)


def middle_part(info, mine, theirs, hidden, cot, weights, vectors, ff):
    half = mine.shape[0]
    rows, width = hidden.shape
    blk = min(512, rows)
    packed = weights.shape
    tall = pl.BlockSpec((blk, width), lambda i, n: (i, 0))
    wide = pl.BlockSpec((half, blk), lambda i, n: (0, i))
    fixed = lambda shape: pl.BlockSpec(shape, lambda i, n: (0,) * len(shape))
    return pl.pallas_call(
        functools.partial(middle_kernel, ff=ff),
        grid_spec=pltpu.PrefetchScalarGridSpec(
            num_scalar_prefetch=1,
            grid=(rows // blk,),
            in_specs=[wide, wide, tall, tall, fixed(packed), fixed(vectors.shape)],
            out_specs=[tall, tall, wide, wide, fixed(packed), fixed((8, ff))],
            scratch_shapes=[pltpu.VMEM((packed[0], packed[1] - 16, width), f32), pltpu.VMEM((blk, ff), bf16), pltpu.VMEM((blk, ff), f32)],
        ),
        out_shape=[
            jax.ShapeDtypeStruct((rows, width), bf16),
            jax.ShapeDtypeStruct((rows, width), f32),
            jax.ShapeDtypeStruct((half, rows), bf16),
            jax.ShapeDtypeStruct((half, rows), bf16),
            jax.ShapeDtypeStruct(packed, bf16),
            jax.ShapeDtypeStruct((8, ff), f32),
        ],
        cost_estimate=pl.CostEstimate(flops=12 * rows * width * (2 * ff + width) // 2, bytes_accessed=16 << 20, transcendentals=rows * ff),
        name="middle",
    )(info, mine, theirs, hidden, cot, weights, vectors)


def pack_kernel(out_ref, down_ref, up_ref, row_ref, packed_ref):
    shard, width = out_ref.shape
    at = shard + down_ref.shape[0]
    packed_ref[0:shard] = out_ref[...]
    packed_ref[shard:at] = down_ref[...]
    for j in range(up_ref.shape[1] // width):
        packed_ref[at + j * shard : at + (j + 1) * shard] = up_ref[:, j * width : (j + 1) * width]
    end = at + up_ref.shape[1] // width * shard
    packed_ref[end:] = jnp.broadcast_to(row_ref[...], (packed_ref.shape[0] - end, width))


def pack_part(out_weight, down_weight, up_weight, row):
    shard, width = out_weight.shape
    total = shard + down_weight.shape[0] + up_weight.shape[1] // width * shard + 16
    return pl.pallas_call(pack_kernel, out_shape=jax.ShapeDtypeStruct((total, width), bf16), name="pack")(out_weight, down_weight, up_weight, row)


def shape_kernel(info_ref, w_ref, small_ref, out_ref):
    part = w_ref.shape[0] // 2
    heads = HEADS // 2
    half = heads * HEAD_DIM
    block = w_ref[pl.ds(pl.multiple_of(info_ref[0] * part, part), part)]
    for which in range(2):
        cols = [block[:, which * half : (which + 1) * half]]
        for head in range(heads):
            for kind in (1, 2):
                at = (2 * kind + which) * half + head * HEAD_DIM
                cols.append(block[:, at : at + HEAD_DIM])
        out_ref[which * part : (which + 1) * part] = jnp.concatenate(cols, 1)
    out_ref[2 * part :] = jnp.broadcast_to(small_ref[...], (8, 3 * half))


def shape_part(info, weight, small):
    shard, cols = weight.shape
    full = pl.BlockSpec(memory_space=pltpu.VMEM)
    return pl.pallas_call(
        shape_kernel,
        in_specs=[pl.BlockSpec(memory_space=pltpu.SMEM), full, full],
        out_specs=full,
        out_shape=jax.ShapeDtypeStruct((shard + 8, cols // 2), bf16),
        name="shape",
    )(info, weight, small)


def place_kernel(info_ref, *refs, lows):
    own, other, out_ref, small_ref = refs[:lows], refs[lows : 2 * lows], refs[2 * lows], refs[2 * lows + 1]
    part, cols = out_ref.shape[3:]
    for j in range(lows):
        for k in range(own[j].shape[0]):
            at = info_ref[4] ^ (k * lows + j)
            out_ref[:, pl.ds(at, 1), pl.ds(info_ref[0], 1)] = own[j][k, 0 : 2 * part].reshape(2, part, cols)[:, None, None]
            out_ref[:, pl.ds(at, 1), pl.ds(1 - info_ref[0], 1)] = other[j][k, 0 : 2 * part].reshape(2, part, cols)[:, None, None]
            small_ref[pl.ds(at, 1)] = own[j][k, 2 * part :][None]


def place_part(info, own, other):
    count, rows, cols = own[0].shape
    full = pl.BlockSpec(memory_space=pltpu.VMEM)
    return pl.pallas_call(
        functools.partial(place_kernel, lows=len(own)),
        in_specs=[pl.BlockSpec(memory_space=pltpu.SMEM)] + [full] * (2 * len(own)),
        out_specs=[full, full],
        out_shape=[
            jax.ShapeDtypeStruct((2, count * len(own), 2, rows // 2 - 4, cols), bf16),
            jax.ShapeDtypeStruct((count * len(own), 8, cols), bf16),
        ],
        name="place",
    )(info, *own, *other)


def finish_kernel(info_ref, hidden_ref, mid_ref, w_ref, vec_ref, *refs, groups):
    many_groups = len(groups)
    parts, (mine_ref, theirs_ref, bias_ref, out_ref, sums_ref, total, grads) = refs[: 6 * many_groups], refs[6 * many_groups :]
    step = pl.program_id(0)
    rows, width = hidden_ref.shape
    half = width // 2

    @pl.when(step == 0)
    def _():
        total[...] = jnp.zeros_like(total)
        sums_ref[...] = jnp.zeros_like(sums_ref)

    ones = jnp.where(lax.broadcasted_iota(jnp.int32, (16, rows), 0) == 0, 1.0, 0.0).astype(bf16)
    hat, scale = norm_parts(hidden_ref[...].astype(f32))
    gain, shift = vec_ref[0:1], vec_ref[1:2]
    left = jnp.concatenate([(hat * gain + shift).astype(bf16).T, ones], 0)
    grad_norm = jnp.zeros((width, rows), f32)
    for which in range(2):
        dqs, dkvs, far = [parts[(3 * which + n) * many_groups : (3 * which + n + 1) * many_groups] for n in range(3)]
        for (at, many), dq_ref, dkv_ref, far_ref in zip(groups, dqs, dkvs, far):
            grads[which, at * HEAD_DIM : (at + many) * HEAD_DIM] = dq_ref[...]
            where = slice(half + at * 2 * HEAD_DIM, half + (at + many) * 2 * HEAD_DIM)
            grads[which, where] = (dkv_ref[...].astype(f32) + far_ref[...].astype(f32)).astype(bf16)
        total[which] += dot(left, grads[which], 1, 1)
        weights = w_ref[pl.ds(info_ref[0] ^ which, 1)].reshape(width, 3 * half)
        grad_norm = grad_norm + dot(weights, grads[which], 1, 0)
    grad_norm = grad_norm.T
    sums_ref[0:1] += jnp.sum(grad_norm * hat, axis=0, keepdims=True)
    sums_ref[1:2] += jnp.sum(grad_norm, axis=0, keepdims=True)
    out_ref[...] = (mid_ref[...] + norm_back(grad_norm, hat, scale, gain)).astype(bf16)

    @pl.when(step == pl.num_programs(0) - 1)
    def _():
        mine_ref[...] = total[0, 0:width].astype(bf16)
        theirs_ref[...] = total[1, 0:width].astype(bf16)
        for which in range(2):
            bias_ref[which] = jnp.broadcast_to(total[which, width : width + 1], bias_ref.shape[1:])


def finish_part(info, hidden, grad_mid, weights, vectors, mine, theirs, groups):
    rows, width = hidden.shape
    cols = 3 * width // 2
    blk = min(512, rows)
    wide = lambda n: pl.BlockSpec((n, blk), lambda i, n_: (0, i))
    tall = pl.BlockSpec((blk, width), lambda i, n: (i, 0))
    fixed = lambda shape: pl.BlockSpec(shape, lambda i, n: (0,) * len(shape))
    parts = [x for side in (mine, theirs) for kind in side for x in kind]
    return pl.pallas_call(
        functools.partial(finish_kernel, groups=groups),
        grid_spec=pltpu.PrefetchScalarGridSpec(
            num_scalar_prefetch=1,
            grid=(rows // blk,),
            in_specs=[tall, tall, fixed(weights.shape), fixed(vectors.shape)] + [wide(x.shape[0]) for x in parts],
            out_specs=[fixed((width, cols)), fixed((width, cols)), fixed((2, 8, cols)), tall, fixed((8, width))],
            scratch_shapes=[pltpu.VMEM((2, width + 16, cols), f32), pltpu.VMEM((2, cols, blk), bf16)],
        ),
        out_shape=[
            jax.ShapeDtypeStruct((width, cols), bf16),
            jax.ShapeDtypeStruct((width, cols), bf16),
            jax.ShapeDtypeStruct((2, 8, cols), f32),
            jax.ShapeDtypeStruct((rows, width), bf16),
            jax.ShapeDtypeStruct((8, width), f32),
        ],
        cost_estimate=pl.CostEstimate(flops=8 * rows * width * cols, bytes_accessed=16 << 20, transcendentals=rows),
        name="finish",
    )(info, hidden, grad_mid, weights, vectors, *parts)


def join_kernel(info_ref, held_ref, got_ref, out_ref, small_ref):
    shard = out_ref.shape[0]
    heads = HEADS // 2
    half = heads * HEAD_DIM
    held, got = held_ref[...].astype(f32), got_ref[...].astype(f32)
    for which in range(2):
        block = jnp.where(info_ref[0] == which, got[:shard], held[:shard])
        out_ref[:, which * half : (which + 1) * half] = block[:, :half]
        for kind in (1, 2):
            at = (2 * kind + which) * half
            starts = [half + (2 * head + kind - 1) * HEAD_DIM for head in range(heads)]
            out_ref[:, at : at + half] = jnp.concatenate([block[:, start : start + HEAD_DIM] for start in starts], 1)
    small_ref[...] = held[shard:] + got[shard:]


def join_part(info, held, got):
    rows, cols = held.shape
    full = pl.BlockSpec(memory_space=pltpu.VMEM)
    return pl.pallas_call(
        join_kernel,
        in_specs=[pl.BlockSpec(memory_space=pltpu.SMEM), full, full],
        out_specs=[full, full],
        out_shape=[jax.ShapeDtypeStruct((rows - 8, 2 * cols), f32), jax.ShapeDtypeStruct((8, cols), f32)],
        name="join",
    )(info, held, got)


def swap(values, axis, flip):
    size = lax.axis_size(axis)
    return lax.ppermute(values, axis, [(i, i ^ flip) for i in range(size)])


def gelu_and_slope(u):
    a = 0.7978845608028654
    inner = a * (u + 0.044715 * u * u * u)
    t = jnp.tanh(inner)
    slope = 0.5 * (1 + t) + 0.5 * u * (1 - t * t) * a * (1 + 3 * 0.044715 * u * u)
    return 0.5 * u * (1 + t), slope


def norm_parts(inputs):
    center = inputs - jnp.mean(inputs, axis=-1, keepdims=True)
    scale = lax.rsqrt(jnp.mean(center * center, axis=-1, keepdims=True) + EPS)
    return center * scale, scale


def norm_back(grad, hat, scale, gain):
    e = grad * gain
    return scale * (e - jnp.mean(e, axis=-1, keepdims=True) - hat * jnp.mean(e * hat, axis=-1, keepdims=True))


def tie(*values):
    return lax.optimization_barrier(values)


def on_device(
    hidden_in, seq_lengths, out_cotangent, norm1_gain, norm1_shift, qkv_weight, qv_bias, out_weight, out_bias,
    norm2_gain, norm2_shift, up_weight, up_bias, down_weight, down_bias,
):
    rows, width = hidden_in.shape[1:]
    hidden_in, out_cotangent = hidden_in[0], out_cotangent[0]
    ff = up_weight.shape[1]
    dp, ctx = lax.axis_size("dp"), lax.axis_size("ctx")
    dp_low = 2 if dp == 8 else 4
    dp_high, high_at = dp // dp_low, dp_low.bit_length() - 1
    ring = ctx // 2
    me = lax.axis_index("ctx")
    core = me % 2
    heads = HEADS // 2
    half = heads * HEAD_DIM
    shard = width // dp
    length = seq_lengths[0]
    info = jnp.stack([core, jnp.clip(length - me * rows, 0, rows), length, me, lax.axis_index("dp")]).astype(jnp.int32)

    def by_core(cols):
        lead = cols.shape[:-1]
        cols = cols.reshape(lead + (3, 2, heads, HEAD_DIM))
        asks = cols[..., 0, :, :, :].reshape(lead + (2, half))
        pairs = jnp.moveaxis(cols[..., 1:, :, :, :], -4, -2).reshape(lead + (2, 2 * half))
        return jnp.concatenate([asks, pairs], -1)

    def from_core(cols):
        lead = cols.shape[:-2]
        asks = cols[..., :half].reshape(lead + (1, 2, heads, HEAD_DIM))
        pairs = jnp.moveaxis(cols[..., half:].reshape(lead + (2, heads, 2, HEAD_DIM)), -2, -4)
        return jnp.concatenate([asks, pairs], -4).reshape(lead + (6 * half,))

    high_stage = lambda x: [swap(x, "dp", k << high_at) for k in range(1, dp_high)]
    low_stage = lambda x: [swap(x, "dp", j) for j in range(1, dp_low)]

    early = jnp.concatenate([norm1_gain, norm1_shift, qv_bias[0], qv_bias[1]])
    early = jnp.pad(early, (0, 3 * half - early.shape[0]))[None]
    piece = shape_part(info, qkv_weight, early)
    pieces = [piece] + high_stage(piece)
    late = jnp.concatenate([out_bias, norm2_gain, norm2_shift, down_bias, up_bias])
    late = jnp.pad(late, (0, width - late.shape[0]))[None]
    others = pack_part(out_weight, down_weight, up_weight, late)
    others, pieces = tie(others, pieces)
    others = lax.all_gather(others, "dp", axis=0, tiled=False)
    stack = jnp.stack(pieces)
    own = [stack] + low_stage(stack)
    other = [swap(x, "ctx", 1) for x in own]
    w_qkv, early = place_part(info, own, other)
    w_qkv = w_qkv.reshape(2, width, 3 * half)
    early = early[:, 0, : 4 * shard].reshape(dp, 4, shard).swapaxes(0, 1).reshape(4, width).astype(f32)
    gain_one, shift_one, bias_q, bias_v = early

    hat_one, _ = norm_parts(hidden_in.astype(f32))
    normed_one = (hat_one * gain_one + shift_one).astype(bf16)
    bias_full = by_core(jnp.concatenate([bias_q, jnp.zeros_like(bias_q), bias_v]))
    factors = jnp.where(jnp.arange(3 * half) < half, LOG2E * HEAD_DIM**-0.5, 1.0)

    def projected(which):
        pick = lambda x: lax.dynamic_index_in_dim(x, which, 0, keepdims=False)
        return ((dot(pick(w_qkv), normed_one, 0, 1) + pick(bias_full)[:, None]) * factors[:, None]).astype(bf16)

    foreign = projected(1 - core)
    mine = projected(core)
    theirs = swap(foreign, "ctx", 1)

    groups = [(0, 2), (2, 2)] if ring == 2 else [(0, heads)]
    far = []
    for k in range(1, ring):
        for at, many in groups:
            cut = slice(half + at * 2 * HEAD_DIM, half + (at + many) * 2 * HEAD_DIM)
            there = tie(foreign[cut], mine, theirs)[0] if at else foreign[cut]
            far.append((k, at, many, swap(mine[cut], "ctx", 2 * k), swap(there, "ctx", 2 * k + 1)))
    *sums, own_top, probs = attend(info, 0, mine, theirs, mine, theirs, heads, 0, heads, None, None, ring == 1)
    near = (own_top, probs)
    saved, low = [], None
    for k, at, many, key_a, key_b in far:
        last = k == ring - 1
        out = attend(info, k, mine, theirs, key_a, key_b, 0, at, many, sums, low if last else None, last)
        if last:
            low, out = out[:2], out[2:]
        sums, own_top, probs = out[:2], out[2], out[3]
        saved.append((own_top, probs))
    attended, stat = sums
    low_theirs = swap(low[1], "ctx", 1)

    rest = others[:, -16].astype(f32)
    vector = lambda at: rest[:, at * shard : (at + 1) * shard].reshape(width)
    second_rows = jnp.pad(
        jnp.stack([jnp.concatenate([vector(0), vector(1), vector(2), vector(3)]), rest[:, 4 * shard : 4 * shard + ff // dp].reshape(ff)]), ((0, 6), (0, 0))
    )
    hidden_out, grad_mid, grad_mine, grad_theirs, packed, sums_two = middle_part(
        info, low[0], low_theirs, hidden_in, out_cotangent, others, second_rows, ff
    )
    grad_theirs = swap(grad_theirs, "ctx", 1)

    spread = lambda x: x.reshape(-1, dp, x.shape[-1] // dp).swapaxes(0, 1).reshape(dp, -1)
    late = jnp.concatenate([spread(sums_two[1].reshape(4, width)), spread(sums_two[0].reshape(1, ff))], 1)
    late = jnp.pad(late, ((0, 0), (0, width - late.shape[1])))[:, None].astype(bf16)
    packed = lax.dynamic_update_slice(packed, jnp.broadcast_to(late, (dp, 16, width)), (0, packed.shape[1] - 16, 0))
    packed = lax.psum_scatter(packed, "dp", scatter_dimension=0, tiled=False)

    buffer, flying, back_mine, back_theirs = None, [], {}, {}
    shared = (grad_mine, grad_theirs, attended, stat)
    calls = [(k, at, many, key_a, key_b, 0, 0, kept) for (k, at, many, key_a, key_b), kept in zip(far, saved)]
    calls = calls + [(0, at, many, mine, theirs, heads + 2 * at, at, near) for at, many in groups]
    ends = []
    for n, (k, at, many, key_a, key_b, kv_base, p_base, kept) in enumerate(calls):
        call_info = info
        if ends:
            call_info, kept_back = tie(info, ends[-1][2])
            ends[-1] = ends[-1][:2] + (kept_back,) + ends[-1][3:]
        if n > 1 and flying:
            call_info, (got_mine, got_theirs), where = *tie(call_info, flying[0][:2]), flying.pop(0)[2]
            back_mine.setdefault(where, []).append(got_mine)
            back_theirs.setdefault(where, []).append(got_theirs)
        outs = attend_back(call_info, k, mine, theirs, key_a, key_b, kv_base, p_base, at, many, *shared, *kept, (buffer, k == 0 or k > 1), k == 0)
        if k:
            buffer = outs[0]
            flying.append((swap(outs[1], "ctx", 2 * k), swap(outs[2], "ctx", 2 * k + 1), at))
        else:
            dq_a, dq_b, dkv_a, dkv_b = outs
            ends.append((dq_a, swap(dq_b, "ctx", 1), dkv_a, swap(dkv_b, "ctx", 1)))
    for got_mine, got_theirs, where in flying:
        back_mine.setdefault(where, []).append(got_mine)
        back_theirs.setdefault(where, []).append(got_theirs)
    dqs_mine, dqs_theirs, dkvs_mine, dkvs_theirs = zip(*ends)
    sum_far = lambda parts: [functools.reduce(lambda a, b: (a.astype(f32) + b.astype(f32)).astype(bf16), parts[at]) for at, _ in groups]

    sides = [(dqs_mine, dkvs_mine, sum_far(back_mine)), (dqs_theirs, dkvs_theirs, sum_far(back_theirs))]
    packed = packed.reshape((2, -1) + packed.shape[1:])
    packed_first, packed_send = [lax.dynamic_index_in_dim(packed, core ^ k, 0, keepdims=False) for k in range(2)]
    call_info, packed_send = tie(info, packed_send)
    dw_out, dw, bias_sides, grad_hidden, sums_one = finish_part(call_info, hidden_in, grad_mid, w_qkv, early, *sides, groups)
    dw_in = swap(dw_out, "ctx", 1)

    def halves(total, axis, shift, count, dim):
        index = (lax.axis_index(axis) >> shift) & (count - 1)
        pick = lambda k: lax.dynamic_index_in_dim(total, index ^ k, dim, keepdims=False)
        return pick(0).astype(f32), [pick(k).astype(bf16) for k in range(1, count)]

    swaps = lambda parts, axis, shift: [swap(part, axis, k << shift) for k, part in enumerate(parts, 1)]
    add = lambda first, rest: functools.reduce(lambda a, b: a + b.astype(f32), rest, first.astype(f32))

    def sum_chips(total, covers=None):
        for flip in [2 << b for b in range(ring.bit_length() - 1)]:
            total = total.astype(bf16)
            got = swap(total, "ctx", flip)
            if covers is not None:
                got, _ = tie(got, covers)
            total = add(total, [got])
        return total.astype(bf16)

    bias_one = jnp.where(core == 0, bias_sides[0, 0], bias_sides[1, 0])
    bias_two = jnp.where(core == 0, bias_sides[1, 0], bias_sides[0, 0])
    bias_sums = from_core(jnp.stack([bias_one, bias_two])).reshape(3, width)
    smalls = jnp.concatenate([spread(sums_one[0:2]), spread(bias_sums[0:1]), spread(bias_sums[2:3])], 1)
    smalls = jnp.pad(smalls[:, None], ((0, 0), (0, 7), (0, 3 * half - smalls.shape[1])))
    total = jnp.concatenate([add(dw, [dw_in]).reshape(dp, shard, 3 * half), smalls], 1)
    first, sent = halves(total.reshape((dp_high, dp_low) + total.shape[1:]), "dp", 0, dp_low, 1)
    sent, packed_send = tie(sent, packed_send)
    sent = swaps(sent, "dp", 0)
    packed = add(packed_first, [swap(packed_send, "ctx", 1)]).astype(bf16)
    sent, _ = tie(sent, packed)
    packed = sum_chips(packed)
    first, sent = halves(add(first, sent), "dp", high_at, dp_high, 0)
    sent = swaps(sent, "dp", high_at)
    sent, _ = tie(sent, packed)
    packed_got = swap(packed, "ctx", 1)
    by_index = lambda a, b: [jnp.where(core == 0, a, b), jnp.where(core == 0, b, a)]
    packed = jnp.concatenate(by_index(packed, packed_got), 0).astype(f32)
    down_at, up_at, end = shard, shard + ff // dp, shard + 2 * (ff // dp)
    grad_up = packed[up_at:end].reshape(ff // width, shard, width).swapaxes(0, 1).reshape(shard, ff)
    grad_out_weight, grad_down, last_row = packed[:shard], packed[down_at:up_at], packed[-16]
    total = sum_chips(add(first, sent), (grad_out_weight, grad_down, grad_up, last_row))
    grad_qkv, smalls = join_part(info, total, swap(total, "ctx", 1))
    smalls = smalls[0]
    small_out = lambda at: smalls[at * shard : (at + 1) * shard]
    late_out = lambda at: last_row[at * shard : (at + 1) * shard]
    return (
        hidden_out[None],
        grad_hidden[None],
        small_out(0),
        small_out(1),
        grad_qkv,
        jnp.stack([small_out(2), small_out(3)]),
        grad_out_weight,
        late_out(0),
        late_out(1),
        late_out(2),
        grad_up,
        last_row[4 * shard : 4 * shard + ff // dp],
        grad_down,
        late_out(3),
    )


def solution(mesh):
    return jax.shard_map(
        on_device,
        mesh=mesh,
        in_specs=(
            P("dp", "ctx", None), P("dp"), P("dp", "ctx", None), P("dp"), P("dp"), P("dp", None), P(None, "dp"),
            P("dp", None), P("dp"), P("dp"), P("dp"), P("dp", None), P("dp"), P("dp", None), P("dp"),
        ),
        out_specs=(
            P("dp", "ctx", None), P("dp", "ctx", None), P("dp"), P("dp"), P("dp", None), P(None, "dp"), P("dp", None),
            P("dp"), P("dp"), P("dp"), P("dp", None), P("dp"), P("dp", None), P("dp"),
        ),
        check_vma=False,
    )
```
